256 devices in a mesh: dir: 8 (over z_lo, core), box: 32 (over z_hi, x, y).
Axes of the slice: x: 4, y: 4, z: 8 (z_hi: 2, z_lo: 4; z = z_hi * 4 + z_lo), core: 2. Of those that a mesh axis runs over, the one named last changes fastest.
Arguments:
- pattern: bfloat16 [64, 128, 256, 128], P('dir', 'box'), may hold values from -6 to 6
- tap_theta: int32 [64, 12], replicated, may hold values from 0 to 31, as said below
- tap_phi: int32 [128, 12], replicated, may hold values from 0 to 63, as said below
- weight_theta: bfloat16 [64, 12], replicated, may hold values from -1.75 to 1.75
- weight_phi: bfloat16 [128, 12], replicated, may hold values from -1.75 to 1.75
- row_box: int32 [524288], P(('dir', 'box')), may hold values from 0 to 2047, as said below
- row_offset: bfloat16 [3, 524288], P(None, ('dir', 'box')), may hold values from -0.5 to 0.5
- row_fwd: bfloat16 [524288, 128], P(('dir', 'box')), may hold values from -6 to 6
Outputs:
- row_field: bfloat16 [524288, 128], P(('dir', 'box'))
- gradient: float32 [524288], P(('dir', 'box'))
The draws below stay inside these ranges and needn't reach their ends.
Inputs may be any that keep to these rules, and one draw needn't show every extreme that they name: `tap_theta`: row T holds 12 consecutive increasing indices of the child theta samples. `tap_phi`: row P holds 12 consecutive indices of the child phi samples, taken modulo 64. Device i of the dir+box layout holds rows whose parent box row_box // 8 satisfies parent // 32 == i // 32. From one device at most 256 rows name parent boxes with one remainder modulo 32. In each dir group one remainder, drawn from the seed, is named by exactly 256 rows of every device of the group; a device's other rows are spread over the other remainders as evenly as possible. Octants are arbitrary.
All inputs are finite; a program needn't handle non-finite values.
Results may differ from the reference program's by a relative error of at most 0.0065.
Values may be sent and summed in bfloat16 or wider, within the bound.
A program may use at most 64 MiB of HBM per device.

```python
import math
import jax
import jax.numpy as jnp
from jax import lax

NT = 64
NP = 128
NT_F = 32
NP_F = 64
TAPS = 12
C = 128
ROW_DEV = 2048
CAP = 256
ROWS = 524288
BOXES = 256
N_BOX = 32
DEVICES = 256


def draw_tap_theta(key, part):
    offset = jax.random.randint(jax.random.fold_in(key, 11), (NT,), -2, 3)
    start = jnp.clip(jnp.arange(NT) * NT_F // NT - 5 + offset, 0, NT_F - TAPS)
    return (start[:, None] + jnp.arange(TAPS)[None, :]).astype(jnp.int32)


def draw_tap_phi(key, part):
    offset = jax.random.randint(jax.random.fold_in(key, 13), (NP,), -2, 3)
    start = jnp.arange(NP) * NP_F // NP - 5 + offset
    return ((start[:, None] + jnp.arange(TAPS)[None, :]) % NP_F).astype(jnp.int32)


def draw_row_box(key, part):
    group_count = DEVICES // N_BOX
    hot = jax.random.randint(jax.random.fold_in(key, 1), (group_count,), 0, N_BOX)

    def one_block(source):
        block_key = jax.random.fold_in(jax.random.fold_in(key, 2), source)
        group = source // N_BOX
        hot_dest = hot[group]
        order = jax.random.permutation(jax.random.fold_in(block_key, 1), ROW_DEV)
        others = jax.random.permutation(jax.random.fold_in(block_key, 2), N_BOX - 1)
        rank = jnp.arange(ROW_DEV)
        rest = others[jnp.maximum(rank - CAP, 0) % (N_BOX - 1)]
        rest = rest + (rest >= hot_dest).astype(jnp.int32)
        by_rank = jnp.where(rank < CAP, hot_dest, rest)
        dest = jnp.zeros((ROW_DEV,), jnp.int32).at[order].set(by_rank.astype(jnp.int32))
        octant = jax.random.randint(jax.random.fold_in(block_key, 3), (ROW_DEV,), 0, 8)
        return ((group * N_BOX + dest) * 8 + octant).astype(jnp.int32)
    return jax.vmap(one_block)(jnp.arange(DEVICES)).reshape(ROWS)


def shard_levels(rng, dims, cuts, least, high):
    def one(position, blocks):
        steps = jax.random.uniform(jax.random.fold_in(jax.random.fold_in(rng, 6), position), (blocks,), jnp.float32, least / len(cuts), high / len(cuts))
        return jnp.repeat(jnp.exp(steps), dims[position] // blocks).reshape((-1,) + (1,) * (len(dims) - position - 1))

    factor_of = one(*cuts[0])
    for cut in cuts[1:]:
        factor_of = factor_of * one(*cut)
    return factor_of


def centred(rng, shape, width, bound, pieces=(), held_as=jnp.bfloat16):
    loudness = shard_levels(rng, shape, pieces, -0.22, 0.18) if pieces else 1.0
    drawn = jax.random.normal(rng, shape, jnp.float32) * width * loudness
    return jnp.minimum(jnp.maximum(drawn, -bound), bound).astype(held_as)


def setup_inputs(seed: int = 0) -> dict:
    key_of = jax.random.split(jax.random.key(seed), 9)
    pattern = centred(key_of[0], (NT, NP, BOXES, C), 1.0, 6.0, ((0, 8), (1, 32)))
    tap_theta = draw_tap_theta(jax.random.fold_in(key_of[8], 71), 0)
    tap_phi = draw_tap_phi(jax.random.fold_in(key_of[8], 71), 0)
    weight_theta = centred(key_of[3], (NT, TAPS), TAPS ** -0.5, 1.75)
    weight_phi = centred(key_of[4], (NP, TAPS), TAPS ** -0.5, 1.75)
    row_box = draw_row_box(jax.random.fold_in(key_of[8], 71), 0)
    row_offset = jnp.clip(jax.random.uniform(key_of[6], (3, ROWS), jnp.float32, -0.5, 0.5) * shard_levels(key_of[6], (3, ROWS), ((1, 256),), -0.4, 0.0), -0.5, 0.5).astype(jnp.bfloat16)
    row_fwd = centred(key_of[7], (ROWS, C), 1.0, 6.0, ((0, 256),))
    return dict(pattern=pattern, tap_theta=tap_theta, tap_phi=tap_phi, weight_theta=weight_theta, weight_phi=weight_phi, row_box=row_box, row_offset=row_offset, row_fwd=row_fwd)


box_phase = 50.265482

def spread(taps, weights, count):
    grid = jnp.arange(count, dtype=jnp.int32)
    hit = taps[None, :, :] == grid[:, None, None]
    picked = jnp.where(hit, weights[None, :, :].astype(jnp.float32), jnp.float32(0.0))
    return lax.optimization_barrier(jnp.sum(picked, axis=2)).astype(jnp.bfloat16)

def directions(n_theta, n_phi):
    theta = (jnp.arange(n_theta, dtype=jnp.float32) + 0.5) * (math.pi / n_theta)
    angle_phi = jnp.arange(n_phi, dtype=jnp.float32) * (2.0 * math.pi / n_phi)
    sin_t = jnp.repeat(jnp.sin(theta), n_phi)
    cos_t = jnp.repeat(jnp.cos(theta), n_phi)
    phi_all = jnp.tile(angle_phi, n_theta)
    quad = sin_t * math.sqrt(2.0 / (n_theta * n_phi))
    return (sin_t * jnp.cos(phi_all), sin_t * jnp.sin(phi_all), cos_t, quad)

def positions(offset, octant):
    bits = jnp.stack([octant % 2, octant // 2 % 2, octant // 4], axis=1)
    signs = (2 * bits - 1).astype(jnp.float32)
    return box_phase * (signs * 0.25 + offset.astype(jnp.float32) * 0.5)

def field_rows(pos, stacked, kx, ky, kz, quad):
    angle = pos[:, 0:1] * kx[None, :] + pos[:, 1:2] * ky[None, :] + pos[:, 2:3] * kz[None, :]
    cos_w = (quad[None, :] * jnp.cos(angle)).astype(jnp.bfloat16)
    sin_w = (quad[None, :] * jnp.sin(angle)).astype(jnp.bfloat16)
    phase = jnp.concatenate([cos_w, sin_w], axis=1)
    return jnp.dot(phase, stacked, preferred_element_type=jnp.float32)

def child_block(box_pattern, a_theta, a_phi):
    n_big, p_big, chans = box_pattern.shape
    n_small = a_theta.shape[0]
    p_small = a_phi.shape[0]
    theta_part = jnp.dot(a_theta, box_pattern.reshape(n_big, p_big * chans), preferred_element_type=jnp.float32)
    theta_part = theta_part.astype(jnp.bfloat16).reshape(n_small, p_big, chans)
    child = jnp.einsum('pP,tPc->tpc', a_phi.astype(jnp.float32), theta_part.astype(jnp.float32)).astype(jnp.bfloat16)
    flat = child.reshape(n_small * p_small, chans)
    half = chans // 2
    return jnp.concatenate([flat, jnp.concatenate([-flat[:, half:], flat[:, :half]], axis=1)], axis=0)

def reference(pattern, tap_theta, tap_phi, weight_theta, weight_phi, row_box, row_offset, row_fwd):
    a_theta = spread(tap_theta, weight_theta, NT_F)
    a_phi = spread(tap_phi, weight_phi, NP_F)
    count_boxes = pattern.shape[2]

    def per_box(index):
        return child_block(lax.dynamic_index_in_dim(pattern, index, 2, keepdims=False), a_theta, a_phi)
    stacked_all = lax.map(per_box, jnp.arange(count_boxes, dtype=jnp.int32))
    kx, ky, kz, quad = directions(NT_F, NP_F)
    parent = row_box // 8
    octant = row_box % 8
    pos = positions(row_offset.T, octant)
    order = jnp.argsort(parent, stable=True)
    par_sorted = parent[order]
    pos_sorted = pos[order]
    total = row_box.shape[0]
    block = 512

    def one_block(index):
        start = (index * block).astype(jnp.int32)
        chosen = lax.dynamic_slice_in_dim(par_sorted, start, block)
        where_pos = lax.dynamic_slice_in_dim(pos_sorted, start, block, 0)

        def add_box(g, acc):
            part = field_rows(where_pos, stacked_all[g], kx, ky, kz, quad)
            return acc + jnp.where((chosen == g)[:, None], part, jnp.float32(0.0))
        first = chosen[0].astype(jnp.int32)
        last = chosen[block - 1].astype(jnp.int32)
        return lax.fori_loop(first, last + 1, add_box, jnp.zeros((block, C), jnp.float32))
    fields = lax.map(one_block, jnp.arange(total // block, dtype=jnp.int32)).reshape(total, C).astype(jnp.bfloat16)
    row_field = jnp.zeros_like(fields).at[order].set(fields)
    gradient = lax.optimization_barrier(jnp.sum(row_fwd.astype(jnp.float32) * row_field.astype(jnp.float32), axis=1)) * (0.5 / math.sqrt(C))
    return (row_field, gradient)
```

```python
import functools
import math

import jax
import jax.numpy as jnp
import numpy as np
from jax import lax
from jax.experimental import pallas as pl
from jax.experimental.pallas import tpu as pltpu
from jax.sharding import PartitionSpec as P

NT = 64
NP = 128
NT_F = 32
NP_F = 64
C = 128
HALF = 64
N_DIR = 8
N_BOX = 32
N_XY = 16
ROW_DEV = 2048
SLOT = 64
HOT = 256
SLOTS = N_BOX * SLOT + HOT
P_DEV = NP // N_BOX
T_DEV = NT // N_DIR

box_phase = 50.265482

MESH = pl.DeviceIdType.MESH
BF = jnp.bfloat16
F32 = jnp.float32


def polynomials():
    z2 = 0.5 + 0.5 * np.cos(np.pi * (np.arange(400) + 0.5) / 400)
    z = np.sqrt(z2)
    s = np.polynomial.chebyshev.Chebyshev.fit(z2, np.sin(np.pi * z) / z, 7, domain=[0, 1])
    k = np.polynomial.chebyshev.Chebyshev.fit(z2, np.cos(np.pi * z), 8, domain=[0, 1])
    to = np.polynomial.polynomial.Polynomial
    return tuple(
        [float(v) for v in f.convert(kind=to, domain=[-1, 1], window=[-1, 1]).coef] for f in (s, k)
    )


SIN_POLY, COS_POLY = polynomials()


def turns(u):
    z = (u - jnp.round(u)) * 2.0
    w = z * z
    s = jnp.full_like(w, SIN_POLY[-1])
    for v in SIN_POLY[-2::-1]:
        s = s * w + v
    k = jnp.full_like(w, COS_POLY[-1])
    for v in COS_POLY[-2::-1]:
        k = k * w + v
    return k, s * z


def spread(taps, weights, count):
    grid = jnp.arange(count, dtype=jnp.int32)
    hit = taps[None, :, :] == grid[:, None, None]
    picked = jnp.where(hit, weights[None, :, :].astype(F32), F32(0.0))
    return jnp.sum(picked, axis=2).astype(BF)


def theta_signs():
    h = np.zeros((NT_F, NT_F), np.float32)
    for t in range(16):
        for c in range(2):
            h[c * 16 + t, t] = 1.0
            h[c * 16 + t, 31 - t] = (-1.0) ** c
    return h


def phi_signs():
    h = np.zeros((NP_F, NP_F), np.float32)
    for q in range(1, 16):
        for a in range(2):
            for b in range(2):
                r = q * 4 + a * 2 + b
                h[r, q] = 1.0
                h[r, 32 - q] = (-1.0) ** a
                h[r, 64 - q] = (-1.0) ** b
                h[r, 32 + q] = (-1.0) ** (a + b)
    for a in range(2):
        h[a * 2, 0] = 1.0
        h[a * 2, 32] = (-1.0) ** a
    h[1, 16], h[1, 48] = 1.0, -1.0
    h[3, 16], h[3, 48] = 1.0, 1.0
    return h


def prepare_kernel(ah, bh, rows, off, mt, mp, go, hotg, pos, geo, acc):
    box = rows[...]
    parent = box // 8
    octant = box - parent * 8
    dest = parent % N_BOX
    owner = lax.broadcasted_iota(jnp.int32, (N_BOX, ROW_DEV), 0)
    onehot = jnp.where(owner == dest, 1.0, 0.0).astype(F32)
    width = 256
    before = jnp.where(
        lax.broadcasted_iota(jnp.int32, (width, width), 0)
        < lax.broadcasted_iota(jnp.int32, (width, width), 1),
        1.0,
        0.0,
    ).astype(BF)
    carry = jnp.zeros((N_BOX, 1), F32)
    ranks = []
    for i in range(ROW_DEV // width):
        one = onehot[:, i * width : (i + 1) * width]
        pre = jnp.dot(one.astype(BF), before, preferred_element_type=F32) + carry
        ranks.append(jnp.sum(one * pre, axis=0, keepdims=True))
        carry = carry + jnp.sum(one, axis=1, keepdims=True)
    rank = jnp.concatenate(ranks, axis=1)
    is_hot = jnp.where(carry > float(SLOT), 1.0, 0.0)
    hot_row = jnp.sum(onehot * is_hot, axis=0, keepdims=True)
    number = lax.broadcasted_iota(jnp.int32, (N_BOX, 1), 0).astype(F32)
    hot = jnp.sum(number * is_hot, axis=0, keepdims=True)
    where_to = jnp.where(
        hot_row > 0.5, float(N_BOX * SLOT) + rank, dest.astype(F32) * float(SLOT) + rank
    )
    pos[...] = where_to
    col = lax.broadcasted_iota(jnp.int32, (NT, NT * N_XY), 1)
    row = lax.broadcasted_iota(jnp.int32, (NT, NT * N_XY), 0)
    wide = jnp.where(col // N_XY == row, 1.0, 0.0).astype(BF)
    v = jnp.dot(ah[...], wide, preferred_element_type=F32)
    lane_g = lax.broadcasted_iota(jnp.int32, v.shape, 1) % N_XY
    for g in range(N_XY):
        mt[g * NT_F : (g + 1) * NT_F, :] = jnp.where(lane_g == g, v, 0.0).astype(BF)
    half = lax.axis_index("box") // N_XY
    local = hot - (half * N_XY).astype(F32)
    mt[N_XY * NT_F :, :] = jnp.where(lane_g.astype(F32) == local, v, 0.0).astype(BF)
    col = lax.broadcasted_iota(jnp.int32, (NP, NP * 16), 1)
    row = lax.broadcasted_iota(jnp.int32, (NP, NP * 16), 0)
    wide = jnp.where(col // 16 == row, 1.0, 0.0).astype(BF)
    v = jnp.dot(bh[...], wide, preferred_element_type=F32)
    same = (
        lax.broadcasted_iota(jnp.int32, (16, NP * 16), 1) % 16
        == lax.broadcasted_iota(jnp.int32, (16, NP * 16), 0)
    )
    for r in range(NP_F):
        mp[r * 16 : (r + 1) * 16, :] = jnp.where(same, v[r : r + 1, :], 0.0).astype(BF)
    sub = lax.broadcasted_iota(jnp.int32, (16, ROW_DEV), 0)
    o = off[...].astype(F32)
    g = jnp.where(sub == 3, octant.astype(F32), 0.0)
    for i in range(3):
        g = jnp.where(sub == i, o[i : i + 1, :], g)
    geo[...] = g.astype(BF)
    acc[...] = jnp.zeros_like(acc)
    lane = lax.broadcasted_iota(jnp.int32, (128, 128), 1).astype(F32)

    def block(i, carry):
        at = pl.multiple_of(i * 256, 256)
        p = pos[:, pl.ds(at, 256)]
        oh = one_hot(p, lane)
        acc[...] += jnp.dot(geo[:, pl.ds(at, 256)], oh, preferred_element_type=F32)
        return carry

    lax.fori_loop(0, ROW_DEV // 256, block, 0)
    for m in range(N_BOX // 2):
        go[m] = acc[:, m * 128 : (m + 1) * 128].astype(BF)
    for m in range(2):
        hotg[m] = acc[:, N_BOX * SLOT + m * 128 : N_BOX * SLOT + (m + 1) * 128].astype(BF)


def one_hot(p, lane):
    parts = []
    for h in range(2):
        column = jnp.broadcast_to(p[:, h * 128 : (h + 1) * 128], (128, 128)).T
        parts.append(
            jnp.concatenate(
                [
                    jnp.where(column == lane + float(j * 128), 1.0, 0.0).astype(BF)
                    for j in range(SLOTS // 128)
                ],
                axis=1,
            )
        )
    return jnp.concatenate(parts, axis=0)


def prepare(ah, bh, rows, off):
    vm = pl.BlockSpec(memory_space=pltpu.VMEM)
    return pl.pallas_call(
        prepare_kernel,
        out_shape=(
            jax.ShapeDtypeStruct((N_XY * NT_F + NT_F, NT * N_XY), BF),
            jax.ShapeDtypeStruct((NP_F * 16, NP * 16), BF),
            jax.ShapeDtypeStruct((N_BOX // 2, 16, 128), BF),
            jax.ShapeDtypeStruct((2, 16, 128), BF),
            jax.ShapeDtypeStruct((1, ROW_DEV), F32),
        ),
        in_specs=[vm] * 4,
        out_specs=(vm,) * 5,
        scratch_shapes=[pltpu.VMEM((16, ROW_DEV), BF), pltpu.VMEM((16, SLOTS), F32)],
        compiler_params=pltpu.CompilerParams(vmem_limit_bytes=56 << 20),
        name="prepare",
    )(ah, bh, rows, off)


def exchange_kernel(
    pat, mt, go, ry, rh, rg, recv, ybuf, hbuf, twin, hsum,
    z_send, z_recv, z_self, g_send, g_recv, y_send, y_recv, t_send, t_recv, h_send, h_recv, self_sem,
):
    d = lax.axis_index("dir")
    b = lax.axis_index("box")
    zh = b // N_XY
    xy = b % N_XY
    e = zh * N_DIR + d

    barrier = pltpu.get_barrier_semaphore()

    def greet_z(k, carry):
        e2 = (e + k) % 16
        pl.semaphore_signal(
            barrier, inc=1, device_id=(e2 % N_DIR, e2 // N_DIR * N_XY + xy), device_id_type=MESH
        )
        return carry

    def greet_box(k, carry):
        pl.semaphore_signal(barrier, inc=1, device_id=(d, (b + k) % N_BOX), device_id_type=MESH)
        return carry

    lax.fori_loop(1, 16, greet_z, 0)
    lax.fori_loop(1, N_BOX, greet_box, 0)
    pl.semaphore_wait(barrier, 15 + N_BOX - 1)

    def z_copy(pi, k):
        e2 = (e + k) % 16
        d2, zh2 = e2 % N_DIR, e2 // N_DIR
        first = pl.multiple_of(d2 * N_BOX + zh2 * N_XY, N_XY)
        return pltpu.make_async_remote_copy(
            src_ref=pat.at[:, pi, pl.ds(first, N_XY), :],
            dst_ref=recv.at[pi, zh, d],
            send_sem=z_send.at[pi, k],
            recv_sem=z_recv.at[pi, k],
            device_id=(d2, zh2 * N_XY + xy),
            device_id_type=MESH,
        )

    def z_own(pi):
        first = pl.multiple_of(d * N_BOX + zh * N_XY, N_XY)
        return pltpu.make_async_copy(
            pat.at[:, pi, pl.ds(first, N_XY), :], recv.at[pi, zh, d], z_self.at[pi]
        )

    def g_copy(k):
        b2 = (b + k) % N_BOX
        return pltpu.make_async_remote_copy(
            src_ref=go.at[b2 // 2],
            dst_ref=rg.at[b],
            send_sem=g_send.at[k],
            recv_sem=g_recv.at[k],
            device_id=(d, b2),
            device_id_type=MESH,
        )

    def y_copy(pi, k):
        xy2 = (xy + k) % N_XY
        return pltpu.make_async_remote_copy(
            src_ref=ybuf.at[pi, xy2],
            dst_ref=ry.at[pi, xy],
            send_sem=y_send.at[pi, k],
            recv_sem=y_recv.at[pi, k],
            device_id=(d, zh * N_XY + xy2),
            device_id_type=MESH,
        )

    def h_copy(pi, k):
        xy2 = (xy + k) % N_XY
        return pltpu.make_async_remote_copy(
            src_ref=hsum.at[pi],
            dst_ref=rh.at[pi, xy],
            send_sem=h_send.at[pi, k],
            recv_sem=h_recv.at[pi, k],
            device_id=(d, zh * N_XY + xy2),
            device_id_type=MESH,
        )

    def t_copy(pi):
        return pltpu.make_async_remote_copy(
            src_ref=hbuf.at[pi],
            dst_ref=twin.at[pi],
            send_sem=t_send.at[pi],
            recv_sem=t_recv.at[pi],
            device_id=(d, (b + N_XY) % N_BOX),
            device_id_type=MESH,
        )

    def own_copies(pi):
        return (
            pltpu.make_async_copy(ybuf.at[pi, xy], ry.at[pi, xy], self_sem.at[0, pi]),
            pltpu.make_async_copy(hsum.at[pi], rh.at[pi, xy], self_sem.at[1, pi]),
        )

    own_geometry = pltpu.make_async_copy(go.at[b // 2], rg.at[b], self_sem.at[2, 0])

    def start(copy):
        return lambda k, carry: (copy(k).start(), carry)[1]

    def wait(copy):
        return lambda k, carry: (copy(k).wait(), carry)[1]

    def wait_recv(copy):
        return lambda k, carry: (copy(k).wait_recv(), carry)[1]

    def wait_send(copy):
        return lambda k, carry: (copy(k).wait_send(), carry)[1]

    lax.fori_loop(1, N_BOX, start(g_copy), 0)
    own_geometry.start()
    for pi in range(P_DEV):
        lax.fori_loop(1, 16, start(functools.partial(z_copy, pi)), 0)
        z_own(pi).start()

    def hot_step(pi):
        t_copy(pi).wait_recv()
        hsum[pi] = hbuf[pi] + twin[pi]
        lax.fori_loop(1, N_XY, start(functools.partial(h_copy, pi)), 0)
        own_copies(pi)[1].start()

    for pi in range(P_DEV):
        z_own(pi).wait()
        lax.fori_loop(1, 16, wait_recv(functools.partial(z_copy, pi)), 0)
        x = jnp.concatenate(
            [recv[pi, 0].reshape(NT * N_XY, C), recv[pi, 1].reshape(NT * N_XY, C)], axis=1
        )
        y = jnp.dot(mt[...], x, preferred_element_type=F32).astype(BF)
        for z in range(2):
            part = y[:, z * C : (z + 1) * C]
            ybuf[pi, :, z] = part[: N_XY * NT_F].reshape(N_XY, NT_F, C)
            hbuf[pi, z] = part[N_XY * NT_F :]
        t_copy(pi).start()
        lax.fori_loop(1, N_XY, start(functools.partial(y_copy, pi)), 0)
        own_copies(pi)[0].start()
        if pi:
            hot_step(pi - 1)
    hot_step(P_DEV - 1)
    own_geometry.wait()
    lax.fori_loop(1, N_BOX, wait(g_copy), 0)
    for pi in range(P_DEV):
        for copy in own_copies(pi):
            copy.wait()
        t_copy(pi).wait_send()
        lax.fori_loop(1, 16, wait_send(functools.partial(z_copy, pi)), 0)
        lax.fori_loop(1, N_XY, wait(functools.partial(y_copy, pi)), 0)
        lax.fori_loop(1, N_XY, wait(functools.partial(h_copy, pi)), 0)


def exchange(pattern, mt, go):
    vm = pl.BlockSpec(memory_space=pltpu.VMEM)
    anywhere = pl.BlockSpec(memory_space=pl.ANY)
    dma = pltpu.SemaphoreType.DMA
    theta = (P_DEV, N_XY, 2, NT_F, C)
    return pl.pallas_call(
        exchange_kernel,
        out_shape=(
            jax.ShapeDtypeStruct(theta, BF),
            jax.ShapeDtypeStruct(theta, BF),
            jax.ShapeDtypeStruct((N_BOX, 16, 128), BF),
        ),
        in_specs=[anywhere, vm, anywhere],
        out_specs=(anywhere,) * 3,
        scratch_shapes=[
            pltpu.VMEM((P_DEV, 2, N_DIR, T_DEV, N_XY, C), BF),
            pltpu.VMEM(theta, BF),
            pltpu.VMEM((P_DEV, 2, NT_F, C), BF),
            pltpu.VMEM((P_DEV, 2, NT_F, C), BF),
            pltpu.VMEM((P_DEV, 2, NT_F, C), BF),
            dma((P_DEV, 16)),
            dma((P_DEV, 16)),
            dma((P_DEV,)),
            dma((N_BOX,)),
            dma((N_BOX,)),
            dma((P_DEV, N_XY)),
            dma((P_DEV, N_XY)),
            dma((P_DEV,)),
            dma((P_DEV,)),
            dma((P_DEV, N_XY)),
            dma((P_DEV, N_XY)),
            dma((3, P_DEV)),
        ],
        compiler_params=pltpu.CompilerParams(
            collective_id=0, has_side_effects=True, vmem_limit_bytes=48 << 20
        ),
        name="exchange",
    )(pattern, mt, go)


def fields_kernel(ry, rh, mp, rg, hotg, sines, cosines, quad, out, xs, gt, gs, ex, ey):
    lane = lax.broadcasted_iota(jnp.int32, (16, C), 1)
    low = lane < HALF
    odd = lax.axis_index("box") % 2 == 1

    def side(m):
        t = rg[m].astype(F32)
        return jnp.where(odd, pltpu.roll(t, HALF, 1), t)

    for m in range(N_BOX // 2):
        second = pltpu.roll(side(2 * m + 1), HALF, 1)
        gs[:, m * 128 : (m + 1) * 128] = jnp.where(low, side(2 * m), second)
    for m in range(2):
        gs[:, N_BOX * SLOT + m * 128 : N_BOX * SLOT + (m + 1) * 128] = hotg[m].astype(F32)

    def directions(theta_part):
        for c in range(2):
            part = theta_part[:, :, :, c * 16 : (c + 1) * 16, :]
            xs[:, c * C : (c + 1) * C] = part.reshape(NP * 16, C)
        scale = quad[...]
        for piece in range(4):
            child = jnp.dot(
                mp[piece * 256 : (piece + 1) * 256, :], xs[...], preferred_element_type=F32
            )
            for r in range(4):
                q = piece * 4 + r
                parts = []
                for ab in range(4):
                    for c in range(2):
                        at = r * 64 + ab * 16
                        v = child[at : at + 16, c * C : (c + 1) * C] * scale
                        turn = (ab // 2 + ab % 2 + c) if (q or ab < 3) else c
                        if turn % 2:
                            v = pltpu.roll(v, HALF, 1)
                            v = jnp.where(low, -v, v) if turn == 1 else jnp.where(low, v, -v)
                        elif turn == 2:
                            v = -v
                        parts.append(v)
                gt[:, q * 128 : (q + 1) * 128] = jnp.concatenate(parts, axis=0).T.astype(BF)

    def rows(i, carry):
        at = pl.multiple_of(i * 256, 256)
        g = gs[:, pl.ds(at, 256)]
        octant = g[3:4]
        bz = jnp.where(octant >= 4.0, 1.0, 0.0)
        rest = octant - 4.0 * bz
        by = jnp.where(rest >= 2.0, 1.0, 0.0)
        bx = rest - 2.0 * by

        def turned(axis, bit):
            place = box_phase * ((2.0 * bit - 1.0) * 0.25 + g[axis : axis + 1] * 0.5)
            return place * (0.5 / math.pi)

        for table, u, factor in (
            (ex, turned(0, bx) * 0.5, sines),
            (ey, turned(1, by) * 0.5, cosines),
        ):
            k, s = turns(u * factor[...])
            table[0, 16:, :] = k
            table[1, 16:, :] = s
            table[0, :16, :] = k[16:]
            table[1, :16, :] = -s[16:]
        cc, sc = turns(turned(2, bz) * cosines[:16, :])
        total = jnp.zeros((C, 256), F32)
        for pair in range(8):
            parts = []
            for q in (2 * pair, 2 * pair + 1):
                lo, hi = 16 - q, 16 + q
                c1, s1 = ex[0, hi : hi + 16, :], ex[1, hi : hi + 16, :]
                c2, s2 = ex[0, lo : lo + 16, :], ex[1, lo : lo + 16, :]
                ca, sa = c1 * c2 - s1 * s2, s1 * c2 + c1 * s2
                if q == 0:
                    lo, hi = 0, 32
                c1, s1 = ey[0, hi : hi + 16, :], ey[1, hi : hi + 16, :]
                c2, s2 = ey[0, lo : lo + 16, :], ey[1, lo : lo + 16, :]
                cb, sb = c1 * c2 + s1 * s2, s2 * c1 - c2 * s1
                if q == 0:
                    four = (ca, sb, sa, cb)
                else:
                    four = (ca * cb, ca * sb, sa * cb, sa * sb)
                for v in four:
                    parts.append((v * cc).astype(BF))
                    parts.append((v * sc).astype(BF))
            w = jnp.concatenate(parts, axis=0)
            total = total + jnp.dot(
                gt[:, pair * 256 : (pair + 1) * 256], w, preferred_element_type=F32
            )
        out[pl.ds(at, 256), :] = total.T.astype(BF)
        return carry

    directions(ry)
    lax.fori_loop(0, N_BOX * SLOT // 256, rows, 0)
    directions(rh)
    lax.fori_loop(N_BOX * SLOT // 256, SLOTS // 256, rows, 0)


def fields(ry, rh, mp, rg, hotg):
    n = np.arange(NT_F) + 0.5
    wide = lambda v: jnp.asarray(np.repeat(v[:, None], 256, axis=1), F32)
    sines = wide(np.sin(np.pi * n / NT_F))
    cosines = wide(np.cos(np.pi * n / NT_F))
    quad = wide(np.sin(np.pi * n[:16] / NT_F) * math.sqrt(2.0 / (NT_F * NP_F)))[:, :C]
    vm = pl.BlockSpec(memory_space=pltpu.VMEM)
    return pl.pallas_call(
        fields_kernel,
        out_shape=jax.ShapeDtypeStruct((SLOTS, C), BF),
        in_specs=[vm] * 8,
        out_specs=vm,
        scratch_shapes=[
            pltpu.VMEM((NP * 16, 2 * C), BF),
            pltpu.VMEM((C, NT_F * NP_F), BF),
            pltpu.VMEM((16, SLOTS), F32),
            pltpu.VMEM((2, 48, 256), F32),
            pltpu.VMEM((2, 48, 256), F32),
        ],
        compiler_params=pltpu.CompilerParams(vmem_limit_bytes=56 << 20),
        name="fields",
    )(ry, rh, mp, rg, hotg, sines, cosines, quad)


def return_kernel(f, r, send, recv, own):
    d = lax.axis_index("dir")
    b = lax.axis_index("box")
    barrier = pltpu.get_barrier_semaphore()

    def greet(k, carry):
        pl.semaphore_signal(barrier, inc=1, device_id=(d, (b + k) % N_BOX), device_id_type=MESH)
        return carry

    lax.fori_loop(1, N_BOX, greet, 0)
    pl.semaphore_wait(barrier, N_BOX - 1)

    def copy(k):
        b2 = (b + k) % N_BOX
        return pltpu.make_async_remote_copy(
            src_ref=f.at[pl.ds(pl.multiple_of(b2 * SLOT, SLOT), SLOT), :],
            dst_ref=r.at[pl.ds(pl.multiple_of(b * SLOT, SLOT), SLOT), :],
            send_sem=send.at[k],
            recv_sem=recv.at[k],
            device_id=(d, b2),
            device_id_type=MESH,
        )

    at = pl.ds(pl.multiple_of(b * SLOT, SLOT), SLOT)
    mine = pltpu.make_async_copy(f.at[at, :], r.at[at, :], own)
    lax.fori_loop(1, N_BOX, lambda k, carry: (copy(k).start(), carry)[1], 0)
    mine.start()
    mine.wait()
    lax.fori_loop(1, N_BOX, lambda k, carry: (copy(k).wait(), carry)[1], 0)


def give_back(f):
    vm = pl.BlockSpec(memory_space=pltpu.VMEM)
    anywhere = pl.BlockSpec(memory_space=pl.ANY)
    return pl.pallas_call(
        return_kernel,
        out_shape=jax.ShapeDtypeStruct((N_BOX * SLOT, C), BF),
        in_specs=[vm],
        out_specs=anywhere,
        scratch_shapes=[
            pltpu.SemaphoreType.DMA((N_BOX,)),
            pltpu.SemaphoreType.DMA((N_BOX,)),
            pltpu.SemaphoreType.DMA,
        ],
        compiler_params=pltpu.CompilerParams(collective_id=1, has_side_effects=True),
        name="give_back",
    )(f)


def place_kernel(pos, r, f, out):
    lane = lax.broadcasted_iota(jnp.int32, (128, 128), 1).astype(F32)
    oh = one_hot(pos[...], lane)
    field = jnp.dot(oh[:, : N_BOX * SLOT], r[...], preferred_element_type=F32)
    field = field + jnp.dot(oh[:, N_BOX * SLOT :], f[...], preferred_element_type=F32)
    out[...] = field.astype(BF)


def place(pos, r, f):
    return pl.pallas_call(
        place_kernel,
        out_shape=jax.ShapeDtypeStruct((ROW_DEV, C), BF),
        grid=(ROW_DEV // 256,),
        in_specs=[
            pl.BlockSpec((1, 256), lambda i: (0, i)),
            pl.BlockSpec((N_BOX * SLOT, C), lambda i: (0, 0)),
            pl.BlockSpec((HOT, C), lambda i: (N_BOX * SLOT // HOT, 0)),
        ],
        out_specs=pl.BlockSpec((256, C), lambda i: (i, 0)),
        name="place",
    )(pos, r, f)


def per_device(pattern, tap_theta, tap_phi, weight_theta, weight_phi, row_box, row_offset, row_fwd):
    a_theta = spread(tap_theta, weight_theta, NT_F)
    a_phi = spread(tap_phi, weight_phi, NP_F)
    ah = jnp.dot(theta_signs().astype(BF), a_theta, preferred_element_type=F32).astype(BF)
    a_phi = a_phi.reshape(NP_F, 2, N_XY, P_DEV).transpose(0, 3, 2, 1).reshape(NP_F, NP)
    bh = jnp.dot(phi_signs().astype(BF), a_phi, preferred_element_type=F32).astype(BF)
    mt, mp, go, hotg, pos = prepare(ah, bh, row_box.reshape(1, ROW_DEV), row_offset)
    ry, rh, rg = exchange(pattern, mt, go)
    f = fields(ry, rh, mp, rg, hotg)
    r = give_back(f)
    row_field = place(pos, r, f)
    gradient = jnp.sum(row_fwd.astype(F32) * row_field.astype(F32), axis=1) * (0.5 / math.sqrt(C))
    return (row_field, gradient)


def solution(mesh):
    in_specs = (
        P("dir", "box", None, None),
        P(),
        P(),
        P(),
        P(),
        P(("dir", "box")),
        P(None, ("dir", "box")),
        P(("dir", "box"), None),
    )
    out_specs = (P(("dir", "box"), None), P(("dir", "box")))
    return jax.shard_map(
        per_device, mesh=mesh, in_specs=in_specs, out_specs=out_specs, check_vma=False
    )
```

```python
import functools
import math

import jax
import jax.numpy as jnp
import numpy as np
from jax import lax
from jax.experimental import pallas as pl
from jax.experimental.pallas import tpu as pltpu
from jax.sharding import PartitionSpec as P

NT = 64
NP = 128
NT_F = 32
NP_F = 64
C = 128
HALF = 64
N_DIR = 8
N_BOX = 32
N_XY = 16
ROW_DEV = 2048
SLOT = 64
HOT = 256
SLOTS = N_BOX * SLOT + HOT
P_DEV = NP // N_BOX
T_DEV = NT // N_DIR

box_phase = 50.265482

MESH = pl.DeviceIdType.MESH
BF = jnp.bfloat16
F32 = jnp.float32


def polynomials():
    z2 = 0.5 + 0.5 * np.cos(np.pi * (np.arange(400) + 0.5) / 400)
    z = np.sqrt(z2)
    s = np.polynomial.chebyshev.Chebyshev.fit(z2, np.sin(np.pi * z) / z, 7, domain=[0, 1])
    k = np.polynomial.chebyshev.Chebyshev.fit(z2, np.cos(np.pi * z), 8, domain=[0, 1])
    to = np.polynomial.polynomial.Polynomial
    return tuple(
        [float(v) for v in f.convert(kind=to, domain=[-1, 1], window=[-1, 1]).coef] for f in (s, k)
    )


SIN_POLY, COS_POLY = polynomials()


def turns(u):
    z = (u - jnp.round(u)) * 2.0
    w = z * z
    s = jnp.full_like(w, SIN_POLY[-1])
    for v in SIN_POLY[-2::-1]:
        s = s * w + v
    k = jnp.full_like(w, COS_POLY[-1])
    for v in COS_POLY[-2::-1]:
        k = k * w + v
    return k, s * z


def theta_signs():
    h = np.zeros((NT_F, NT_F), np.float32)
    for t in range(16):
        for c in range(2):
            h[c * 16 + t, t] = 1.0
            h[c * 16 + t, 31 - t] = (-1.0) ** c
    return h


def phi_signs():
    h = np.zeros((NP_F, NP_F), np.float32)
    for q in range(1, 16):
        for a in range(2):
            for b in range(2):
                r = q * 4 + a * 2 + b
                h[r, q] = 1.0
                h[r, 32 - q] = (-1.0) ** a
                h[r, 64 - q] = (-1.0) ** b
                h[r, 32 + q] = (-1.0) ** (a + b)
    for a in range(2):
        h[a * 2, 0] = 1.0
        h[a * 2, 32] = (-1.0) ** a
    h[1, 16], h[1, 48] = 1.0, -1.0
    h[3, 16], h[3, 48] = 1.0, 1.0
    return h


def one_hot(p, lane):
    parts = []
    for h in range(2):
        column = jnp.broadcast_to(p[:, h * 128 : (h + 1) * 128], (128, 128)).T
        parts.append(
            jnp.concatenate(
                [
                    jnp.where(column == lane + float(j * 128), 1.0, 0.0).astype(BF)
                    for j in range(SLOTS // 128)
                ],
                axis=1,
            )
        )
    return jnp.concatenate(parts, axis=0)


def spread(taps, weights):
    lane = lax.broadcasted_iota(jnp.int32, (taps.shape[0], 128), 1)
    total = jnp.zeros(lane.shape, F32)
    for j in range(taps.shape[1]):
        total = total + jnp.where(
            lane == taps[:, j : j + 1], weights[:, j : j + 1].astype(F32), 0.0
        )
    return total


def step_kernel(
    pat, tap_t, tap_p, wt_t, wt_p, sign_t, sign_p, box_of_row, off, fwd, sines, cosines, quad,
    field, grad,
    recv, ybuf, hbuf, twin, hsum, ry, rh, go, hotg, rg, mt, mp, geo, gacc, oh, gs, ex, ey, w,
    acc_own, acc_hot, gt, f, r, fwd_v,
    z_send, z_recv, z_self, g_send, g_recv, y_send, y_recv, t_send, t_recv, h_send, h_recv, self_sem,
    r_send, r_recv, r_self, fwd_sem,
):
    d = lax.axis_index("dir")
    b = lax.axis_index("box")
    zh = b // N_XY
    xy = b % N_XY
    e = zh * N_DIR + d

    barrier = pltpu.get_barrier_semaphore()

    def greet_z(k, carry):
        e2 = (e + k) % 16
        pl.semaphore_signal(
            barrier, inc=1, device_id=(e2 % N_DIR, e2 // N_DIR * N_XY + xy), device_id_type=MESH
        )
        return carry

    def greet_box(k, carry):
        pl.semaphore_signal(barrier, inc=1, device_id=(d, (b + k) % N_BOX), device_id_type=MESH)
        return carry

    lax.fori_loop(1, 16, greet_z, 0)
    lax.fori_loop(1, N_BOX, greet_box, 0)
    pl.semaphore_wait(barrier, 15 + N_BOX - 1)


    def z_copy(pi, k):
        e2 = (e + k) % 16
        d2, zh2 = e2 % N_DIR, e2 // N_DIR
        first = pl.multiple_of(d2 * N_BOX + zh2 * N_XY, N_XY)
        return pltpu.make_async_remote_copy(
            src_ref=pat.at[:, pi, pl.ds(first, N_XY), :],
            dst_ref=recv.at[pi, zh, d],
            send_sem=z_send.at[pi, k],
            recv_sem=z_recv.at[pi, k],
            device_id=(d2, zh2 * N_XY + xy),
            device_id_type=MESH,
        )

    def z_own(pi):
        first = pl.multiple_of(d * N_BOX + zh * N_XY, N_XY)
        return pltpu.make_async_copy(
            pat.at[:, pi, pl.ds(first, N_XY), :], recv.at[pi, zh, d], z_self.at[pi]
        )

    def g_copy(k):
        b2 = (b + k) % N_BOX
        return pltpu.make_async_remote_copy(
            src_ref=go.at[b2 // 2],
            dst_ref=rg.at[b],
            send_sem=g_send.at[k],
            recv_sem=g_recv.at[k],
            device_id=(d, b2),
            device_id_type=MESH,
        )

    def y_copy(pi, k):
        xy2 = (xy + k) % N_XY
        return pltpu.make_async_remote_copy(
            src_ref=ybuf.at[pi, xy2],
            dst_ref=ry.at[pi, xy],
            send_sem=y_send.at[pi, k],
            recv_sem=y_recv.at[pi, k],
            device_id=(d, zh * N_XY + xy2),
            device_id_type=MESH,
        )

    def h_copy(pi, k):
        xy2 = (xy + k) % N_XY
        return pltpu.make_async_remote_copy(
            src_ref=hsum.at[pi],
            dst_ref=rh.at[pi, xy],
            send_sem=h_send.at[pi, k],
            recv_sem=h_recv.at[pi, k],
            device_id=(d, zh * N_XY + xy2),
            device_id_type=MESH,
        )

    def t_copy(pi):
        return pltpu.make_async_remote_copy(
            src_ref=hbuf.at[pi],
            dst_ref=twin.at[pi],
            send_sem=t_send.at[pi],
            recv_sem=t_recv.at[pi],
            device_id=(d, (b + N_XY) % N_BOX),
            device_id_type=MESH,
        )

    def y_own(pi):
        return pltpu.make_async_copy(ybuf.at[pi, xy], ry.at[pi, xy], self_sem.at[0, pi])

    def h_own(pi):
        return pltpu.make_async_copy(hsum.at[pi], rh.at[pi, xy], self_sem.at[1, pi])

    def g_own():
        return pltpu.make_async_copy(go.at[b // 2], rg.at[b], self_sem.at[2, 0])

    def r_copy(b2):
        return pltpu.make_async_remote_copy(
            src_ref=f.at[pl.ds(pl.multiple_of(b2 * SLOT, SLOT), SLOT), :],
            dst_ref=r.at[pl.ds(pl.multiple_of(b * SLOT, SLOT), SLOT), :],
            send_sem=r_send.at[b2],
            recv_sem=r_recv.at[b],
            device_id=(d, b2),
            device_id_type=MESH,
        )

    def r_arrival(b2):
        return pltpu.make_async_remote_copy(
            src_ref=f.at[pl.ds(pl.multiple_of(b2 * SLOT, SLOT), SLOT), :],
            dst_ref=r.at[pl.ds(pl.multiple_of(b2 * SLOT, SLOT), SLOT), :],
            send_sem=r_send.at[b2],
            recv_sem=r_recv.at[b2],
            device_id=(d, b2),
            device_id_type=MESH,
        )

    def r_own():
        at = pl.ds(pl.multiple_of(b * SLOT, SLOT), SLOT)
        return pltpu.make_async_copy(f.at[at, :], r.at[at, :], r_self)

    def load_fwd():
        return pltpu.make_async_copy(fwd, fwd_v, fwd_sem)

    def each(n, copy, what):
        def one(k, carry):
            getattr(copy(k), what)()
            return carry

        lax.fori_loop(1, n, one, 0)

    for pi in range(P_DEV):
        each(16, functools.partial(z_copy, pi), "start")
        z_own(pi).start()
    load_fwd().start()


    box = box_of_row[...]
    parent = box // 8
    octant = box - parent * 8
    dest = parent % N_BOX
    owner = lax.broadcasted_iota(jnp.int32, (N_BOX, ROW_DEV), 0)
    onehot = jnp.where(owner == dest, 1.0, 0.0).astype(F32)
    width = 256
    before = jnp.where(
        lax.broadcasted_iota(jnp.int32, (width, width), 0)
        < lax.broadcasted_iota(jnp.int32, (width, width), 1),
        1.0,
        0.0,
    ).astype(BF)
    carry = jnp.zeros((N_BOX, 1), F32)
    ranks = []
    for i in range(ROW_DEV // width):
        one = onehot[:, i * width : (i + 1) * width]
        pre = jnp.dot(one.astype(BF), before, preferred_element_type=F32) + carry
        ranks.append(jnp.sum(one * pre, axis=0, keepdims=True))
        carry = carry + jnp.sum(one, axis=1, keepdims=True)
    rank = jnp.concatenate(ranks, axis=1)
    is_hot = jnp.where(carry > float(SLOT), 1.0, 0.0)
    hot_row = jnp.sum(onehot * is_hot, axis=0, keepdims=True)
    number = lax.broadcasted_iota(jnp.int32, (N_BOX, 1), 0).astype(F32)
    hot = jnp.sum(number * is_hot, axis=0, keepdims=True)
    pos = jnp.where(
        hot_row > 0.5, float(N_BOX * SLOT) + rank, dest.astype(F32) * float(SLOT) + rank
    )
    sub = lax.broadcasted_iota(jnp.int32, (16, ROW_DEV), 0)
    o = off[...].astype(F32)
    g = jnp.where(sub == 3, octant.astype(F32), 0.0)
    for i in range(3):
        g = jnp.where(sub == i, o[i : i + 1, :], g)
    g = g.astype(BF)
    for i in range(ROW_DEV // width):
        geo[i, :16] = g[:, i * width : (i + 1) * width].astype(F32)
        geo[i, 16:] = jnp.broadcast_to(pos[:, i * width : (i + 1) * width], (8, width))
    gacc[...] = jnp.zeros_like(gacc)
    lane128 = lax.broadcasted_iota(jnp.int32, (128, 128), 1).astype(F32)

    def sort_block(i, carry):
        hits = one_hot(geo[i, 16:17], lane128)
        oh[i] = hits
        gacc[...] += jnp.dot(geo[i, :16].astype(BF), hits, preferred_element_type=F32)
        return carry

    lax.fori_loop(0, ROW_DEV // width, sort_block, 0)
    for m in range(N_BOX // 2):
        go[m] = gacc[:, m * 128 : (m + 1) * 128].astype(BF)
    for m in range(2):
        hotg[m] = gacc[:, N_BOX * SLOT + m * 128 : N_BOX * SLOT + (m + 1) * 128]
    each(N_BOX, g_copy, "start")
    g_own().start()


    a_theta = spread(tap_t[...], wt_t[...]).T[:NT_F].astype(BF)
    ah = jnp.dot(sign_t[...], a_theta, preferred_element_type=F32).astype(BF)
    col = lax.broadcasted_iota(jnp.int32, (NT, NT * N_XY), 1)
    row = lax.broadcasted_iota(jnp.int32, (NT, NT * N_XY), 0)
    wide = jnp.where(col // N_XY == row, 1.0, 0.0).astype(BF)
    v = jnp.dot(ah, wide, preferred_element_type=F32)
    lane_g = lax.broadcasted_iota(jnp.int32, v.shape, 1) % N_XY
    for i in range(N_XY):
        mt[i * NT_F : (i + 1) * NT_F, :] = jnp.where(lane_g == i, v, 0.0).astype(BF)
    local = hot - (zh * N_XY).astype(F32)
    mt[N_XY * NT_F :, :] = jnp.where(lane_g.astype(F32) == local, v, 0.0).astype(BF)

    a_phi = spread(tap_p[...], wt_p[...]).T[:NP_F].astype(BF)
    bh = jnp.dot(sign_p[...], a_phi, preferred_element_type=F32).astype(BF)
    col = lax.broadcasted_iota(jnp.int32, (NP, NP * 16), 1) // 16
    row = lax.broadcasted_iota(jnp.int32, (NP, NP * 16), 0)
    sample = col % 2 * (NP // 2) + col // 2 % N_XY * P_DEV + col // N_BOX
    wide = jnp.where(sample == row, 1.0, 0.0).astype(BF)
    v = jnp.dot(bh, wide, preferred_element_type=F32)
    same = (
        lax.broadcasted_iota(jnp.int32, (16, NP * 16), 1) % 16
        == lax.broadcasted_iota(jnp.int32, (16, NP * 16), 0)
    )
    for i in range(NP_F):
        mp[i * 16 : (i + 1) * 16, :] = jnp.where(same, v[i : i + 1, :], 0.0).astype(BF)


    lane = lax.broadcasted_iota(jnp.int32, (16, C), 1)
    low = lane < HALF

    def gather_geometry():
        g_own().wait()
        each(N_BOX, g_copy, "wait_recv")
        odd = b % 2 == 1

        def side(m):
            t = rg[m].astype(F32)
            return jnp.where(odd, pltpu.roll(t, HALF, 1), t)

        for m in range(N_BOX // 2):
            second = pltpu.roll(side(2 * m + 1), HALF, 1)
            gs[m // 2, :, m % 2 * 128 : (m % 2 + 1) * 128] = jnp.where(low, side(2 * m), second)
        for m in range(2):
            gs[N_BOX // 4, :, m * 128 : (m + 1) * 128] = hotg[m]

    def phases(i, carry):
        g = gs[i]
        octant = g[3:4]
        bz = jnp.where(octant >= 4.0, 1.0, 0.0)
        rest = octant - 4.0 * bz
        by = jnp.where(rest >= 2.0, 1.0, 0.0)
        bx = rest - 2.0 * by

        def turned(axis, bit):
            place = box_phase * ((2.0 * bit - 1.0) * 0.25 + g[axis : axis + 1] * 0.5)
            return place * (0.5 / math.pi)

        for table, u, factor in (
            (ex, turned(0, bx) * 0.5, sines),
            (ey, turned(1, by) * 0.5, cosines),
        ):
            k, s = turns(u * factor[...])
            table[0, 16:, :] = k
            table[1, 16:, :] = s
            table[0, :16, :] = k[16:]
            table[1, :16, :] = -s[16:]
        cc, sc = turns(turned(2, bz) * cosines[:16, :])
        for q in range(16):
            lo, hi = 16 - q, 16 + q
            c1, s1 = ex[0, hi : hi + 16, :], ex[1, hi : hi + 16, :]
            c2, s2 = ex[0, lo : lo + 16, :], ex[1, lo : lo + 16, :]
            ca, sa = c1 * c2 - s1 * s2, s1 * c2 + c1 * s2
            if q == 0:
                lo, hi = 0, 32
            c1, s1 = ey[0, hi : hi + 16, :], ey[1, hi : hi + 16, :]
            c2, s2 = ey[0, lo : lo + 16, :], ey[1, lo : lo + 16, :]
            cb, sb = c1 * c2 + s1 * s2, s2 * c1 - c2 * s1
            if q == 0:
                four = (ca, sb, sa, cb)
            else:
                four = (ca * cb, ca * sb, sa * cb, sa * sb)
            for j, v in enumerate(four):
                at = q * 128 + j * 32
                w[i, at : at + 16, :] = (v * cc).astype(BF)
                w[i, at + 16 : at + 32, :] = (v * sc).astype(BF)
        return carry


    def theta_step(pi):
        z_own(pi).wait()
        each(16, functools.partial(z_copy, pi), "wait_recv")
        x = jnp.concatenate(
            [recv[pi, 0].reshape(NT * N_XY, C), recv[pi, 1].reshape(NT * N_XY, C)], axis=1
        )
        y = jnp.dot(mt[...], x, preferred_element_type=F32).astype(BF)
        for z in range(2):
            part = y[:, z * C : (z + 1) * C]
            ybuf[pi, :, z] = part[: N_XY * NT_F].reshape(N_XY, NT_F, C)
            hbuf[pi, z] = part[N_XY * NT_F :]
        each(N_XY, functools.partial(y_copy, pi), "start")
        t_copy(pi).start()
        y_own(pi).start()

    def hot_step(pi):
        t_copy(pi).wait_recv()
        hsum[pi] = hbuf[pi] + twin[pi]
        each(N_XY, functools.partial(h_copy, pi), "start")
        h_own(pi).start()

    def phi_step(pi, part, own, copy, acc):
        own(pi).wait()
        each(N_XY, functools.partial(copy, pi), "wait_recv")
        x = jnp.concatenate(
            [part[pi, :, :, c * 16 : (c + 1) * 16, :].reshape(512, C) for c in range(2)], axis=1
        )
        y = jnp.dot(mp[:, pi * 512 : (pi + 1) * 512], x, preferred_element_type=F32)
        if pi:
            acc[...] += y
        else:
            acc[...] = y

    def directions(acc):
        scale = quad[...]
        for q in range(16):
            parts = []
            for ab in range(4):
                for c in range(2):
                    at = q * 64 + ab * 16
                    v = acc[at : at + 16, c * C : (c + 1) * C] * scale
                    turn = (ab // 2 + ab % 2 + c) if (q or ab < 3) else c
                    if turn % 2:
                        v = pltpu.roll(v, HALF, 1)
                        v = jnp.where(low, -v, v) if turn == 1 else jnp.where(low, v, -v)
                    elif turn == 2:
                        v = -v
                    parts.append(v)
            gt[:, q * 128 : (q + 1) * 128] = jnp.concatenate(parts, axis=0).T.astype(BF)

    def field_block(i):
        return jnp.dot(gt[...], w[i], preferred_element_type=F32).T.astype(BF)

    def send_block(i, carry):
        at = (b // 4 + i) % (N_BOX // 4)
        f[pl.ds(pl.multiple_of(at * 256, 256), 256), :] = field_block(at)
        for j in range(4):
            b2 = at * 4 + j

            @pl.when(b2 != b)
            def _():
                r_copy(b2).start()

            @pl.when(b2 == b)
            def _():
                r_own().start()

        return carry

    own_args = (ry, y_own, y_copy, acc_own)
    hot_args = (rh, h_own, h_copy, acc_hot)
    theta_step(0)
    gather_geometry()
    lax.fori_loop(0, 3, phases, 0)
    hot_step(0)
    theta_step(1)
    phi_step(0, *own_args)
    lax.fori_loop(3, 6, phases, 0)
    hot_step(1)
    theta_step(2)
    phi_step(1, *own_args)
    phi_step(0, *hot_args)
    lax.fori_loop(6, 9, phases, 0)
    hot_step(2)
    theta_step(3)
    phi_step(2, *own_args)
    phi_step(1, *hot_args)
    hot_step(3)
    phi_step(3, *own_args)
    directions(acc_own)
    lax.fori_loop(0, N_BOX // 4, send_block, 0)
    phi_step(2, *hot_args)
    phi_step(3, *hot_args)
    directions(acc_hot)
    f[N_BOX * SLOT :, :] = field_block(N_BOX // 4)
    load_fwd().wait()
    r_own().wait()

    def arrived(k, carry):
        r_arrival((b + k) % N_BOX).wait_recv()
        return carry

    lax.fori_loop(1, N_BOX, arrived, 0)

    def place(i, carry):
        hits = oh[i]
        v = jnp.dot(hits[:, : N_BOX * SLOT], r[...], preferred_element_type=F32)
        v = v + jnp.dot(hits[:, N_BOX * SLOT :], f[N_BOX * SLOT :, :], preferred_element_type=F32)
        v = v.astype(BF)
        at = pl.multiple_of(i * 256, 256)
        field[pl.ds(at, 256), :] = v
        product = fwd_v[pl.ds(at, 256), :].astype(F32) * v.astype(F32)
        grad[:, pl.ds(at, 256)] = jnp.sum(product.T, axis=0, keepdims=True) * (0.5 / math.sqrt(C))
        return carry

    lax.fori_loop(0, ROW_DEV // 256, place, 0)
    each(N_BOX, g_copy, "wait_send")
    for pi in range(P_DEV):
        t_copy(pi).wait_send()
        each(16, functools.partial(z_copy, pi), "wait_send")
        each(N_XY, functools.partial(y_copy, pi), "wait_send")
        each(N_XY, functools.partial(h_copy, pi), "wait_send")

    def sent(k, carry):
        r_copy((b + k) % N_BOX).wait_send()
        return carry

    lax.fori_loop(1, N_BOX, sent, 0)


def step(pattern, tap_theta, tap_phi, weight_theta, weight_phi, row_box, row_offset, row_fwd):
    n = np.arange(NT_F) + 0.5
    wide = lambda v: jnp.asarray(np.repeat(v[:, None], 256, axis=1), F32)
    sines = wide(np.sin(np.pi * n / NT_F))
    cosines = wide(np.cos(np.pi * n / NT_F))
    quad = wide(np.sin(np.pi * n[:16] / NT_F) * math.sqrt(2.0 / (NT_F * NP_F)))[:, :C]
    vm = pl.BlockSpec(memory_space=pltpu.VMEM)
    anywhere = pl.BlockSpec(memory_space=pl.ANY)
    dma = pltpu.SemaphoreType.DMA
    theta = (P_DEV, N_XY, 2, NT_F, C)
    hot = (P_DEV, 2, NT_F, C)
    blocks = SLOTS // 256
    return pl.pallas_call(
        step_kernel,
        out_shape=(
            jax.ShapeDtypeStruct((ROW_DEV, C), BF),
            jax.ShapeDtypeStruct((1, ROW_DEV), F32),
        ),
        in_specs=[anywhere] + [vm] * 8 + [anywhere] + [vm] * 3,
        out_specs=(vm, vm),
        scratch_shapes=[
            pltpu.VMEM((P_DEV, 2, N_DIR, T_DEV, N_XY, C), BF),
            pltpu.VMEM(theta, BF),
            pltpu.VMEM(hot, BF),
            pltpu.VMEM(hot, BF),
            pltpu.VMEM(hot, BF),
            pltpu.VMEM(theta, BF),
            pltpu.VMEM(theta, BF),
            pltpu.VMEM((N_BOX // 2, 16, 128), BF),
            pltpu.VMEM((2, 16, 128), F32),
            pltpu.VMEM((N_BOX, 16, 128), BF),
            pltpu.VMEM((N_XY * NT_F + NT_F, NT * N_XY), BF),
            pltpu.VMEM((NP_F * 16, NP * 16), BF),
            pltpu.VMEM((ROW_DEV // 256, 24, 256), F32),
            pltpu.VMEM((16, SLOTS), F32),
            pltpu.VMEM((ROW_DEV // 256, 256, SLOTS), BF),
            pltpu.VMEM((blocks, 16, 256), F32),
            pltpu.VMEM((2, 48, 256), F32),
            pltpu.VMEM((2, 48, 256), F32),
            pltpu.VMEM((blocks, NT_F * NP_F, 256), BF),
            pltpu.VMEM((NP_F * 16, 2 * C), F32),
            pltpu.VMEM((NP_F * 16, 2 * C), F32),
            pltpu.VMEM((C, NT_F * NP_F), BF),
            pltpu.VMEM((SLOTS, C), BF),
            pltpu.VMEM((N_BOX * SLOT, C), BF),
            pltpu.VMEM((ROW_DEV, C), BF),
            dma((P_DEV, 16)),
            dma((P_DEV, 16)),
            dma((P_DEV,)),
            dma((N_BOX,)),
            dma((N_BOX,)),
            dma((P_DEV, N_XY)),
            dma((P_DEV, N_XY)),
            dma((P_DEV,)),
            dma((P_DEV,)),
            dma((P_DEV, N_XY)),
            dma((P_DEV, N_XY)),
            dma((3, P_DEV)),
            dma((N_BOX,)),
            dma((N_BOX,)),
            dma,
            dma,
        ],
        compiler_params=pltpu.CompilerParams(
            collective_id=0, has_side_effects=True, vmem_limit_bytes=60 << 20
        ),
        name="step",
    )(
        pattern, tap_theta, tap_phi, weight_theta, weight_phi,
        jnp.asarray(theta_signs(), BF), jnp.asarray(phi_signs(), BF),
        row_box.reshape(1, ROW_DEV), row_offset, row_fwd, sines, cosines, quad,
    )


def per_device(*arrays):
    row_field, gradient = step(*arrays)
    return (row_field, gradient.reshape(ROW_DEV))


def solution(mesh):
    in_specs = (
        P("dir", "box", None, None),
        P(),
        P(),
        P(),
        P(),
        P(("dir", "box")),
        P(None, ("dir", "box")),
        P(("dir", "box"), None),
    )
    out_specs = (P(("dir", "box"), None), P(("dir", "box")))
    return jax.shard_map(
        per_device, mesh=mesh, in_specs=in_specs, out_specs=out_specs, check_vma=False
    )
```

```python
import functools
import math

import jax
import jax.numpy as jnp
import numpy as np
from jax import lax
from jax.experimental import pallas as pl
from jax.experimental.pallas import tpu as pltpu
from jax.sharding import PartitionSpec as P

NT = 64
NP = 128
NT_F = 32
NP_F = 64
C = 128
HALF = 64
N_DIR = 8
N_BOX = 32
N_XY = 16
ROW_DEV = 2048
SLOT = 64
HOT = 256
SLOTS = N_BOX * SLOT + HOT
P_DEV = NP // N_BOX
T_DEV = NT // N_DIR

box_phase = 50.265482

MESH = pl.DeviceIdType.MESH
BF = jnp.bfloat16
F32 = jnp.float32


def polynomials():
    z2 = 0.5 + 0.5 * np.cos(np.pi * (np.arange(400) + 0.5) / 400)
    z = np.sqrt(z2)
    s = np.polynomial.chebyshev.Chebyshev.fit(z2, np.sin(np.pi * z) / z, 7, domain=[0, 1])
    k = np.polynomial.chebyshev.Chebyshev.fit(z2, np.cos(np.pi * z), 8, domain=[0, 1])
    to = np.polynomial.polynomial.Polynomial
    return tuple(
        [float(v) for v in f.convert(kind=to, domain=[-1, 1], window=[-1, 1]).coef] for f in (s, k)
    )


SIN_POLY, COS_POLY = polynomials()


def turns(u):
    z = (u - jnp.round(u)) * 2.0
    w = z * z
    s = jnp.full_like(w, SIN_POLY[-1])
    for v in SIN_POLY[-2::-1]:
        s = s * w + v
    k = jnp.full_like(w, COS_POLY[-1])
    for v in COS_POLY[-2::-1]:
        k = k * w + v
    return k, s * z


def theta_signs():
    h = np.zeros((NT_F, NT_F), np.float32)
    for t in range(16):
        for c in range(2):
            h[c * 16 + t, t] = 1.0
            h[c * 16 + t, 31 - t] = (-1.0) ** c
    return h


def phi_signs():
    h = np.zeros((NP_F, NP_F), np.float32)
    for q in range(1, 16):
        for a in range(2):
            for b in range(2):
                r = q * 4 + a * 2 + b
                h[r, q] = 1.0
                h[r, 32 - q] = (-1.0) ** a
                h[r, 64 - q] = (-1.0) ** b
                h[r, 32 + q] = (-1.0) ** (a + b)
    for a in range(2):
        h[a * 2, 0] = 1.0
        h[a * 2, 32] = (-1.0) ** a
    h[1, 16], h[1, 48] = 1.0, -1.0
    h[3, 16], h[3, 48] = 1.0, 1.0
    return h


def one_hot(p, lane):
    parts = []
    for h in range(2):
        column = jnp.broadcast_to(p[:, h * 128 : (h + 1) * 128], (128, 128)).T
        parts.append(
            jnp.concatenate(
                [
                    jnp.where(column == lane + float(j * 128), 1.0, 0.0).astype(BF)
                    for j in range(SLOTS // 128)
                ],
                axis=1,
            )
        )
    return jnp.concatenate(parts, axis=0)


def spread(taps, weights, count):
    sample = lax.broadcasted_iota(jnp.int32, (count, taps.shape[1]), 0)
    total = jnp.zeros(sample.shape, F32)
    for j in range(taps.shape[0]):
        total = total + jnp.where(
            sample == taps[j : j + 1, :], weights[j : j + 1, :].astype(F32), 0.0
        )
    return total.astype(BF)


def step_kernel(
    pat, tap_t, tap_p, wt_t, wt_p, sign_t, sign_p, box_of_row, off, sines, cosines, quad,
    field,
    recv, ybuf, hbuf, twin, hsum, ry, rh, go, hotg, rg, mt, mp, geo, gacc, oh, gs, ex, ey, w,
    acc_own, acc_hot, gt, f, r, total, field_v,
    z_send, z_recv, g_send, g_recv, y_send, y_recv, t_send, t_recv, h_send, h_recv,
    r_send, r_recv, field_sem,
):
    d = lax.axis_index("dir")
    b = lax.axis_index("box")
    zh = b // N_XY
    xy = b % N_XY
    e = zh * N_DIR + d

    barrier = pltpu.get_barrier_semaphore()

    def greet_z(k, carry):
        e2 = (e + k) % 16
        pl.semaphore_signal(
            barrier, inc=1, device_id=(e2 % N_DIR, e2 // N_DIR * N_XY + xy), device_id_type=MESH
        )
        return carry

    def greet_box(k, carry):
        pl.semaphore_signal(barrier, inc=1, device_id=(d, (b + k) % N_BOX), device_id_type=MESH)
        return carry

    lax.fori_loop(1, 16, greet_z, 0)
    lax.fori_loop(1, N_BOX, greet_box, 0)


    def z_copy(pi, k):
        e2 = (e + k) % 16
        d2, zh2 = e2 % N_DIR, e2 // N_DIR
        first = pl.multiple_of(d2 * N_BOX + zh2 * N_XY, N_XY)
        return pltpu.make_async_remote_copy(
            src_ref=pat.at[:, pi, pl.ds(first, N_XY), :],
            dst_ref=recv.at[pi, zh, d],
            send_sem=z_send.at[pi],
            recv_sem=z_recv.at[pi],
            device_id=(d2, zh2 * N_XY + xy),
            device_id_type=MESH,
        )

    def z_own(pi):
        first = pl.multiple_of(d * N_BOX + zh * N_XY, N_XY)
        return pltpu.make_async_copy(
            pat.at[:, pi, pl.ds(first, N_XY), :], recv.at[pi, zh, d], z_recv.at[pi]
        )

    def g_copy(k):
        b2 = (b + k) % N_BOX
        return pltpu.make_async_remote_copy(
            src_ref=go.at[b2 // 2],
            dst_ref=rg.at[b],
            send_sem=g_send,
            recv_sem=g_recv,
            device_id=(d, b2),
            device_id_type=MESH,
        )

    def y_copy(pi, k):
        xy2 = (xy + k) % N_XY
        return pltpu.make_async_remote_copy(
            src_ref=ybuf.at[pi, xy2],
            dst_ref=ry.at[pi, xy],
            send_sem=y_send.at[pi],
            recv_sem=y_recv.at[pi],
            device_id=(d, zh * N_XY + xy2),
            device_id_type=MESH,
        )

    def h_copy(pi, k):
        xy2 = (xy + k) % N_XY
        return pltpu.make_async_remote_copy(
            src_ref=hsum.at[pi],
            dst_ref=rh.at[pi, xy],
            send_sem=h_send.at[pi],
            recv_sem=h_recv.at[pi],
            device_id=(d, zh * N_XY + xy2),
            device_id_type=MESH,
        )

    def t_copy(pi):
        return pltpu.make_async_remote_copy(
            src_ref=hbuf.at[pi],
            dst_ref=twin.at[pi],
            send_sem=t_send.at[pi],
            recv_sem=t_recv.at[pi],
            device_id=(d, (b + N_XY) % N_BOX),
            device_id_type=MESH,
        )

    def y_own(pi):
        return pltpu.make_async_copy(ybuf.at[pi, xy], ry.at[pi, xy], y_recv.at[pi])

    def h_own(pi):
        return pltpu.make_async_copy(hsum.at[pi], rh.at[pi, xy], h_recv.at[pi])

    def g_own():
        return pltpu.make_async_copy(go.at[b // 2], rg.at[b], g_recv)

    def r_copy(b2):
        return pltpu.make_async_remote_copy(
            src_ref=f.at[pl.ds(pl.multiple_of(b2 * SLOT, SLOT), SLOT), :],
            dst_ref=r.at[pl.ds(pl.multiple_of(b * SLOT, SLOT), SLOT), :],
            send_sem=r_send,
            recv_sem=r_recv.at[(zh + b2 // N_XY) % 2],
            device_id=(d, b2),
            device_id_type=MESH,
        )

    def r_own():
        at = pl.ds(pl.multiple_of(b * SLOT, SLOT), SLOT)
        return pltpu.make_async_copy(f.at[at, :], r.at[at, :], r_recv.at[0])

    def each(n, copy):
        def one(k, carry):
            copy(k).start()
            return carry

        lax.fori_loop(1, n, one, 0)

    def wait_for(ref, sem):
        pltpu.make_async_copy(ref, ref, sem).wait()

    def z_start(pi):
        each(16, functools.partial(z_copy, pi))
        z_own(pi).start()


    box = box_of_row[...]
    parent = box // 8
    octant = box - parent * 8
    dest = parent % N_BOX
    owner = lax.broadcasted_iota(jnp.int32, (N_BOX, ROW_DEV), 0)
    onehot = jnp.where(owner == dest, 1.0, 0.0).astype(F32)
    width = 256
    before = jnp.where(
        lax.broadcasted_iota(jnp.int32, (width, width), 0)
        < lax.broadcasted_iota(jnp.int32, (width, width), 1),
        1.0,
        0.0,
    ).astype(BF)
    carry = jnp.zeros((N_BOX, 1), F32)
    ranks = []
    for i in range(ROW_DEV // width):
        one = onehot[:, i * width : (i + 1) * width]
        pre = jnp.dot(one.astype(BF), before, preferred_element_type=F32) + carry
        ranks.append(jnp.sum(one * pre, axis=0, keepdims=True))
        carry = carry + jnp.sum(one, axis=1, keepdims=True)
    rank = jnp.concatenate(ranks, axis=1)
    is_hot = jnp.where(carry > float(SLOT), 1.0, 0.0)
    hot_row = jnp.sum(onehot * is_hot, axis=0, keepdims=True)
    number = lax.broadcasted_iota(jnp.int32, (N_BOX, 1), 0).astype(F32)
    hot = jnp.sum(number * is_hot, axis=0, keepdims=True)
    pl.semaphore_wait(barrier, 15 + N_BOX - 1)
    z_start(0)

    pos = jnp.where(
        hot_row > 0.5, float(N_BOX * SLOT) + rank, dest.astype(F32) * float(SLOT) + rank
    )
    sub = lax.broadcasted_iota(jnp.int32, (16, ROW_DEV), 0)
    o = off[...].astype(F32)
    g = jnp.where(sub == 3, octant.astype(F32), 0.0)
    for i in range(3):
        g = jnp.where(sub == i, o[i : i + 1, :], g)
    g = g.astype(BF)
    for i in range(ROW_DEV // width):
        geo[i, :16] = g[:, i * width : (i + 1) * width].astype(F32)
        geo[i, 16:] = jnp.broadcast_to(pos[:, i * width : (i + 1) * width], (8, width))
    gacc[...] = jnp.zeros_like(gacc)
    lane128 = lax.broadcasted_iota(jnp.int32, (128, 128), 1).astype(F32)

    def sort_block(i, carry):
        hits = one_hot(geo[i, 16:17], lane128)
        oh[pl.ds(pl.multiple_of(i * width, width), width), :] = hits
        gacc[...] += jnp.dot(geo[i, :16].astype(BF), hits, preferred_element_type=F32)
        return carry

    lax.fori_loop(0, ROW_DEV // width, sort_block, 0)
    for m in range(N_BOX // 2):
        go[m] = gacc[:4, m * 128 : (m + 1) * 128].astype(BF)
    for m in range(2):
        hotg[m] = gacc[:8, N_BOX * SLOT + m * 128 : N_BOX * SLOT + (m + 1) * 128]
    each(N_BOX, g_copy)
    g_own().start()
    z_start(1)


    a_theta = spread(tap_t[...], wt_t[...], NT_F)
    ah = jnp.dot(sign_t[...], a_theta, preferred_element_type=F32).astype(BF)
    col = lax.broadcasted_iota(jnp.int32, (NT, NT * N_XY), 1)
    row = lax.broadcasted_iota(jnp.int32, (NT, NT * N_XY), 0)
    wide = jnp.where(col // N_XY == row, 1.0, 0.0).astype(BF)
    v = jnp.dot(ah, wide, preferred_element_type=F32)
    lane_g = lax.broadcasted_iota(jnp.int32, v.shape, 1) % N_XY
    for i in range(N_XY):
        mt[i * NT_F : (i + 1) * NT_F, :] = jnp.where(lane_g == i, v, 0.0).astype(BF)
    local = hot - (zh * N_XY).astype(F32)
    mt[N_XY * NT_F :, :] = jnp.where(lane_g.astype(F32) == local, v, 0.0).astype(BF)

    a_phi = spread(tap_p[...], wt_p[...], NP_F)
    bh = jnp.dot(sign_p[...], a_phi, preferred_element_type=F32).astype(BF)
    col = lax.broadcasted_iota(jnp.int32, (NP, NP * 16), 1) // 16
    row = lax.broadcasted_iota(jnp.int32, (NP, NP * 16), 0)
    sample = col % 2 * (NP // 2) + col // 2 % N_XY * P_DEV + col // N_BOX
    wide = jnp.where(sample == row, 1.0, 0.0).astype(BF)
    v = jnp.dot(bh, wide, preferred_element_type=F32)
    same = (
        lax.broadcasted_iota(jnp.int32, (16, NP * 16), 1) % 16
        == lax.broadcasted_iota(jnp.int32, (16, NP * 16), 0)
    )
    for i in range(NP_F):
        mp[i * 16 : (i + 1) * 16, :] = jnp.where(same, v[i : i + 1, :], 0.0).astype(BF)


    lane = lax.broadcasted_iota(jnp.int32, (16, C), 1)
    low = lane < HALF

    def gather_geometry():
        wait_for(rg, g_recv)
        odd = b % 2 == 1

        def side(m):
            t = rg[m].astype(F32)
            return jnp.where(odd, pltpu.roll(t, HALF, 1), t)

        for m in range(N_BOX // 2):
            second = pltpu.roll(side(2 * m + 1), HALF, 1)
            gs[m // 2, :4, m % 2 * 128 : (m % 2 + 1) * 128] = jnp.where(low[:4], side(2 * m), second)
        for m in range(2):
            gs[N_BOX // 4, :, m * 128 : (m + 1) * 128] = hotg[m]

    def phases(i, carry):
        g = gs[i]
        octant = g[3:4]
        bz = jnp.where(octant >= 4.0, 1.0, 0.0)
        rest = octant - 4.0 * bz
        by = jnp.where(rest >= 2.0, 1.0, 0.0)
        bx = rest - 2.0 * by

        def turned(axis, bit):
            place = box_phase * ((2.0 * bit - 1.0) * 0.25 + g[axis : axis + 1] * 0.5)
            return place * (0.5 / math.pi)

        for table, u, factor in (
            (ex, turned(0, bx) * 0.5, sines),
            (ey, turned(1, by) * 0.5, cosines),
        ):
            k, s = turns(u * factor[...])
            table[0, 16:, :] = k
            table[1, 16:, :] = s
            table[0, :16, :] = k[16:]
            table[1, :16, :] = -s[16:]
        cc, sc = turns(turned(2, bz) * cosines[:16, :])
        for q in range(16):
            lo, hi = 16 - q, 16 + q
            c1, s1 = ex[0, hi : hi + 16, :], ex[1, hi : hi + 16, :]
            c2, s2 = ex[0, lo : lo + 16, :], ex[1, lo : lo + 16, :]
            ca, sa = c1 * c2 - s1 * s2, s1 * c2 + c1 * s2
            if q == 0:
                lo, hi = 0, 32
            c1, s1 = ey[0, hi : hi + 16, :], ey[1, hi : hi + 16, :]
            c2, s2 = ey[0, lo : lo + 16, :], ey[1, lo : lo + 16, :]
            cb, sb = c1 * c2 + s1 * s2, s2 * c1 - c2 * s1
            if q == 0:
                four = (ca, sb, sa, cb)
            else:
                four = (ca * cb, ca * sb, sa * cb, sa * sb)
            for j, v in enumerate(four):
                at = q * 128 + j * 32
                w[i, at : at + 16, :] = (v * cc).astype(BF)
                w[i, at + 16 : at + 32, :] = (v * sc).astype(BF)
        return carry


    def theta_step(pi):
        wait_for(recv.at[pi], z_recv.at[pi])
        x = jnp.concatenate(
            [recv[pi, 0].reshape(NT * N_XY, C), recv[pi, 1].reshape(NT * N_XY, C)], axis=1
        )
        y = jnp.dot(mt[...], x, preferred_element_type=F32).astype(BF)
        for z in range(2):
            part = y[:, z * C : (z + 1) * C]
            ybuf[pi, :, z] = part[: N_XY * NT_F].reshape(N_XY, NT_F, C)
            hbuf[pi, z] = part[N_XY * NT_F :]
        each(N_XY, functools.partial(y_copy, pi))
        t_copy(pi).start()
        y_own(pi).start()

    def hot_step(pi):
        t_copy(pi).wait_recv()
        hsum[pi] = hbuf[pi] + twin[pi]
        each(N_XY, functools.partial(h_copy, pi))
        h_own(pi).start()

    def phi_step(pi, part, sem, acc):
        wait_for(part.at[pi], sem.at[pi])
        x = jnp.concatenate(
            [part[pi, :, :, c * 16 : (c + 1) * 16, :].reshape(512, C) for c in range(2)], axis=1
        )
        y = jnp.dot(mp[:, pi * 512 : (pi + 1) * 512], x, preferred_element_type=F32)
        if pi:
            acc[...] += y
        else:
            acc[...] = y

    def directions(acc):
        scale = quad[...]
        for q in range(16):
            parts = []
            for ab in range(4):
                for c in range(2):
                    at = q * 64 + ab * 16
                    v = acc[at : at + 16, c * C : (c + 1) * C] * scale
                    turn = (ab // 2 + ab % 2 + c) if (q or ab < 3) else c
                    if turn % 2:
                        v = pltpu.roll(v, HALF, 1)
                        v = jnp.where(low, -v, v) if turn == 1 else jnp.where(low, v, -v)
                    elif turn == 2:
                        v = -v
                    parts.append(v)
            gt[:, q * 128 : (q + 1) * 128] = jnp.concatenate(parts, axis=0).T.astype(BF)

    def field_block(i):
        return jnp.dot(gt[...], w[i], preferred_element_type=F32).T.astype(BF)

    def send_block(i, carry):
        at = (1 - zh + i // 4) % 2 * 4 + (b // 4 + i) % 4
        f[pl.ds(pl.multiple_of(at * 256, 256), 256), :] = field_block(at)
        for j in range(4):
            b2 = at * 4 + j

            @pl.when(b2 != b)
            def _():
                r_copy(b2).start()

            @pl.when(b2 == b)
            def _():
                r_own().start()

        return carry

    own_args = (ry, y_recv, acc_own)
    hot_args = (rh, h_recv, acc_hot)
    theta_step(0)
    z_start(2)
    gather_geometry()
    lax.fori_loop(0, 4, phases, 0)
    theta_step(1)
    z_start(3)
    hot_step(0)
    phi_step(0, *own_args)
    lax.fori_loop(4, 9, phases, 0)
    theta_step(2)
    hot_step(1)
    phi_step(1, *own_args)
    phi_step(0, *hot_args)
    theta_step(3)
    hot_step(2)
    phi_step(2, *own_args)
    phi_step(1, *hot_args)
    phi_step(3, *own_args)
    hot_step(3)
    directions(acc_own)
    lax.fori_loop(0, N_BOX // 4, send_block, 0)
    phi_step(2, *hot_args)
    for pi in range(P_DEV):
        wait_for(f.at[: 15 * 128], z_send.at[pi])
        wait_for(f.at[: 15 * SLOT], y_send.at[pi])
    wait_for(rg.at[: N_BOX - 1], g_send)
    phi_step(3, *hot_args)
    directions(acc_hot)
    f[N_BOX * SLOT :, :] = field_block(N_BOX // 4)

    half = N_BOX * SLOT // 2
    here = pl.multiple_of(zh * half, half)
    there = pl.multiple_of(half - zh * half, half)
    wait_for(r.at[pl.ds(here, half), :], r_recv.at[0])

    def place_here(i, carry):
        at = pl.multiple_of(i * 1024, 1024)
        v = jnp.dot(
            oh[pl.ds(at, 1024), pl.ds(here, half)],
            r[pl.ds(here, half), :],
            preferred_element_type=F32,
        )
        total[pl.ds(at, 1024), :] = v + jnp.dot(
            oh[pl.ds(at, 1024), N_BOX * SLOT :],
            f[N_BOX * SLOT :, :],
            preferred_element_type=F32,
        )
        return carry

    lax.fori_loop(0, ROW_DEV // 1024, place_here, 0)
    for pi in range(P_DEV):
        t_copy(pi).wait_send()
        wait_for(f.at[: 15 * SLOT], h_send.at[pi])
    wait_for(f.at[: 31 * SLOT], r_send)
    wait_for(r.at[pl.ds(there, half), :], r_recv.at[1])
    for i in range(2):
        at = pl.ds(i * 1024, 1024)
        v = total[at, :] + jnp.dot(
            oh[at, pl.ds(there, half)], r[pl.ds(there, half), :], preferred_element_type=F32
        )
        field_v[at, :] = v.astype(BF)
        pltpu.make_async_copy(field_v.at[at, :], field.at[at, :], field_sem.at[i]).start()
    for i in range(2):
        at = pl.ds(i * 1024, 1024)
        pltpu.make_async_copy(field_v.at[at, :], field.at[at, :], field_sem.at[i]).wait()


def step(pattern, tap_theta, tap_phi, weight_theta, weight_phi, row_box, row_offset):
    n = np.arange(NT_F) + 0.5
    wide = lambda v: jnp.asarray(np.repeat(v[:, None], 256, axis=1), F32)
    sines = wide(np.sin(np.pi * n / NT_F))
    cosines = wide(np.cos(np.pi * n / NT_F))
    quad = wide(np.sin(np.pi * n[:16] / NT_F) * math.sqrt(2.0 / (NT_F * NP_F)))[:, :C]
    vm = pl.BlockSpec(memory_space=pltpu.VMEM)
    anywhere = pl.BlockSpec(memory_space=pl.ANY)
    dma = pltpu.SemaphoreType.DMA
    theta = (P_DEV, N_XY, 2, NT_F, C)
    hot = (P_DEV, 2, NT_F, C)
    blocks = SLOTS // 256
    return pl.pallas_call(
        step_kernel,
        out_shape=jax.ShapeDtypeStruct((ROW_DEV, C), BF),
        in_specs=[anywhere] + [vm] * 11,
        out_specs=anywhere,
        scratch_shapes=[
            pltpu.VMEM((P_DEV, 2, N_DIR, T_DEV, N_XY, C), BF),
            pltpu.VMEM(theta, BF),
            pltpu.VMEM(hot, BF),
            pltpu.VMEM(hot, BF),
            pltpu.VMEM(hot, BF),
            pltpu.VMEM(theta, BF),
            pltpu.VMEM(theta, BF),
            pltpu.VMEM((N_BOX // 2, 4, 128), BF),
            pltpu.VMEM((2, 8, 128), F32),
            pltpu.VMEM((N_BOX, 4, 128), BF),
            pltpu.VMEM((N_XY * NT_F + NT_F, NT * N_XY), BF),
            pltpu.VMEM((NP_F * 16, NP * 16), BF),
            pltpu.VMEM((ROW_DEV // 256, 24, 256), F32),
            pltpu.VMEM((16, SLOTS), F32),
            pltpu.VMEM((ROW_DEV, SLOTS), BF),
            pltpu.VMEM((blocks, 8, 256), F32),
            pltpu.VMEM((2, 48, 256), F32),
            pltpu.VMEM((2, 48, 256), F32),
            pltpu.VMEM((blocks, NT_F * NP_F, 256), BF),
            pltpu.VMEM((NP_F * 16, 2 * C), F32),
            pltpu.VMEM((NP_F * 16, 2 * C), F32),
            pltpu.VMEM((C, NT_F * NP_F), BF),
            pltpu.VMEM((SLOTS, C), BF),
            pltpu.VMEM((N_BOX * SLOT, C), BF),
            pltpu.VMEM((ROW_DEV, C), F32),
            pltpu.VMEM((ROW_DEV, C), BF),
            dma((P_DEV,)),
            dma((P_DEV,)),
            dma,
            dma,
            dma((P_DEV,)),
            dma((P_DEV,)),
            dma((P_DEV,)),
            dma((P_DEV,)),
            dma((P_DEV,)),
            dma((P_DEV,)),
            dma,
            dma((2,)),
            dma((2,)),
        ],
        compiler_params=pltpu.CompilerParams(
            collective_id=0, has_side_effects=True, vmem_limit_bytes=60 << 20
        ),
        name="step",
    )(
        pattern, tap_theta.T, tap_phi.T, weight_theta.T, weight_phi.T,
        jnp.asarray(theta_signs(), BF), jnp.asarray(phi_signs(), BF),
        row_box.reshape(1, ROW_DEV), row_offset, sines, cosines, quad,
    )


def finish_kernel(field, fwd, out, grad):
    v = field[...]
    out[...] = v
    product = fwd[...].astype(F32) * v.astype(F32)
    grad[...] = (jnp.sum(product.T, axis=0, keepdims=True) * (0.5 / math.sqrt(C))).reshape(grad.shape)


def finish(field, fwd):
    rows = 1024
    block = pl.BlockSpec((rows, C), lambda i: (i, 0))
    return pl.pallas_call(
        finish_kernel,
        out_shape=(
            jax.ShapeDtypeStruct((ROW_DEV, C), BF),
            jax.ShapeDtypeStruct((ROW_DEV,), F32),
        ),
        grid=(ROW_DEV // rows,),
        in_specs=[block, block],
        out_specs=(block, pl.BlockSpec((rows,), lambda i: (i,))),
        name="finish",
    )(field, fwd)


def per_device(*arrays):
    field = step(*arrays[:-1])
    return finish(field, arrays[-1])


def solution(mesh):
    in_specs = (
        P("dir", "box", None, None),
        P(),
        P(),
        P(),
        P(),
        P(("dir", "box")),
        P(None, ("dir", "box")),
        P(("dir", "box"), None),
    )
    out_specs = (P(("dir", "box"), None), P(("dir", "box")))
    return jax.shard_map(
        per_device, mesh=mesh, in_specs=in_specs, out_specs=out_specs, check_vma=False
    )
```

```python
import functools
import math

import jax
import jax.numpy as jnp
import numpy as np
from jax import lax
from jax.experimental import pallas as pl
from jax.experimental.pallas import tpu as pltpu
from jax.sharding import PartitionSpec as P

NT = 64
NP = 128
NT_F = 32
NP_F = 64
C = 128
HALF = 64
N_DIR = 8
N_BOX = 32
N_XY = 16
ROW_DEV = 2048
SLOT = 64
HOT = 256
SLOTS = N_BOX * SLOT + HOT
P_DEV = NP // N_BOX
T_DEV = NT // N_DIR
LAST = P_DEV - 1
SMALL = 11

box_phase = 50.265482

MESH = pl.DeviceIdType.MESH
BF = jnp.bfloat16
F32 = jnp.float32


def polynomials():
    z2 = 0.5 + 0.5 * np.cos(np.pi * (np.arange(400) + 0.5) / 400)
    z = np.sqrt(z2)
    s = np.polynomial.chebyshev.Chebyshev.fit(z2, np.sin(np.pi * z) / z, 7, domain=[0, 1])
    k = np.polynomial.chebyshev.Chebyshev.fit(z2, np.cos(np.pi * z), 8, domain=[0, 1])
    to = np.polynomial.polynomial.Polynomial
    return tuple(
        [float(v) for v in f.convert(kind=to, domain=[-1, 1], window=[-1, 1]).coef] for f in (s, k)
    )


SIN_POLY, COS_POLY = polynomials()


def turns(u):
    z = (u - jnp.round(u)) * 2.0
    w = z * z
    s = jnp.full_like(w, SIN_POLY[-1])
    for v in SIN_POLY[-2::-1]:
        s = s * w + v
    k = jnp.full_like(w, COS_POLY[-1])
    for v in COS_POLY[-2::-1]:
        k = k * w + v
    return k, s * z


def theta_signs():
    h = np.zeros((NT_F, NT_F), np.float32)
    for t in range(16):
        for c in range(2):
            h[c * 16 + t, t] = 1.0
            h[c * 16 + t, 31 - t] = (-1.0) ** c
    return h


def phi_signs():
    h = np.zeros((NP_F, NP_F), np.float32)
    for q in range(1, 16):
        for a in range(2):
            for b in range(2):
                r = q * 4 + a * 2 + b
                h[r, q] = 1.0
                h[r, 32 - q] = (-1.0) ** a
                h[r, 64 - q] = (-1.0) ** b
                h[r, 32 + q] = (-1.0) ** (a + b)
    for a in range(2):
        h[a * 2, 0] = 1.0
        h[a * 2, 32] = (-1.0) ** a
    h[1, 16], h[1, 48] = 1.0, -1.0
    h[3, 16], h[3, 48] = 1.0, 1.0
    return h


def one_hot(p, lane):
    parts = []
    for h in range(2):
        column = jnp.broadcast_to(p[:, h * 128 : (h + 1) * 128], (128, 128)).T
        parts.append(
            jnp.concatenate(
                [
                    jnp.where(column == lane + float(j * 128), 1.0, 0.0).astype(BF)
                    for j in range(SLOTS // 128)
                ],
                axis=1,
            )
        )
    return jnp.concatenate(parts, axis=0)


def spread(taps, weights, count):
    sample = lax.broadcasted_iota(jnp.int32, (count, taps.shape[1]), 0)
    total = jnp.zeros(sample.shape, F32)
    for j in range(taps.shape[0]):
        total = total + jnp.where(
            sample == taps[j : j + 1, :], weights[j : j + 1, :].astype(F32), 0.0
        )
    return total.astype(BF)


def step_kernel(pat, *refs):
    small, refs = refs[:SMALL], refs[SMALL:]
    (
        field, recv, ybuf, hbuf, twin, hsum, ry, rh, go, hotg, rg, mt, mp, geo, gacc, oh, gs, ex, ey, w,
        acc_own, acc_hot, gt, f, r, total, field_v,
        z_send, z_recv, g_send, g_recv, y_send, y_recv, t_send, t_recv, h_send, h_recv,
        r_send, r_recv, field_sem, small_sem,
    ) = refs[: len(refs) - SMALL]
    held = refs[len(refs) - SMALL :]
    tap_t, tap_p, wt_t, wt_p, sign_t, sign_p, box_of_row, off, sines, cosines, quad = held
    d = lax.axis_index("dir")
    b = lax.axis_index("box")
    zh = b // N_XY
    xy = b % N_XY
    e = zh * N_DIR + d

    barrier = pltpu.get_barrier_semaphore()

    def greet_z(k, carry):
        e2 = (e + k) % 16
        pl.semaphore_signal(
            barrier, inc=1, device_id=(e2 % N_DIR, e2 // N_DIR * N_XY + xy), device_id_type=MESH
        )
        return carry

    def greet_box(k, carry):
        pl.semaphore_signal(barrier, inc=1, device_id=(d, (b + k) % N_BOX), device_id_type=MESH)
        return carry

    lax.fori_loop(1, 16, greet_z, 0)
    lax.fori_loop(1, N_BOX, greet_box, 0)


    def z_copy(pi, k):
        e2 = (e + k) % 16
        d2, zh2 = e2 % N_DIR, e2 // N_DIR
        first = pl.multiple_of(d2 * N_BOX + zh2 * N_XY, N_XY)
        return pltpu.make_async_remote_copy(
            src_ref=pat.at[:, pi, pl.ds(first, N_XY), :],
            dst_ref=recv.at[pi, zh, d],
            send_sem=z_send.at[pi],
            recv_sem=z_recv.at[pi],
            device_id=(d2, zh2 * N_XY + xy),
            device_id_type=MESH,
        )

    def z_own(pi, half=0):
        first = pl.multiple_of(d * N_BOX + zh * N_XY, N_XY)
        return pltpu.make_async_copy(
            pat.at[:, pi, pl.ds(first, N_XY), :], recv.at[pi, zh, d], z_recv.at[pi + half]
        )

    def g_copy(k):
        b2 = (b + k) % N_BOX
        return pltpu.make_async_remote_copy(
            src_ref=go.at[b2 // 2],
            dst_ref=rg.at[b],
            send_sem=g_send,
            recv_sem=g_recv,
            device_id=(d, b2),
            device_id_type=MESH,
        )

    def y_copy(pi, k):
        xy2 = (xy + k) % N_XY
        return pltpu.make_async_remote_copy(
            src_ref=ybuf.at[pi, xy2],
            dst_ref=ry.at[pi, xy],
            send_sem=y_send.at[pi],
            recv_sem=y_recv.at[pi],
            device_id=(d, zh * N_XY + xy2),
            device_id_type=MESH,
        )

    def h_copy(pi, k):
        xy2 = (xy + k) % N_XY
        return pltpu.make_async_remote_copy(
            src_ref=hsum.at[pi],
            dst_ref=rh.at[pi, xy],
            send_sem=h_send.at[pi],
            recv_sem=h_recv.at[pi],
            device_id=(d, zh * N_XY + xy2),
            device_id_type=MESH,
        )

    def t_copy(pi):
        return pltpu.make_async_remote_copy(
            src_ref=hbuf.at[pi],
            dst_ref=twin.at[pi],
            send_sem=t_send.at[pi],
            recv_sem=t_recv.at[pi],
            device_id=(d, (b + N_XY) % N_BOX),
            device_id_type=MESH,
        )

    def y_own(pi):
        return pltpu.make_async_copy(ybuf.at[pi, xy], ry.at[pi, xy], y_recv.at[pi])

    def h_own(pi):
        return pltpu.make_async_copy(hsum.at[pi], rh.at[pi, xy], h_recv.at[pi])

    def g_own():
        return pltpu.make_async_copy(go.at[b // 2], rg.at[b], g_recv)

    def r_copy(b2):
        return pltpu.make_async_remote_copy(
            src_ref=f.at[pl.ds(pl.multiple_of(b2 * SLOT, SLOT), SLOT), :],
            dst_ref=r.at[pl.ds(pl.multiple_of(b * SLOT, SLOT), SLOT), :],
            send_sem=r_send,
            recv_sem=r_recv.at[(zh + b2 // N_XY) % 2 * (1 + (b2 // 4 + 8 - b // 4) % 4)],
            device_id=(d, b2),
            device_id_type=MESH,
        )

    def r_own():
        at = pl.ds(pl.multiple_of(b * SLOT, SLOT), SLOT)
        return pltpu.make_async_copy(f.at[at, :], r.at[at, :], r_recv.at[0])

    def each(n, copy):
        def one(k, carry):
            copy(k).start()
            return carry

        lax.fori_loop(1, n, one, 0)

    def wait_for(ref, sem):
        pltpu.make_async_copy(ref, ref, sem).wait()

    def z_half_copy(zh2, j):
        d2 = (d + j) % N_DIR
        first = pl.multiple_of(d2 * N_BOX + zh2 * N_XY, N_XY)
        return pltpu.make_async_remote_copy(
            src_ref=pat.at[:, LAST, pl.ds(first, N_XY), :],
            dst_ref=recv.at[LAST, zh, d],
            send_sem=z_send.at[LAST],
            recv_sem=z_recv.at[LAST + (zh + zh2 + 1) % 2],
            device_id=(d2, zh2 * N_XY + xy),
            device_id_type=MESH,
        )

    def z_start_last():
        def other(j, carry):
            z_half_copy(1 - zh, j).start()
            return carry

        lax.fori_loop(0, N_DIR, other, 0)
        each(N_DIR, functools.partial(z_half_copy, zh))
        z_own(LAST, 1).start()

    def y_half_copy(half, sem, k):
        xy2 = (xy + k) % N_XY
        return pltpu.make_async_remote_copy(
            src_ref=ybuf.at[LAST, xy2, half],
            dst_ref=ry.at[LAST, xy, half],
            send_sem=y_send.at[LAST],
            recv_sem=y_recv.at[sem],
            device_id=(d, zh * N_XY + xy2),
            device_id_type=MESH,
        )

    def theta_half(half, sem):
        wait_for(recv.at[LAST, half], z_recv.at[sem])
        x = recv[LAST, half].reshape(NT * N_XY, C)
        y = jnp.dot(mt[...], x, preferred_element_type=F32).astype(BF)
        ybuf[LAST, :, half] = y[: N_XY * NT_F].reshape(N_XY, NT_F, C)
        hbuf[LAST, half] = y[N_XY * NT_F :]
        each(N_XY, functools.partial(y_half_copy, half, sem))
        pltpu.make_async_copy(
            ybuf.at[LAST, xy, half], ry.at[LAST, xy, half], y_recv.at[sem]
        ).start()

    def z_start(pi):
        each(16, functools.partial(z_copy, pi))
        z_own(pi).start()

    for i in range(SMALL):
        pltpu.make_async_copy(small[i], held[i], small_sem.at[i]).start()
    pl.semaphore_wait(barrier, 15 + N_BOX - 1)
    z_start(0)
    for i in range(SMALL):
        pltpu.make_async_copy(small[i], held[i], small_sem.at[i]).wait()


    box = box_of_row[...]
    parent = box // 8
    octant = box - parent * 8
    dest = parent % N_BOX
    owner = lax.broadcasted_iota(jnp.int32, (N_BOX, ROW_DEV), 0)
    onehot = jnp.where(owner == dest, 1.0, 0.0).astype(F32)
    width = 256
    before = jnp.where(
        lax.broadcasted_iota(jnp.int32, (width, width), 0)
        < lax.broadcasted_iota(jnp.int32, (width, width), 1),
        1.0,
        0.0,
    ).astype(BF)
    carry = jnp.zeros((N_BOX, 1), F32)
    ranks = []
    for i in range(ROW_DEV // width):
        one = onehot[:, i * width : (i + 1) * width]
        pre = jnp.dot(one.astype(BF), before, preferred_element_type=F32) + carry
        ranks.append(jnp.sum(one * pre, axis=0, keepdims=True))
        carry = carry + jnp.sum(one, axis=1, keepdims=True)
    rank = jnp.concatenate(ranks, axis=1)
    is_hot = jnp.where(carry > float(SLOT), 1.0, 0.0)
    hot_row = jnp.sum(onehot * is_hot, axis=0, keepdims=True)
    number = lax.broadcasted_iota(jnp.int32, (N_BOX, 1), 0).astype(F32)
    hot = jnp.sum(number * is_hot, axis=0, keepdims=True)

    pos = jnp.where(
        hot_row > 0.5, float(N_BOX * SLOT) + rank, dest.astype(F32) * float(SLOT) + rank
    )
    sub = lax.broadcasted_iota(jnp.int32, (16, ROW_DEV), 0)
    o = off[...].astype(F32)
    g = jnp.where(sub == 3, octant.astype(F32), 0.0)
    for i in range(3):
        g = jnp.where(sub == i, o[i : i + 1, :], g)
    g = g.astype(BF)
    for i in range(ROW_DEV // width):
        geo[i, :16] = g[:, i * width : (i + 1) * width].astype(F32)
        geo[i, 16:] = jnp.broadcast_to(pos[:, i * width : (i + 1) * width], (8, width))
    gacc[...] = jnp.zeros_like(gacc)
    lane128 = lax.broadcasted_iota(jnp.int32, (128, 128), 1).astype(F32)

    def sort_block(i, carry):
        hits = one_hot(geo[i, 16:17], lane128)
        oh[pl.ds(pl.multiple_of(i * width, width), width), :] = hits
        gacc[...] += jnp.dot(geo[i, :16].astype(BF), hits, preferred_element_type=F32)
        return carry

    lax.fori_loop(0, ROW_DEV // width, sort_block, 0)
    for m in range(N_BOX // 2):
        go[m] = gacc[:4, m * 128 : (m + 1) * 128].astype(BF)
    for m in range(2):
        hotg[m] = gacc[:8, N_BOX * SLOT + m * 128 : N_BOX * SLOT + (m + 1) * 128]
    each(N_BOX, g_copy)
    g_own().start()
    z_start(1)


    a_theta = spread(tap_t[...], wt_t[...], NT_F)
    ah = jnp.dot(sign_t[...], a_theta, preferred_element_type=F32).astype(BF)
    col = lax.broadcasted_iota(jnp.int32, (NT, NT * N_XY), 1)
    row = lax.broadcasted_iota(jnp.int32, (NT, NT * N_XY), 0)
    wide = jnp.where(col // N_XY == row, 1.0, 0.0).astype(BF)
    v = jnp.dot(ah, wide, preferred_element_type=F32)
    lane_g = lax.broadcasted_iota(jnp.int32, v.shape, 1) % N_XY
    for i in range(N_XY):
        mt[i * NT_F : (i + 1) * NT_F, :] = jnp.where(lane_g == i, v, 0.0).astype(BF)
    local = hot - (zh * N_XY).astype(F32)
    mt[N_XY * NT_F :, :] = jnp.where(lane_g.astype(F32) == local, v, 0.0).astype(BF)

    a_phi = spread(tap_p[...], wt_p[...], NP_F)
    bh = jnp.dot(sign_p[...], a_phi, preferred_element_type=F32).astype(BF)
    col = lax.broadcasted_iota(jnp.int32, (NP, NP * 16), 1) // 16
    row = lax.broadcasted_iota(jnp.int32, (NP, NP * 16), 0)
    sample = col % 2 * (NP // 2) + col // 2 % N_XY * P_DEV + col // N_BOX
    wide = jnp.where(sample == row, 1.0, 0.0).astype(BF)
    v = jnp.dot(bh, wide, preferred_element_type=F32)
    same = (
        lax.broadcasted_iota(jnp.int32, (16, NP * 16), 1) % 16
        == lax.broadcasted_iota(jnp.int32, (16, NP * 16), 0)
    )
    for i in range(NP_F):
        mp[i * 16 : (i + 1) * 16, :] = jnp.where(same, v[i : i + 1, :], 0.0).astype(BF)


    lane = lax.broadcasted_iota(jnp.int32, (16, C), 1)
    low = lane < HALF

    def gather_geometry():
        wait_for(rg, g_recv)
        odd = b % 2 == 1

        def side(m):
            t = rg[m].astype(F32)
            return jnp.where(odd, pltpu.roll(t, HALF, 1), t)

        for m in range(N_BOX // 2):
            second = pltpu.roll(side(2 * m + 1), HALF, 1)
            gs[m // 2, :4, m % 2 * 128 : (m % 2 + 1) * 128] = jnp.where(low[:4], side(2 * m), second)
        for m in range(2):
            gs[N_BOX // 4, :, m * 128 : (m + 1) * 128] = hotg[m]

    def phases(i, carry):
        g = gs[i]
        octant = g[3:4]
        bz = jnp.where(octant >= 4.0, 1.0, 0.0)
        rest = octant - 4.0 * bz
        by = jnp.where(rest >= 2.0, 1.0, 0.0)
        bx = rest - 2.0 * by

        def turned(axis, bit):
            place = box_phase * ((2.0 * bit - 1.0) * 0.25 + g[axis : axis + 1] * 0.5)
            return place * (0.5 / math.pi)

        for table, u, factor in (
            (ex, turned(0, bx) * 0.5, sines),
            (ey, turned(1, by) * 0.5, cosines),
        ):
            k, s = turns(u * factor[...])
            table[0, 16:, :] = k
            table[1, 16:, :] = s
            table[0, :16, :] = k[16:]
            table[1, :16, :] = -s[16:]
        cc, sc = turns(turned(2, bz) * cosines[:16, :])
        for q in range(16):
            lo, hi = 16 - q, 16 + q
            c1, s1 = ex[0, hi : hi + 16, :], ex[1, hi : hi + 16, :]
            c2, s2 = ex[0, lo : lo + 16, :], ex[1, lo : lo + 16, :]
            ca, sa = c1 * c2 - s1 * s2, s1 * c2 + c1 * s2
            if q == 0:
                lo, hi = 0, 32
            c1, s1 = ey[0, hi : hi + 16, :], ey[1, hi : hi + 16, :]
            c2, s2 = ey[0, lo : lo + 16, :], ey[1, lo : lo + 16, :]
            cb, sb = c1 * c2 + s1 * s2, s2 * c1 - c2 * s1
            if q == 0:
                four = (ca, sb, sa, cb)
            else:
                four = (ca * cb, ca * sb, sa * cb, sa * sb)
            for j, v in enumerate(four):
                at = q * 128 + j * 32
                w[i, at : at + 16, :] = (v * cc).astype(BF)
                w[i, at + 16 : at + 32, :] = (v * sc).astype(BF)
        return carry


    def theta_step(pi):
        wait_for(recv.at[pi], z_recv.at[pi])
        x = jnp.concatenate(
            [recv[pi, 0].reshape(NT * N_XY, C), recv[pi, 1].reshape(NT * N_XY, C)], axis=1
        )
        y = jnp.dot(mt[...], x, preferred_element_type=F32).astype(BF)
        for z in range(2):
            part = y[:, z * C : (z + 1) * C]
            ybuf[pi, :, z] = part[: N_XY * NT_F].reshape(N_XY, NT_F, C)
            hbuf[pi, z] = part[N_XY * NT_F :]
        each(N_XY, functools.partial(y_copy, pi))
        y_own(pi).start()
        if pi < 2:
            t_copy(pi).start()

    def hot_step(pi):
        t_copy(pi).wait_recv()
        hsum[pi] = hbuf[pi] + twin[pi]
        each(N_XY, functools.partial(h_copy, pi))
        h_own(pi).start()

    def phi_step(pi, part, sem, acc):
        bytes_of = part.at[pi, : N_XY // 2] if part is ry and pi == LAST else part.at[pi]
        wait_for(bytes_of, sem.at[pi])
        x = jnp.concatenate(
            [part[pi, :, :, c * 16 : (c + 1) * 16, :].reshape(512, C) for c in range(2)], axis=1
        )
        y = jnp.dot(mp[:, pi * 512 : (pi + 1) * 512], x, preferred_element_type=F32)
        if pi:
            acc[...] += y
        else:
            acc[...] = y

    def directions(acc):
        scale = quad[...]
        for q in range(16):
            parts = []
            for ab in range(4):
                for c in range(2):
                    at = q * 64 + ab * 16
                    v = acc[at : at + 16, c * C : (c + 1) * C] * scale
                    turn = (ab // 2 + ab % 2 + c) if (q or ab < 3) else c
                    if turn % 2:
                        v = pltpu.roll(v, HALF, 1)
                        v = jnp.where(low, -v, v) if turn == 1 else jnp.where(low, v, -v)
                    elif turn == 2:
                        v = -v
                    parts.append(v)
            gt[:, q * 128 : (q + 1) * 128] = jnp.concatenate(parts, axis=0).T.astype(BF)

    def field_block(i):
        return jnp.dot(gt[...], w[i], preferred_element_type=F32).T.astype(BF)

    def send_block(i, carry):
        at = (1 - zh + i // 4) % 2 * 4 + (b // 4 + i) % 4
        f[pl.ds(pl.multiple_of(at * 256, 256), 256), :] = field_block(at)
        for j in range(4):
            b2 = at * 4 + j

            @pl.when(b2 != b)
            def _():
                r_copy(b2).start()

            @pl.when(b2 == b)
            def _():
                r_own().start()

        return carry

    own_args = (ry, y_recv, acc_own)
    hot_args = (rh, h_recv, acc_hot)
    theta_step(0)
    z_start(2)
    gather_geometry()
    lax.fori_loop(0, 4, phases, 0)
    theta_step(1)
    z_start_last()
    hot_step(0)
    phi_step(0, *own_args)
    lax.fori_loop(4, 9, phases, 0)
    theta_step(2)
    hot_step(1)
    phi_step(1, *own_args)
    phi_step(0, *hot_args)
    theta_half(1 - zh, LAST)
    phi_step(2, *own_args)
    theta_half(zh, LAST + 1)
    t_copy(2).start()
    t_copy(3).start()
    phi_step(1, *hot_args)
    wait_for(ry.at[LAST, : N_XY // 2], y_recv.at[LAST + 1])
    phi_step(3, *own_args)
    hot_step(2)
    hot_step(3)
    directions(acc_own)
    lax.fori_loop(0, N_BOX // 4, send_block, 0)
    phi_step(2, *hot_args)
    for pi in range(P_DEV):
        wait_for(f.at[: 15 * 128], z_send.at[pi])
        wait_for(f.at[: 15 * SLOT], y_send.at[pi])
    wait_for(rg.at[: N_BOX - 1], g_send)
    phi_step(3, *hot_args)
    directions(acc_hot)
    f[N_BOX * SLOT :, :] = field_block(N_BOX // 4)

    half = N_BOX * SLOT // 2
    here = pl.multiple_of(zh * half, half)
    there = pl.multiple_of(half - zh * half, half)
    wait_for(r.at[pl.ds(here, half), :], r_recv.at[0])

    def place_here(i, carry):
        at = pl.multiple_of(i * 1024, 1024)
        v = jnp.dot(
            oh[pl.ds(at, 1024), pl.ds(here, half)],
            r[pl.ds(here, half), :],
            preferred_element_type=F32,
        )
        total[pl.ds(at, 1024), :] = v + jnp.dot(
            oh[pl.ds(at, 1024), N_BOX * SLOT :],
            f[N_BOX * SLOT :, :],
            preferred_element_type=F32,
        )
        return carry

    lax.fori_loop(0, ROW_DEV // 1024, place_here, 0)
    for pi in range(P_DEV):
        t_copy(pi).wait_send()
        wait_for(f.at[: 15 * SLOT], h_send.at[pi])
    wait_for(f.at[: 31 * SLOT], r_send)
    for piece in range(4):
        source = (b // 4 + 4 - piece) % 4
        lanes = pl.ds(pl.multiple_of(there + source * 256, 256), 256)
        wait_for(r.at[lanes, :], r_recv.at[1 + piece])
        for i in range(2):
            at = pl.ds(i * 1024, 1024)
            v = total[at, :] + jnp.dot(oh[at, lanes], r[lanes, :], preferred_element_type=F32)
            if piece < 3:
                total[at, :] = v
            else:
                field_v[at, :] = v.astype(BF)
                pltpu.make_async_copy(field_v.at[at, :], field.at[at, :], field_sem.at[i]).start()
    for i in range(2):
        at = pl.ds(i * 1024, 1024)
        pltpu.make_async_copy(field_v.at[at, :], field.at[at, :], field_sem.at[i]).wait()


def step(pattern, tap_theta, tap_phi, weight_theta, weight_phi, row_box, row_offset):
    n = np.arange(NT_F) + 0.5
    wide = lambda v: jnp.asarray(np.repeat(v[:, None], 256, axis=1), F32)
    sines = wide(np.sin(np.pi * n / NT_F))
    cosines = wide(np.cos(np.pi * n / NT_F))
    quad = wide(np.sin(np.pi * n[:16] / NT_F) * math.sqrt(2.0 / (NT_F * NP_F)))[:, :C]
    small = (
        tap_theta.T, tap_phi.T, weight_theta.T, weight_phi.T,
        jnp.asarray(theta_signs(), BF), jnp.asarray(phi_signs(), BF),
        row_box.reshape(1, ROW_DEV), row_offset, sines, cosines, quad,
    )
    anywhere = pl.BlockSpec(memory_space=pl.ANY)
    dma = pltpu.SemaphoreType.DMA
    theta = (P_DEV, N_XY, 2, NT_F, C)
    hot = (P_DEV, 2, NT_F, C)
    blocks = SLOTS // 256
    return pl.pallas_call(
        step_kernel,
        out_shape=jax.ShapeDtypeStruct((ROW_DEV, C), BF),
        in_specs=[anywhere] * (1 + SMALL),
        out_specs=anywhere,
        scratch_shapes=[
            pltpu.VMEM((P_DEV, 2, N_DIR, T_DEV, N_XY, C), BF),
            pltpu.VMEM(theta, BF),
            pltpu.VMEM(hot, BF),
            pltpu.VMEM(hot, BF),
            pltpu.VMEM(hot, BF),
            pltpu.VMEM(theta, BF),
            pltpu.VMEM(theta, BF),
            pltpu.VMEM((N_BOX // 2, 4, 128), BF),
            pltpu.VMEM((2, 8, 128), F32),
            pltpu.VMEM((N_BOX, 4, 128), BF),
            pltpu.VMEM((N_XY * NT_F + NT_F, NT * N_XY), BF),
            pltpu.VMEM((NP_F * 16, NP * 16), BF),
            pltpu.VMEM((ROW_DEV // 256, 24, 256), F32),
            pltpu.VMEM((16, SLOTS), F32),
            pltpu.VMEM((ROW_DEV, SLOTS), BF),
            pltpu.VMEM((blocks, 8, 256), F32),
            pltpu.VMEM((2, 48, 256), F32),
            pltpu.VMEM((2, 48, 256), F32),
            pltpu.VMEM((blocks, NT_F * NP_F, 256), BF),
            pltpu.VMEM((NP_F * 16, 2 * C), F32),
            pltpu.VMEM((NP_F * 16, 2 * C), F32),
            pltpu.VMEM((C, NT_F * NP_F), BF),
            pltpu.VMEM((SLOTS, C), BF),
            pltpu.VMEM((N_BOX * SLOT, C), BF),
            pltpu.VMEM((ROW_DEV, C), F32),
            pltpu.VMEM((ROW_DEV, C), BF),
            dma((P_DEV,)),
            dma((P_DEV + 1,)),
            dma,
            dma,
            dma((P_DEV,)),
            dma((P_DEV + 1,)),
            dma((P_DEV,)),
            dma((P_DEV,)),
            dma((P_DEV,)),
            dma((P_DEV,)),
            dma,
            dma((5,)),
            dma((2,)),
            dma((SMALL,)),
        ]
        + [pltpu.VMEM(v.shape, v.dtype) for v in small],
        compiler_params=pltpu.CompilerParams(
            collective_id=0, has_side_effects=True, vmem_limit_bytes=60 << 20
        ),
        name="step",
    )(pattern, *small)


def finish_kernel(field, fwd, out, grad):
    v = field[...]
    out[...] = v
    product = fwd[...].astype(F32) * v.astype(F32)
    grad[...] = (jnp.sum(product.T, axis=0, keepdims=True) * (0.5 / math.sqrt(C))).reshape(grad.shape)


def finish(field, fwd):
    rows = 1024
    block = pl.BlockSpec((rows, C), lambda i: (i, 0))
    return pl.pallas_call(
        finish_kernel,
        out_shape=(
            jax.ShapeDtypeStruct((ROW_DEV, C), BF),
            jax.ShapeDtypeStruct((ROW_DEV,), F32),
        ),
        grid=(ROW_DEV // rows,),
        in_specs=[block, block],
        out_specs=(block, pl.BlockSpec((rows,), lambda i: (i,))),
        name="finish",
    )(field, fwd)


def per_device(*arrays):
    field = step(*arrays[:-1])
    return finish(field, arrays[-1])


def solution(mesh):
    in_specs = (
        P("dir", "box", None, None),
        P(),
        P(),
        P(),
        P(),
        P(("dir", "box")),
        P(None, ("dir", "box")),
        P(("dir", "box"), None),
    )
    out_specs = (P(("dir", "box"), None), P(("dir", "box")))
    return jax.shard_map(
        per_device, mesh=mesh, in_specs=in_specs, out_specs=out_specs, check_vma=False
    )
```

```python
import functools
import math

import jax
import jax.numpy as jnp
import numpy as np
from jax import lax
from jax.experimental import pallas as pl
from jax.experimental.pallas import tpu as pltpu
from jax.sharding import PartitionSpec as P

NT = 64
NP = 128
NT_F = 32
NP_F = 64
C = 128
HALF = 64
N_DIR = 8
N_BOX = 32
N_XY = 16
ROW_DEV = 2048
SLOT = 64
HOT = 256
SLOTS = N_BOX * SLOT + HOT
P_DEV = NP // N_BOX
T_DEV = NT // N_DIR
LAST = P_DEV - 1
SMALL = 11

box_phase = 50.265482

MESH = pl.DeviceIdType.MESH
BF = jnp.bfloat16
F32 = jnp.float32


def polynomials():
    z2 = 0.5 + 0.5 * np.cos(np.pi * (np.arange(400) + 0.5) / 400)
    z = np.sqrt(z2)
    s = np.polynomial.chebyshev.Chebyshev.fit(z2, np.sin(np.pi * z) / z, 7, domain=[0, 1])
    k = np.polynomial.chebyshev.Chebyshev.fit(z2, np.cos(np.pi * z), 8, domain=[0, 1])
    to = np.polynomial.polynomial.Polynomial
    return tuple(
        [float(v) for v in f.convert(kind=to, domain=[-1, 1], window=[-1, 1]).coef] for f in (s, k)
    )


SIN_POLY, COS_POLY = polynomials()


def turns(u):
    z = (u - jnp.round(u)) * 2.0
    w = z * z
    s = jnp.full_like(w, SIN_POLY[-1])
    for v in SIN_POLY[-2::-1]:
        s = s * w + v
    k = jnp.full_like(w, COS_POLY[-1])
    for v in COS_POLY[-2::-1]:
        k = k * w + v
    return k, s * z


def theta_signs():
    h = np.zeros((NT_F, NT_F), np.float32)
    for t in range(16):
        for c in range(2):
            h[c * 16 + t, t] = 1.0
            h[c * 16 + t, 31 - t] = (-1.0) ** c
    return h


def phi_signs():
    h = np.zeros((NP_F, NP_F), np.float32)
    for q in range(1, 16):
        for a in range(2):
            for b in range(2):
                r = q * 4 + a * 2 + b
                h[r, q] = 1.0
                h[r, 32 - q] = (-1.0) ** a
                h[r, 64 - q] = (-1.0) ** b
                h[r, 32 + q] = (-1.0) ** (a + b)
    for a in range(2):
        h[a * 2, 0] = 1.0
        h[a * 2, 32] = (-1.0) ** a
    h[1, 16], h[1, 48] = 1.0, -1.0
    h[3, 16], h[3, 48] = 1.0, 1.0
    return h


def one_hot(p, lane):
    parts = []
    for h in range(2):
        column = jnp.broadcast_to(p[:, h * 128 : (h + 1) * 128], (128, 128)).T
        parts.append(
            jnp.concatenate(
                [
                    jnp.where(column == lane + float(j * 128), 1.0, 0.0).astype(BF)
                    for j in range(SLOTS // 128)
                ],
                axis=1,
            )
        )
    return jnp.concatenate(parts, axis=0)


def spread(taps, weights, count):
    sample = lax.broadcasted_iota(jnp.int32, (count, taps.shape[1]), 0)
    total = jnp.zeros(sample.shape, F32)
    for j in range(taps.shape[0]):
        total = total + jnp.where(
            sample == taps[j : j + 1, :], weights[j : j + 1, :].astype(F32), 0.0
        )
    return total.astype(BF)


def step_kernel(pat, *refs):
    small, refs = refs[:SMALL], refs[SMALL:]
    (
        field, recv, ybuf, hbuf, twin, hsum, ry, rh, go, hotg, rg, mt, mp, geo, gacc, oh, gs, ex, ey, w,
        acc_own, acc_hot, gt, f, r, total, field_v,
        z_send, z_recv, g_send, g_recv, y_send, y_recv, t_send, t_recv, h_send, h_recv,
        r_send, r_recv, field_sem, small_sem,
    ) = refs[: len(refs) - SMALL]
    held = refs[len(refs) - SMALL :]
    tap_t, tap_p, wt_t, wt_p, sign_t, sign_p, box_of_row, off, sines, cosines, quad = held
    d = lax.axis_index("dir")
    b = lax.axis_index("box")
    zh = b // N_XY
    xy = b % N_XY
    e = zh * N_DIR + d

    barrier = pltpu.get_barrier_semaphore()

    def greet_z(k, carry):
        e2 = (e + k) % 16
        pl.semaphore_signal(
            barrier, inc=1, device_id=(e2 % N_DIR, e2 // N_DIR * N_XY + xy), device_id_type=MESH
        )
        return carry

    def greet_box(k, carry):
        pl.semaphore_signal(barrier, inc=1, device_id=(d, (b + k) % N_BOX), device_id_type=MESH)
        return carry

    lax.fori_loop(1, 16, greet_z, 0)
    lax.fori_loop(1, N_BOX, greet_box, 0)


    def z_copy(pi, k):
        e2 = (e + k) % 16
        d2, zh2 = e2 % N_DIR, e2 // N_DIR
        first = pl.multiple_of(d2 * N_BOX + zh2 * N_XY, N_XY)
        return pltpu.make_async_remote_copy(
            src_ref=pat.at[:, pi, pl.ds(first, N_XY), :],
            dst_ref=recv.at[pi, zh, d],
            send_sem=z_send.at[pi],
            recv_sem=z_recv.at[pi],
            device_id=(d2, zh2 * N_XY + xy),
            device_id_type=MESH,
        )

    def z_own(pi, half=0):
        first = pl.multiple_of(d * N_BOX + zh * N_XY, N_XY)
        return pltpu.make_async_copy(
            pat.at[:, pi, pl.ds(first, N_XY), :], recv.at[pi, zh, d], z_recv.at[pi + half]
        )

    def g_copy(k):
        b2 = (b + k) % N_BOX
        return pltpu.make_async_remote_copy(
            src_ref=go.at[b2 // 2],
            dst_ref=rg.at[b],
            send_sem=g_send,
            recv_sem=g_recv,
            device_id=(d, b2),
            device_id_type=MESH,
        )

    def y_copy(pi, k):
        xy2 = (xy + k) % N_XY
        return pltpu.make_async_remote_copy(
            src_ref=ybuf.at[pi, xy2],
            dst_ref=ry.at[pi, xy],
            send_sem=y_send.at[pi],
            recv_sem=y_recv.at[pi],
            device_id=(d, zh * N_XY + xy2),
            device_id_type=MESH,
        )

    def h_copy(pi, k):
        xy2 = (xy + k) % N_XY
        return pltpu.make_async_remote_copy(
            src_ref=hsum.at[pi],
            dst_ref=rh.at[pi, xy],
            send_sem=h_send.at[pi],
            recv_sem=h_recv.at[pi],
            device_id=(d, zh * N_XY + xy2),
            device_id_type=MESH,
        )

    def t_copy(pi):
        return pltpu.make_async_remote_copy(
            src_ref=hbuf.at[pi],
            dst_ref=twin.at[pi],
            send_sem=t_send.at[pi],
            recv_sem=t_recv.at[pi],
            device_id=(d, (b + N_XY) % N_BOX),
            device_id_type=MESH,
        )

    def y_own(pi):
        return pltpu.make_async_copy(ybuf.at[pi, xy], ry.at[pi, xy], y_recv.at[pi])

    def h_own(pi):
        return pltpu.make_async_copy(hsum.at[pi], rh.at[pi, xy], h_recv.at[pi])

    def g_own():
        return pltpu.make_async_copy(go.at[b // 2], rg.at[b], g_recv)

    def r_copy(b2):
        return pltpu.make_async_remote_copy(
            src_ref=f.at[pl.ds(pl.multiple_of(b2 * SLOT, SLOT), SLOT), :],
            dst_ref=r.at[pl.ds(pl.multiple_of(b * SLOT, SLOT), SLOT), :],
            send_sem=r_send,
            recv_sem=r_recv.at[(zh + b2 // N_XY) % 2 * (1 + (b2 // 4 + 8 - b // 4) % 4 // 2)],
            device_id=(d, b2),
            device_id_type=MESH,
        )

    def r_own():
        at = pl.ds(pl.multiple_of(b * SLOT, SLOT), SLOT)
        return pltpu.make_async_copy(f.at[at, :], r.at[at, :], r_recv.at[0])

    def each(n, copy):
        def one(k, carry):
            copy(k).start()
            return carry

        lax.fori_loop(1, n, one, 0)

    def wait_for(ref, sem):
        pltpu.make_async_copy(ref, ref, sem).wait()

    def z_half_copy(zh2, j):
        d2 = (d + j) % N_DIR
        first = pl.multiple_of(d2 * N_BOX + zh2 * N_XY, N_XY)
        return pltpu.make_async_remote_copy(
            src_ref=pat.at[:, LAST, pl.ds(first, N_XY), :],
            dst_ref=recv.at[LAST, zh, d],
            send_sem=z_send.at[LAST],
            recv_sem=z_recv.at[LAST + (zh + zh2 + 1) % 2],
            device_id=(d2, zh2 * N_XY + xy),
            device_id_type=MESH,
        )

    def z_start_last():
        def other(j, carry):
            z_half_copy(1 - zh, j).start()
            return carry

        lax.fori_loop(0, N_DIR, other, 0)
        each(N_DIR, functools.partial(z_half_copy, zh))
        z_own(LAST, 1).start()

    def y_half_copy(half, sem, k):
        xy2 = (xy + k) % N_XY
        return pltpu.make_async_remote_copy(
            src_ref=ybuf.at[LAST, xy2, half],
            dst_ref=ry.at[LAST, xy, half],
            send_sem=y_send.at[LAST],
            recv_sem=y_recv.at[sem],
            device_id=(d, zh * N_XY + xy2),
            device_id_type=MESH,
        )

    def theta_half(half, sem):
        wait_for(recv.at[LAST, half], z_recv.at[sem])
        x = recv[LAST, half].reshape(NT * N_XY, C)
        y = jnp.dot(mt[...], x, preferred_element_type=F32).astype(BF)
        ybuf[LAST, :, half] = y[: N_XY * NT_F].reshape(N_XY, NT_F, C)
        hbuf[LAST, half] = y[N_XY * NT_F :]
        each(N_XY, functools.partial(y_half_copy, half, sem))
        pltpu.make_async_copy(
            ybuf.at[LAST, xy, half], ry.at[LAST, xy, half], y_recv.at[sem]
        ).start()

    def z_start(pi):
        each(16, functools.partial(z_copy, pi))
        z_own(pi).start()

    for i in range(SMALL):
        pltpu.make_async_copy(small[i], held[i], small_sem.at[i]).start()
    pl.semaphore_wait(barrier, 15 + N_BOX - 1)
    z_start(0)
    for i in range(SMALL):
        pltpu.make_async_copy(small[i], held[i], small_sem.at[i]).wait()


    box = box_of_row[...]
    parent = box // 8
    octant = box - parent * 8
    dest = parent % N_BOX
    owner = lax.broadcasted_iota(jnp.int32, (N_BOX, ROW_DEV), 0)
    onehot = jnp.where(owner == dest, 1.0, 0.0).astype(F32)
    width = 256
    before = jnp.where(
        lax.broadcasted_iota(jnp.int32, (width, width), 0)
        < lax.broadcasted_iota(jnp.int32, (width, width), 1),
        1.0,
        0.0,
    ).astype(BF)
    carry = jnp.zeros((N_BOX, 1), F32)
    ranks = []
    for i in range(ROW_DEV // width):
        one = onehot[:, i * width : (i + 1) * width]
        pre = jnp.dot(one.astype(BF), before, preferred_element_type=F32) + carry
        ranks.append(jnp.sum(one * pre, axis=0, keepdims=True))
        carry = carry + jnp.sum(one, axis=1, keepdims=True)
    rank = jnp.concatenate(ranks, axis=1)
    is_hot = jnp.where(carry > float(SLOT), 1.0, 0.0)
    hot_row = jnp.sum(onehot * is_hot, axis=0, keepdims=True)
    number = lax.broadcasted_iota(jnp.int32, (N_BOX, 1), 0).astype(F32)
    hot = jnp.sum(number * is_hot, axis=0, keepdims=True)

    pos = jnp.where(
        hot_row > 0.5, float(N_BOX * SLOT) + rank, dest.astype(F32) * float(SLOT) + rank
    )
    sub = lax.broadcasted_iota(jnp.int32, (16, ROW_DEV), 0)
    o = off[...].astype(F32)
    g = jnp.where(sub == 3, octant.astype(F32), 0.0)
    for i in range(3):
        g = jnp.where(sub == i, o[i : i + 1, :], g)
    g = g.astype(BF)
    for i in range(ROW_DEV // width):
        geo[i, :16] = g[:, i * width : (i + 1) * width].astype(F32)
        geo[i, 16:] = jnp.broadcast_to(pos[:, i * width : (i + 1) * width], (8, width))
    gacc[...] = jnp.zeros_like(gacc)
    lane128 = lax.broadcasted_iota(jnp.int32, (128, 128), 1).astype(F32)

    def sort_block(i, carry):
        hits = one_hot(geo[i, 16:17], lane128)
        oh[pl.ds(pl.multiple_of(i * width, width), width), :] = hits
        gacc[...] += jnp.dot(geo[i, :16].astype(BF), hits, preferred_element_type=F32)
        return carry

    lax.fori_loop(0, ROW_DEV // width, sort_block, 0)
    for m in range(N_BOX // 2):
        go[m] = gacc[:4, m * 128 : (m + 1) * 128].astype(BF)
    for m in range(2):
        hotg[m] = gacc[:8, N_BOX * SLOT + m * 128 : N_BOX * SLOT + (m + 1) * 128]
    each(N_BOX, g_copy)
    g_own().start()
    z_start(1)


    a_theta = spread(tap_t[...], wt_t[...], NT_F)
    ah = jnp.dot(sign_t[...], a_theta, preferred_element_type=F32).astype(BF)
    col = lax.broadcasted_iota(jnp.int32, (NT, NT * N_XY), 1)
    row = lax.broadcasted_iota(jnp.int32, (NT, NT * N_XY), 0)
    wide = jnp.where(col // N_XY == row, 1.0, 0.0).astype(BF)
    v = jnp.dot(ah, wide, preferred_element_type=F32)
    lane_g = lax.broadcasted_iota(jnp.int32, v.shape, 1) % N_XY
    for i in range(N_XY):
        mt[i * NT_F : (i + 1) * NT_F, :] = jnp.where(lane_g == i, v, 0.0).astype(BF)
    local = hot - (zh * N_XY).astype(F32)
    mt[N_XY * NT_F :, :] = jnp.where(lane_g.astype(F32) == local, v, 0.0).astype(BF)

    a_phi = spread(tap_p[...], wt_p[...], NP_F)
    bh = jnp.dot(sign_p[...], a_phi, preferred_element_type=F32).astype(BF)
    col = lax.broadcasted_iota(jnp.int32, (NP, NP * 16), 1) // 16
    row = lax.broadcasted_iota(jnp.int32, (NP, NP * 16), 0)
    sample = col % 2 * (NP // 2) + col // 2 % N_XY * P_DEV + col // N_BOX
    wide = jnp.where(sample == row, 1.0, 0.0).astype(BF)
    v = jnp.dot(bh, wide, preferred_element_type=F32)
    same = (
        lax.broadcasted_iota(jnp.int32, (16, NP * 16), 1) % 16
        == lax.broadcasted_iota(jnp.int32, (16, NP * 16), 0)
    )
    for i in range(NP_F):
        mp[i * 16 : (i + 1) * 16, :] = jnp.where(same, v[i : i + 1, :], 0.0).astype(BF)


    lane = lax.broadcasted_iota(jnp.int32, (16, C), 1)
    low = lane < HALF

    def gather_geometry():
        wait_for(rg, g_recv)
        odd = b % 2 == 1

        def side(m):
            t = rg[m].astype(F32)
            return jnp.where(odd, pltpu.roll(t, HALF, 1), t)

        for m in range(N_BOX // 2):
            second = pltpu.roll(side(2 * m + 1), HALF, 1)
            gs[m // 2, :4, m % 2 * 128 : (m % 2 + 1) * 128] = jnp.where(low[:4], side(2 * m), second)
        for m in range(2):
            gs[N_BOX // 4, :, m * 128 : (m + 1) * 128] = hotg[m]

    def phases(i, carry):
        g = gs[i]
        octant = g[3:4]
        bz = jnp.where(octant >= 4.0, 1.0, 0.0)
        rest = octant - 4.0 * bz
        by = jnp.where(rest >= 2.0, 1.0, 0.0)
        bx = rest - 2.0 * by

        def turned(axis, bit):
            place = box_phase * ((2.0 * bit - 1.0) * 0.25 + g[axis : axis + 1] * 0.5)
            return place * (0.5 / math.pi)

        for table, u, factor in (
            (ex, turned(0, bx) * 0.5, sines),
            (ey, turned(1, by) * 0.5, cosines),
        ):
            k, s = turns(u * factor[...])
            table[0, 16:, :] = k
            table[1, 16:, :] = s
            table[0, :16, :] = k[16:]
            table[1, :16, :] = -s[16:]
        cc, sc = turns(turned(2, bz) * cosines[:16, :])
        for q in range(16):
            lo, hi = 16 - q, 16 + q
            c1, s1 = ex[0, hi : hi + 16, :], ex[1, hi : hi + 16, :]
            c2, s2 = ex[0, lo : lo + 16, :], ex[1, lo : lo + 16, :]
            ca, sa = c1 * c2 - s1 * s2, s1 * c2 + c1 * s2
            if q == 0:
                lo, hi = 0, 32
            c1, s1 = ey[0, hi : hi + 16, :], ey[1, hi : hi + 16, :]
            c2, s2 = ey[0, lo : lo + 16, :], ey[1, lo : lo + 16, :]
            cb, sb = c1 * c2 + s1 * s2, s2 * c1 - c2 * s1
            if q == 0:
                four = (ca, sb, sa, cb)
            else:
                four = (ca * cb, ca * sb, sa * cb, sa * sb)
            for j, v in enumerate(four):
                at = q * 128 + j * 32
                w[i, at : at + 16, :] = (v * cc).astype(BF)
                w[i, at + 16 : at + 32, :] = (v * sc).astype(BF)
        return carry


    def theta_step(pi):
        wait_for(recv.at[pi], z_recv.at[pi])
        x = jnp.concatenate(
            [recv[pi, 0].reshape(NT * N_XY, C), recv[pi, 1].reshape(NT * N_XY, C)], axis=1
        )
        y = jnp.dot(mt[...], x, preferred_element_type=F32).astype(BF)
        for z in range(2):
            part = y[:, z * C : (z + 1) * C]
            ybuf[pi, :, z] = part[: N_XY * NT_F].reshape(N_XY, NT_F, C)
            hbuf[pi, z] = part[N_XY * NT_F :]
        each(N_XY, functools.partial(y_copy, pi))
        y_own(pi).start()
        if pi < 2:
            t_copy(pi).start()

    def hot_step(pi):
        t_copy(pi).wait_recv()
        hsum[pi] = hbuf[pi] + twin[pi]
        each(N_XY, functools.partial(h_copy, pi))
        h_own(pi).start()

    def phi_step(pi, part, sem, acc):
        bytes_of = part.at[pi, : N_XY // 2] if part is ry and pi == LAST else part.at[pi]
        wait_for(bytes_of, sem.at[pi])
        x = jnp.concatenate(
            [part[pi, :, :, c * 16 : (c + 1) * 16, :].reshape(512, C) for c in range(2)], axis=1
        )
        y = jnp.dot(mp[:, pi * 512 : (pi + 1) * 512], x, preferred_element_type=F32)
        if pi:
            acc[...] += y
        else:
            acc[...] = y

    def directions(acc):
        scale = quad[...]
        for q in range(16):
            parts = []
            for ab in range(4):
                for c in range(2):
                    at = q * 64 + ab * 16
                    v = acc[at : at + 16, c * C : (c + 1) * C] * scale
                    turn = (ab // 2 + ab % 2 + c) if (q or ab < 3) else c
                    if turn % 2:
                        v = pltpu.roll(v, HALF, 1)
                        v = jnp.where(low, -v, v) if turn == 1 else jnp.where(low, v, -v)
                    elif turn == 2:
                        v = -v
                    parts.append(v)
            gt[:, q * 128 : (q + 1) * 128] = jnp.concatenate(parts, axis=0).T.astype(BF)

    def field_block(i):
        return jnp.dot(gt[...], w[i], preferred_element_type=F32).T.astype(BF)

    def send_block(i, carry):
        at = (1 - zh + i // 4) % 2 * 4 + (b // 4 + i) % 4
        f[pl.ds(pl.multiple_of(at * 256, 256), 256), :] = field_block(at)
        for j in range(4):
            b2 = at * 4 + j

            @pl.when(b2 != b)
            def _():
                r_copy(b2).start()

            @pl.when(b2 == b)
            def _():
                r_own().start()

        return carry

    own_args = (ry, y_recv, acc_own)
    hot_args = (rh, h_recv, acc_hot)
    theta_step(0)
    z_start(2)
    gather_geometry()
    lax.fori_loop(0, 4, phases, 0)
    theta_step(1)
    z_start_last()
    hot_step(0)
    phi_step(0, *own_args)
    lax.fori_loop(4, 9, phases, 0)
    theta_step(2)
    hot_step(1)
    phi_step(1, *own_args)
    phi_step(0, *hot_args)
    theta_half(1 - zh, LAST)
    phi_step(2, *own_args)
    theta_half(zh, LAST + 1)
    t_copy(2).start()
    t_copy(3).start()
    phi_step(1, *hot_args)
    hot_step(2)
    wait_for(ry.at[LAST, : N_XY // 2], y_recv.at[LAST + 1])
    phi_step(3, *own_args)
    hot_step(3)
    directions(acc_own)
    lax.fori_loop(0, N_BOX // 4, send_block, 0)
    phi_step(2, *hot_args)
    for pi in range(P_DEV):
        wait_for(f.at[: 15 * 128], z_send.at[pi])
        wait_for(f.at[: 15 * SLOT], y_send.at[pi])
    wait_for(rg.at[: N_BOX - 1], g_send)
    phi_step(3, *hot_args)
    directions(acc_hot)
    f[N_BOX * SLOT :, :] = field_block(N_BOX // 4)

    half = N_BOX * SLOT // 2
    here = pl.multiple_of(zh * half, half)
    there = pl.multiple_of(half - zh * half, half)
    wait_for(r.at[pl.ds(here, half), :], r_recv.at[0])

    def place_here(i, carry):
        at = pl.multiple_of(i * 1024, 1024)
        v = jnp.dot(
            oh[pl.ds(at, 1024), pl.ds(here, half)],
            r[pl.ds(here, half), :],
            preferred_element_type=F32,
        )
        total[pl.ds(at, 1024), :] = v + jnp.dot(
            oh[pl.ds(at, 1024), N_BOX * SLOT :],
            f[N_BOX * SLOT :, :],
            preferred_element_type=F32,
        )
        return carry

    lax.fori_loop(0, ROW_DEV // 1024, place_here, 0)
    for pi in range(P_DEV):
        t_copy(pi).wait_send()
        wait_for(f.at[: 15 * SLOT], h_send.at[pi])
    wait_for(f.at[: 31 * SLOT], r_send)
    for piece in range(2):
        lanes = []
        for k in range(2):
            source = (b // 4 + 4 - 2 * piece - k) % 4
            lanes.append(pl.ds(pl.multiple_of(there + source * 256, 256), 256))
        wait_for(f.at[:512, :], r_recv.at[1 + piece])
        part = jnp.concatenate([r[k, :] for k in lanes], axis=0)
        for i in range(4):
            at = pl.ds(i * 512, 512)
            hits = jnp.concatenate([oh[at, k] for k in lanes], axis=1)
            v = total[at, :] + jnp.dot(hits, part, preferred_element_type=F32)
            if piece == 0:
                total[at, :] = v
            else:
                field_v[at, :] = v.astype(BF)
                pltpu.make_async_copy(field_v.at[at, :], field.at[at, :], field_sem.at[i]).start()
    for i in range(4):
        at = pl.ds(i * 512, 512)
        pltpu.make_async_copy(field_v.at[at, :], field.at[at, :], field_sem.at[i]).wait()


def step(pattern, tap_theta, tap_phi, weight_theta, weight_phi, row_box, row_offset):
    n = np.arange(NT_F) + 0.5
    wide = lambda v: jnp.asarray(np.repeat(v[:, None], 256, axis=1), F32)
    sines = wide(np.sin(np.pi * n / NT_F))
    cosines = wide(np.cos(np.pi * n / NT_F))
    quad = wide(np.sin(np.pi * n[:16] / NT_F) * math.sqrt(2.0 / (NT_F * NP_F)))[:, :C]
    small = (
        tap_theta.T, tap_phi.T, weight_theta.T, weight_phi.T,
        jnp.asarray(theta_signs(), BF), jnp.asarray(phi_signs(), BF),
        row_box.reshape(1, ROW_DEV), row_offset, sines, cosines, quad,
    )
    anywhere = pl.BlockSpec(memory_space=pl.ANY)
    dma = pltpu.SemaphoreType.DMA
    theta = (P_DEV, N_XY, 2, NT_F, C)
    hot = (P_DEV, 2, NT_F, C)
    blocks = SLOTS // 256
    return pl.pallas_call(
        step_kernel,
        out_shape=jax.ShapeDtypeStruct((ROW_DEV, C), BF),
        in_specs=[anywhere] * (1 + SMALL),
        out_specs=anywhere,
        scratch_shapes=[
            pltpu.VMEM((P_DEV, 2, N_DIR, T_DEV, N_XY, C), BF),
            pltpu.VMEM(theta, BF),
            pltpu.VMEM(hot, BF),
            pltpu.VMEM(hot, BF),
            pltpu.VMEM(hot, BF),
            pltpu.VMEM(theta, BF),
            pltpu.VMEM(theta, BF),
            pltpu.VMEM((N_BOX // 2, 4, 128), BF),
            pltpu.VMEM((2, 8, 128), F32),
            pltpu.VMEM((N_BOX, 4, 128), BF),
            pltpu.VMEM((N_XY * NT_F + NT_F, NT * N_XY), BF),
            pltpu.VMEM((NP_F * 16, NP * 16), BF),
            pltpu.VMEM((ROW_DEV // 256, 24, 256), F32),
            pltpu.VMEM((16, SLOTS), F32),
            pltpu.VMEM((ROW_DEV, SLOTS), BF),
            pltpu.VMEM((blocks, 8, 256), F32),
            pltpu.VMEM((2, 48, 256), F32),
            pltpu.VMEM((2, 48, 256), F32),
            pltpu.VMEM((blocks, NT_F * NP_F, 256), BF),
            pltpu.VMEM((NP_F * 16, 2 * C), F32),
            pltpu.VMEM((NP_F * 16, 2 * C), F32),
            pltpu.VMEM((C, NT_F * NP_F), BF),
            pltpu.VMEM((SLOTS, C), BF),
            pltpu.VMEM((N_BOX * SLOT, C), BF),
            pltpu.VMEM((ROW_DEV, C), F32),
            pltpu.VMEM((ROW_DEV, C), BF),
            dma((P_DEV,)),
            dma((P_DEV + 1,)),
            dma,
            dma,
            dma((P_DEV,)),
            dma((P_DEV + 1,)),
            dma((P_DEV,)),
            dma((P_DEV,)),
            dma((P_DEV,)),
            dma((P_DEV,)),
            dma,
            dma((3,)),
            dma((4,)),
            dma((SMALL,)),
        ]
        + [pltpu.VMEM(v.shape, v.dtype) for v in small],
        compiler_params=pltpu.CompilerParams(
            collective_id=0, has_side_effects=True, vmem_limit_bytes=60 << 20
        ),
        name="step",
    )(pattern, *small)


def finish_kernel(field, fwd, out, grad):
    v = field[...]
    out[...] = v
    product = fwd[...].astype(F32) * v.astype(F32)
    grad[...] = (jnp.sum(product.T, axis=0, keepdims=True) * (0.5 / math.sqrt(C))).reshape(grad.shape)


def finish(field, fwd):
    rows = 1024
    block = pl.BlockSpec((rows, C), lambda i: (i, 0))
    return pl.pallas_call(
        finish_kernel,
        out_shape=(
            jax.ShapeDtypeStruct((ROW_DEV, C), BF),
            jax.ShapeDtypeStruct((ROW_DEV,), F32),
        ),
        grid=(ROW_DEV // rows,),
        in_specs=[block, block],
        out_specs=(block, pl.BlockSpec((rows,), lambda i: (i,))),
        name="finish",
    )(field, fwd)


def per_device(*arrays):
    field = step(*arrays[:-1])
    return finish(field, arrays[-1])


def solution(mesh):
    in_specs = (
        P("dir", "box", None, None),
        P(),
        P(),
        P(),
        P(),
        P(("dir", "box")),
        P(None, ("dir", "box")),
        P(("dir", "box"), None),
    )
    out_specs = (P(("dir", "box"), None), P(("dir", "box")))
    return jax.shard_map(
        per_device, mesh=mesh, in_specs=in_specs, out_specs=out_specs, check_vma=False
    )
```

```python
import functools
import math

import jax
import jax.numpy as jnp
import numpy as np
from jax import lax
from jax.experimental import pallas as pl
from jax.experimental.pallas import tpu as pltpu
from jax.sharding import PartitionSpec as P

NT = 64
NP = 128
NT_F = 32
NP_F = 64
C = 128
HALF = 64
N_DIR = 8
N_BOX = 32
N_XY = 16
ROW_DEV = 2048
SLOT = 64
HOT = 256
SLOTS = N_BOX * SLOT + HOT
P_DEV = NP // N_BOX
T_DEV = NT // N_DIR
LAST = P_DEV - 1
FAR_FIRST = (2, 3, 1, 0)
SMALL = 11

box_phase = 50.265482

MESH = pl.DeviceIdType.MESH
BF = jnp.bfloat16
F32 = jnp.float32


def polynomials():
    z2 = 0.5 + 0.5 * np.cos(np.pi * (np.arange(400) + 0.5) / 400)
    z = np.sqrt(z2)
    s = np.polynomial.chebyshev.Chebyshev.fit(z2, np.sin(np.pi * z) / z, 7, domain=[0, 1])
    k = np.polynomial.chebyshev.Chebyshev.fit(z2, np.cos(np.pi * z), 8, domain=[0, 1])
    to = np.polynomial.polynomial.Polynomial
    return tuple(
        [float(v) for v in f.convert(kind=to, domain=[-1, 1], window=[-1, 1]).coef] for f in (s, k)
    )


SIN_POLY, COS_POLY = polynomials()


def turns(u):
    z = (u - jnp.round(u)) * 2.0
    w = z * z
    s = jnp.full_like(w, SIN_POLY[-1])
    for v in SIN_POLY[-2::-1]:
        s = s * w + v
    k = jnp.full_like(w, COS_POLY[-1])
    for v in COS_POLY[-2::-1]:
        k = k * w + v
    return k, s * z


def theta_signs():
    h = np.zeros((NT_F, NT_F), np.float32)
    for t in range(16):
        for c in range(2):
            h[c * 16 + t, t] = 1.0
            h[c * 16 + t, 31 - t] = (-1.0) ** c
    return h


def phi_signs():
    h = np.zeros((NP_F, NP_F), np.float32)
    for q in range(1, 16):
        for a in range(2):
            for b in range(2):
                r = q * 4 + a * 2 + b
                h[r, q] = 1.0
                h[r, 32 - q] = (-1.0) ** a
                h[r, 64 - q] = (-1.0) ** b
                h[r, 32 + q] = (-1.0) ** (a + b)
    for a in range(2):
        h[a * 2, 0] = 1.0
        h[a * 2, 32] = (-1.0) ** a
    h[1, 16], h[1, 48] = 1.0, -1.0
    h[3, 16], h[3, 48] = 1.0, 1.0
    return h


def one_hot(p, lane):
    parts = []
    for h in range(2):
        column = jnp.broadcast_to(p[:, h * 128 : (h + 1) * 128], (128, 128)).T
        parts.append(
            jnp.concatenate(
                [
                    jnp.where(column == lane + float(j * 128), 1.0, 0.0).astype(BF)
                    for j in range(SLOTS // 128)
                ],
                axis=1,
            )
        )
    return jnp.concatenate(parts, axis=0)


def spread(taps, weights, count):
    sample = lax.broadcasted_iota(jnp.int32, (count, taps.shape[1]), 0)
    total = jnp.zeros(sample.shape, F32)
    for j in range(taps.shape[0]):
        total = total + jnp.where(
            sample == taps[j : j + 1, :], weights[j : j + 1, :].astype(F32), 0.0
        )
    return total.astype(BF)


def step_kernel(pat, *refs):
    small, refs = refs[:SMALL], refs[SMALL:]
    (
        field, recv, ybuf, hbuf, twin, hsum, ry, rh, go, hotg, rg, mt, mp, geo, gacc, oh, gs, ex, ey, w,
        acc_own, acc_hot, gt, f, r, total, field_v,
        z_send, z_recv, g_send, g_recv, y_send, y_recv, t_send, t_recv, h_send, h_recv,
        r_send, r_recv, field_sem, small_sem,
    ) = refs[: len(refs) - SMALL]
    held = refs[len(refs) - SMALL :]
    tap_t, tap_p, wt_t, wt_p, sign_t, sign_p, box_of_row, off, sines, cosines, quad = held
    d = lax.axis_index("dir")
    b = lax.axis_index("box")
    zh = b // N_XY
    xy = b % N_XY
    e = zh * N_DIR + d

    barrier = pltpu.get_barrier_semaphore()

    def greet_z(k, carry):
        e2 = (e + k) % 16
        pl.semaphore_signal(
            barrier, inc=1, device_id=(e2 % N_DIR, e2 // N_DIR * N_XY + xy), device_id_type=MESH
        )
        return carry

    def greet_box(k, carry):
        pl.semaphore_signal(barrier, inc=1, device_id=(d, (b + k) % N_BOX), device_id_type=MESH)
        return carry

    lax.fori_loop(1, 16, greet_z, 0)
    lax.fori_loop(1, N_BOX, greet_box, 0)


    def z_copy(pi, k):
        e2 = (e + k) % 16
        d2, zh2 = e2 % N_DIR, e2 // N_DIR
        first = pl.multiple_of(d2 * N_BOX + zh2 * N_XY, N_XY)
        return pltpu.make_async_remote_copy(
            src_ref=pat.at[:, pi, pl.ds(first, N_XY), :],
            dst_ref=recv.at[pi, zh, d],
            send_sem=z_send.at[pi],
            recv_sem=z_recv.at[pi],
            device_id=(d2, zh2 * N_XY + xy),
            device_id_type=MESH,
        )

    def z_own(pi, half=0):
        first = pl.multiple_of(d * N_BOX + zh * N_XY, N_XY)
        return pltpu.make_async_copy(
            pat.at[:, pi, pl.ds(first, N_XY), :], recv.at[pi, zh, d], z_recv.at[pi + half]
        )

    def g_copy(k):
        b2 = (b + k) % N_BOX
        return pltpu.make_async_remote_copy(
            src_ref=go.at[b2 // 2],
            dst_ref=rg.at[b],
            send_sem=g_send,
            recv_sem=g_recv,
            device_id=(d, b2),
            device_id_type=MESH,
        )

    def y_copy(pi, k):
        xy2 = (xy + k) % N_XY
        return pltpu.make_async_remote_copy(
            src_ref=ybuf.at[pi, xy2],
            dst_ref=ry.at[pi, xy],
            send_sem=y_send.at[pi],
            recv_sem=y_recv.at[pi],
            device_id=(d, zh * N_XY + xy2),
            device_id_type=MESH,
        )

    def h_copy(pi, k):
        xy2 = (xy + k) % N_XY
        return pltpu.make_async_remote_copy(
            src_ref=hsum.at[pi],
            dst_ref=rh.at[pi, xy],
            send_sem=h_send.at[pi],
            recv_sem=h_recv.at[pi],
            device_id=(d, zh * N_XY + xy2),
            device_id_type=MESH,
        )

    def t_copy(pi):
        return pltpu.make_async_remote_copy(
            src_ref=hbuf.at[pi],
            dst_ref=twin.at[pi],
            send_sem=t_send.at[pi],
            recv_sem=t_recv.at[pi],
            device_id=(d, (b + N_XY) % N_BOX),
            device_id_type=MESH,
        )

    def y_own(pi):
        return pltpu.make_async_copy(ybuf.at[pi, xy], ry.at[pi, xy], y_recv.at[pi])

    def h_own(pi):
        return pltpu.make_async_copy(hsum.at[pi], rh.at[pi, xy], h_recv.at[pi])

    def g_own():
        return pltpu.make_async_copy(go.at[b // 2], rg.at[b], g_recv)

    def r_copy(b2):
        return pltpu.make_async_remote_copy(
            src_ref=f.at[pl.ds(pl.multiple_of(b2 * SLOT, SLOT), SLOT), :],
            dst_ref=r.at[pl.ds(pl.multiple_of(b * SLOT, SLOT), SLOT), :],
            send_sem=r_send,
            recv_sem=r_recv.at[(zh + b2 // N_XY) % 2 * (2 - (b2 // 4 + 8 - b // 4) % 4 // 2)],
            device_id=(d, b2),
            device_id_type=MESH,
        )

    def r_own():
        at = pl.ds(pl.multiple_of(b * SLOT, SLOT), SLOT)
        return pltpu.make_async_copy(f.at[at, :], r.at[at, :], r_recv.at[0])

    def each(n, copy):
        def one(k, carry):
            copy(k).start()
            return carry

        lax.fori_loop(1, n, one, 0)

    def wait_for(ref, sem):
        pltpu.make_async_copy(ref, ref, sem).wait()

    def z_half_copy(zh2, j):
        d2 = (d + j) % N_DIR
        first = pl.multiple_of(d2 * N_BOX + zh2 * N_XY, N_XY)
        return pltpu.make_async_remote_copy(
            src_ref=pat.at[:, LAST, pl.ds(first, N_XY), :],
            dst_ref=recv.at[LAST, zh, d],
            send_sem=z_send.at[LAST],
            recv_sem=z_recv.at[LAST + (zh + zh2 + 1) % 2],
            device_id=(d2, zh2 * N_XY + xy),
            device_id_type=MESH,
        )

    def z_start_last():
        def other(j, carry):
            z_half_copy(1 - zh, j).start()
            return carry

        lax.fori_loop(0, N_DIR, other, 0)
        each(N_DIR, functools.partial(z_half_copy, zh))
        z_own(LAST, 1).start()

    def y_half_copy(half, sem, k):
        xy2 = (xy + k) % N_XY
        return pltpu.make_async_remote_copy(
            src_ref=ybuf.at[LAST, xy2, half],
            dst_ref=ry.at[LAST, xy, half],
            send_sem=y_send.at[LAST],
            recv_sem=y_recv.at[sem],
            device_id=(d, zh * N_XY + xy2),
            device_id_type=MESH,
        )

    def theta_half(half, sem):
        wait_for(recv.at[LAST, half], z_recv.at[sem])
        x = recv[LAST, half].reshape(NT * N_XY, C)
        y = jnp.dot(mt[...], x, preferred_element_type=F32).astype(BF)
        ybuf[LAST, :, half] = y[: N_XY * NT_F].reshape(N_XY, NT_F, C)
        hbuf[LAST, half] = y[N_XY * NT_F :]
        each(N_XY, functools.partial(y_half_copy, half, sem))
        pltpu.make_async_copy(
            ybuf.at[LAST, xy, half], ry.at[LAST, xy, half], y_recv.at[sem]
        ).start()

    def z_start(pi):
        each(16, functools.partial(z_copy, pi))
        z_own(pi).start()

    for i in range(SMALL):
        pltpu.make_async_copy(small[i], held[i], small_sem.at[i]).start()
    pl.semaphore_wait(barrier, 15 + N_BOX - 1)
    z_start(0)
    for i in range(SMALL):
        pltpu.make_async_copy(small[i], held[i], small_sem.at[i]).wait()


    box = box_of_row[...]
    parent = box // 8
    octant = box - parent * 8
    dest = parent % N_BOX
    owner = lax.broadcasted_iota(jnp.int32, (N_BOX, ROW_DEV), 0)
    onehot = jnp.where(owner == dest, 1.0, 0.0).astype(F32)
    width = 256
    before = jnp.where(
        lax.broadcasted_iota(jnp.int32, (width, width), 0)
        < lax.broadcasted_iota(jnp.int32, (width, width), 1),
        1.0,
        0.0,
    ).astype(BF)
    carry = jnp.zeros((N_BOX, 1), F32)
    ranks = []
    for i in range(ROW_DEV // width):
        one = onehot[:, i * width : (i + 1) * width]
        pre = jnp.dot(one.astype(BF), before, preferred_element_type=F32) + carry
        ranks.append(jnp.sum(one * pre, axis=0, keepdims=True))
        carry = carry + jnp.sum(one, axis=1, keepdims=True)
    rank = jnp.concatenate(ranks, axis=1)
    is_hot = jnp.where(carry > float(SLOT), 1.0, 0.0)
    hot_row = jnp.sum(onehot * is_hot, axis=0, keepdims=True)
    number = lax.broadcasted_iota(jnp.int32, (N_BOX, 1), 0).astype(F32)
    hot = jnp.sum(number * is_hot, axis=0, keepdims=True)

    pos = jnp.where(
        hot_row > 0.5, float(N_BOX * SLOT) + rank, dest.astype(F32) * float(SLOT) + rank
    )
    sub = lax.broadcasted_iota(jnp.int32, (16, ROW_DEV), 0)
    o = off[...].astype(F32)
    g = jnp.where(sub == 3, octant.astype(F32), 0.0)
    for i in range(3):
        g = jnp.where(sub == i, o[i : i + 1, :], g)
    g = g.astype(BF)
    for i in range(ROW_DEV // width):
        geo[i, :16] = g[:, i * width : (i + 1) * width].astype(F32)
        geo[i, 16:] = jnp.broadcast_to(pos[:, i * width : (i + 1) * width], (8, width))
    gacc[...] = jnp.zeros_like(gacc)
    lane128 = lax.broadcasted_iota(jnp.int32, (128, 128), 1).astype(F32)

    def sort_block(i, carry):
        hits = one_hot(geo[i, 16:17], lane128)
        oh[pl.ds(pl.multiple_of(i * width, width), width), :] = hits
        gacc[...] += jnp.dot(geo[i, :16].astype(BF), hits, preferred_element_type=F32)
        return carry

    lax.fori_loop(0, ROW_DEV // width, sort_block, 0)
    for m in range(N_BOX // 2):
        go[m] = gacc[:4, m * 128 : (m + 1) * 128].astype(BF)
    for m in range(2):
        hotg[m] = gacc[:8, N_BOX * SLOT + m * 128 : N_BOX * SLOT + (m + 1) * 128]
    each(N_BOX, g_copy)
    g_own().start()
    z_start(1)


    a_theta = spread(tap_t[...], wt_t[...], NT_F)
    ah = jnp.dot(sign_t[...], a_theta, preferred_element_type=F32).astype(BF)
    col = lax.broadcasted_iota(jnp.int32, (NT, NT * N_XY), 1)
    row = lax.broadcasted_iota(jnp.int32, (NT, NT * N_XY), 0)
    wide = jnp.where(col // N_XY == row, 1.0, 0.0).astype(BF)
    v = jnp.dot(ah, wide, preferred_element_type=F32)
    lane_g = lax.broadcasted_iota(jnp.int32, v.shape, 1) % N_XY
    for i in range(N_XY):
        mt[i * NT_F : (i + 1) * NT_F, :] = jnp.where(lane_g == i, v, 0.0).astype(BF)
    local = hot - (zh * N_XY).astype(F32)
    mt[N_XY * NT_F :, :] = jnp.where(lane_g.astype(F32) == local, v, 0.0).astype(BF)

    a_phi = spread(tap_p[...], wt_p[...], NP_F)
    bh = jnp.dot(sign_p[...], a_phi, preferred_element_type=F32).astype(BF)
    col = lax.broadcasted_iota(jnp.int32, (NP, NP * 16), 1) // 16
    row = lax.broadcasted_iota(jnp.int32, (NP, NP * 16), 0)
    sample = col % 2 * (NP // 2) + col // 2 % N_XY * P_DEV + col // N_BOX
    wide = jnp.where(sample == row, 1.0, 0.0).astype(BF)
    v = jnp.dot(bh, wide, preferred_element_type=F32)
    same = (
        lax.broadcasted_iota(jnp.int32, (16, NP * 16), 1) % 16
        == lax.broadcasted_iota(jnp.int32, (16, NP * 16), 0)
    )
    for i in range(NP_F):
        mp[i * 16 : (i + 1) * 16, :] = jnp.where(same, v[i : i + 1, :], 0.0).astype(BF)


    lane = lax.broadcasted_iota(jnp.int32, (16, C), 1)
    low = lane < HALF

    def gather_geometry():
        wait_for(rg, g_recv)
        odd = b % 2 == 1

        def side(m):
            t = rg[m].astype(F32)
            return jnp.where(odd, pltpu.roll(t, HALF, 1), t)

        for m in range(N_BOX // 2):
            second = pltpu.roll(side(2 * m + 1), HALF, 1)
            gs[m // 2, :4, m % 2 * 128 : (m % 2 + 1) * 128] = jnp.where(low[:4], side(2 * m), second)
        for m in range(2):
            gs[N_BOX // 4, :, m * 128 : (m + 1) * 128] = hotg[m]

    def phases(i, carry):
        g = gs[i]
        octant = g[3:4]
        bz = jnp.where(octant >= 4.0, 1.0, 0.0)
        rest = octant - 4.0 * bz
        by = jnp.where(rest >= 2.0, 1.0, 0.0)
        bx = rest - 2.0 * by

        def turned(axis, bit):
            place = box_phase * ((2.0 * bit - 1.0) * 0.25 + g[axis : axis + 1] * 0.5)
            return place * (0.5 / math.pi)

        for table, u, factor in (
            (ex, turned(0, bx) * 0.5, sines),
            (ey, turned(1, by) * 0.5, cosines),
        ):
            k, s = turns(u * factor[...])
            table[0, 16:, :] = k
            table[1, 16:, :] = s
            table[0, :16, :] = k[16:]
            table[1, :16, :] = -s[16:]
        cc, sc = turns(turned(2, bz) * cosines[:16, :])
        for q in range(16):
            lo, hi = 16 - q, 16 + q
            c1, s1 = ex[0, hi : hi + 16, :], ex[1, hi : hi + 16, :]
            c2, s2 = ex[0, lo : lo + 16, :], ex[1, lo : lo + 16, :]
            ca, sa = c1 * c2 - s1 * s2, s1 * c2 + c1 * s2
            if q == 0:
                lo, hi = 0, 32
            c1, s1 = ey[0, hi : hi + 16, :], ey[1, hi : hi + 16, :]
            c2, s2 = ey[0, lo : lo + 16, :], ey[1, lo : lo + 16, :]
            cb, sb = c1 * c2 + s1 * s2, s2 * c1 - c2 * s1
            if q == 0:
                four = (ca, sb, sa, cb)
            else:
                four = (ca * cb, ca * sb, sa * cb, sa * sb)
            for j, v in enumerate(four):
                at = q * 128 + j * 32
                w[i, at : at + 16, :] = (v * cc).astype(BF)
                w[i, at + 16 : at + 32, :] = (v * sc).astype(BF)
        return carry


    def theta_step(pi):
        wait_for(recv.at[pi], z_recv.at[pi])
        x = jnp.concatenate(
            [recv[pi, 0].reshape(NT * N_XY, C), recv[pi, 1].reshape(NT * N_XY, C)], axis=1
        )
        y = jnp.dot(mt[...], x, preferred_element_type=F32).astype(BF)
        for z in range(2):
            part = y[:, z * C : (z + 1) * C]
            ybuf[pi, :, z] = part[: N_XY * NT_F].reshape(N_XY, NT_F, C)
            hbuf[pi, z] = part[N_XY * NT_F :]
        each(N_XY, functools.partial(y_copy, pi))
        y_own(pi).start()
        if pi < 2:
            t_copy(pi).start()

    def hot_step(pi):
        t_copy(pi).wait_recv()
        hsum[pi] = hbuf[pi] + twin[pi]
        each(N_XY, functools.partial(h_copy, pi))
        h_own(pi).start()

    def phi_step(pi, part, sem, acc):
        bytes_of = part.at[pi, : N_XY // 2] if part is ry and pi == LAST else part.at[pi]
        wait_for(bytes_of, sem.at[pi])
        x = jnp.concatenate(
            [part[pi, :, :, c * 16 : (c + 1) * 16, :].reshape(512, C) for c in range(2)], axis=1
        )
        y = jnp.dot(mp[:, pi * 512 : (pi + 1) * 512], x, preferred_element_type=F32)
        if pi:
            acc[...] += y
        else:
            acc[...] = y

    def directions(acc):
        scale = quad[...]
        for q in range(16):
            parts = []
            for ab in range(4):
                for c in range(2):
                    at = q * 64 + ab * 16
                    v = acc[at : at + 16, c * C : (c + 1) * C] * scale
                    turn = (ab // 2 + ab % 2 + c) if (q or ab < 3) else c
                    if turn % 2:
                        v = pltpu.roll(v, HALF, 1)
                        v = jnp.where(low, -v, v) if turn == 1 else jnp.where(low, v, -v)
                    elif turn == 2:
                        v = -v
                    parts.append(v)
            gt[:, q * 128 : (q + 1) * 128] = jnp.concatenate(parts, axis=0).T.astype(BF)

    def field_block(i):
        return jnp.dot(gt[...], w[i], preferred_element_type=F32).T.astype(BF)

    def send_block(i, carry):
        u = 3 - i % 4
        at = (1 - zh + i // 4) % 2 * 4 + (b // 4 + u // 2 * 2 + (u // 2 + u % 2) % 2) % 4
        f[pl.ds(pl.multiple_of(at * 256, 256), 256), :] = field_block(at)
        for j in FAR_FIRST:
            b2 = at * 4 + (b + j) % 4

            @pl.when(b2 != b)
            def _():
                r_copy(b2).start()

            @pl.when(b2 == b)
            def _():
                r_own().start()

        return carry

    own_args = (ry, y_recv, acc_own)
    hot_args = (rh, h_recv, acc_hot)
    theta_step(0)
    z_start(2)
    gather_geometry()
    lax.fori_loop(0, 4, phases, 0)
    theta_step(1)
    z_start_last()
    hot_step(0)
    phi_step(0, *own_args)
    lax.fori_loop(4, 9, phases, 0)
    theta_step(2)
    hot_step(1)
    phi_step(1, *own_args)
    phi_step(0, *hot_args)
    theta_half(1 - zh, LAST)
    phi_step(2, *own_args)
    theta_half(zh, LAST + 1)
    t_copy(2).start()
    t_copy(3).start()
    phi_step(1, *hot_args)
    hot_step(2)
    wait_for(ry.at[LAST, : N_XY // 2], y_recv.at[LAST + 1])
    phi_step(3, *own_args)
    hot_step(3)
    directions(acc_own)
    lax.fori_loop(0, N_BOX // 4, send_block, 0)
    phi_step(2, *hot_args)
    for pi in range(P_DEV):
        wait_for(f.at[: 15 * 128], z_send.at[pi])
        wait_for(f.at[: 15 * SLOT], y_send.at[pi])
    wait_for(rg.at[: N_BOX - 1], g_send)
    phi_step(3, *hot_args)
    directions(acc_hot)
    f[N_BOX * SLOT :, :] = field_block(N_BOX // 4)

    half = N_BOX * SLOT // 2
    here = pl.multiple_of(zh * half, half)
    there = pl.multiple_of(half - zh * half, half)
    wait_for(r.at[pl.ds(here, half), :], r_recv.at[0])

    def place_here(i, carry):
        at = pl.multiple_of(i * 1024, 1024)
        v = jnp.dot(
            oh[pl.ds(at, 1024), pl.ds(here, half)],
            r[pl.ds(here, half), :],
            preferred_element_type=F32,
        )
        total[pl.ds(at, 1024), :] = v + jnp.dot(
            oh[pl.ds(at, 1024), N_BOX * SLOT :],
            f[N_BOX * SLOT :, :],
            preferred_element_type=F32,
        )
        return carry

    lax.fori_loop(0, ROW_DEV // 1024, place_here, 0)
    for pi in range(P_DEV):
        t_copy(pi).wait_send()
        wait_for(f.at[: 15 * SLOT], h_send.at[pi])
    wait_for(f.at[: 31 * SLOT], r_send)
    for piece in range(2):
        lanes = []
        for k in range(2):
            source = (b // 4 + 4 - FAR_FIRST[2 * piece + k]) % 4
            lanes.append(pl.ds(pl.multiple_of(there + source * 256, 256), 256))
        wait_for(f.at[:512, :], r_recv.at[1 + piece])
        part = jnp.concatenate([r[k, :] for k in lanes], axis=0)
        for i in range(4):
            at = pl.ds(i * 512, 512)
            hits = jnp.concatenate([oh[at, k] for k in lanes], axis=1)
            v = total[at, :] + jnp.dot(hits, part, preferred_element_type=F32)
            if piece == 0:
                total[at, :] = v
            else:
                field_v[at, :] = v.astype(BF)
                pltpu.make_async_copy(field_v.at[at, :], field.at[at, :], field_sem.at[i]).start()
    for i in range(4):
        at = pl.ds(i * 512, 512)
        pltpu.make_async_copy(field_v.at[at, :], field.at[at, :], field_sem.at[i]).wait()


def step(pattern, tap_theta, tap_phi, weight_theta, weight_phi, row_box, row_offset):
    n = np.arange(NT_F) + 0.5
    wide = lambda v: jnp.asarray(np.repeat(v[:, None], 256, axis=1), F32)
    sines = wide(np.sin(np.pi * n / NT_F))
    cosines = wide(np.cos(np.pi * n / NT_F))
    quad = wide(np.sin(np.pi * n[:16] / NT_F) * math.sqrt(2.0 / (NT_F * NP_F)))[:, :C]
    small = (
        tap_theta.T, tap_phi.T, weight_theta.T, weight_phi.T,
        jnp.asarray(theta_signs(), BF), jnp.asarray(phi_signs(), BF),
        row_box.reshape(1, ROW_DEV), row_offset, sines, cosines, quad,
    )
    anywhere = pl.BlockSpec(memory_space=pl.ANY)
    dma = pltpu.SemaphoreType.DMA
    theta = (P_DEV, N_XY, 2, NT_F, C)
    hot = (P_DEV, 2, NT_F, C)
    blocks = SLOTS // 256
    return pl.pallas_call(
        step_kernel,
        out_shape=jax.ShapeDtypeStruct((ROW_DEV, C), BF),
        in_specs=[anywhere] * (1 + SMALL),
        out_specs=anywhere,
        scratch_shapes=[
            pltpu.VMEM((P_DEV, 2, N_DIR, T_DEV, N_XY, C), BF),
            pltpu.VMEM(theta, BF),
            pltpu.VMEM(hot, BF),
            pltpu.VMEM(hot, BF),
            pltpu.VMEM(hot, BF),
            pltpu.VMEM(theta, BF),
            pltpu.VMEM(theta, BF),
            pltpu.VMEM((N_BOX // 2, 4, 128), BF),
            pltpu.VMEM((2, 8, 128), F32),
            pltpu.VMEM((N_BOX, 4, 128), BF),
            pltpu.VMEM((N_XY * NT_F + NT_F, NT * N_XY), BF),
            pltpu.VMEM((NP_F * 16, NP * 16), BF),
            pltpu.VMEM((ROW_DEV // 256, 24, 256), F32),
            pltpu.VMEM((16, SLOTS), F32),
            pltpu.VMEM((ROW_DEV, SLOTS), BF),
            pltpu.VMEM((blocks, 8, 256), F32),
            pltpu.VMEM((2, 48, 256), F32),
            pltpu.VMEM((2, 48, 256), F32),
            pltpu.VMEM((blocks, NT_F * NP_F, 256), BF),
            pltpu.VMEM((NP_F * 16, 2 * C), F32),
            pltpu.VMEM((NP_F * 16, 2 * C), F32),
            pltpu.VMEM((C, NT_F * NP_F), BF),
            pltpu.VMEM((SLOTS, C), BF),
            pltpu.VMEM((N_BOX * SLOT, C), BF),
            pltpu.VMEM((ROW_DEV, C), F32),
            pltpu.VMEM((ROW_DEV, C), BF),
            dma((P_DEV,)),
            dma((P_DEV + 1,)),
            dma,
            dma,
            dma((P_DEV,)),
            dma((P_DEV + 1,)),
            dma((P_DEV,)),
            dma((P_DEV,)),
            dma((P_DEV,)),
            dma((P_DEV,)),
            dma,
            dma((3,)),
            dma((4,)),
            dma((SMALL,)),
        ]
        + [pltpu.VMEM(v.shape, v.dtype) for v in small],
        compiler_params=pltpu.CompilerParams(
            collective_id=0, has_side_effects=True, vmem_limit_bytes=60 << 20
        ),
        name="step",
    )(pattern, *small)


def finish_kernel(field, fwd, out, grad):
    v = field[...]
    out[...] = v
    product = fwd[...].astype(F32) * v.astype(F32)
    grad[...] = (jnp.sum(product.T, axis=0, keepdims=True) * (0.5 / math.sqrt(C))).reshape(grad.shape)


def finish(field, fwd):
    rows = 1024
    block = pl.BlockSpec((rows, C), lambda i: (i, 0))
    return pl.pallas_call(
        finish_kernel,
        out_shape=(
            jax.ShapeDtypeStruct((ROW_DEV, C), BF),
            jax.ShapeDtypeStruct((ROW_DEV,), F32),
        ),
        grid=(ROW_DEV // rows,),
        in_specs=[block, block],
        out_specs=(block, pl.BlockSpec((rows,), lambda i: (i,))),
        name="finish",
    )(field, fwd)


def per_device(*arrays):
    field = step(*arrays[:-1])
    return finish(field, arrays[-1])


def solution(mesh):
    in_specs = (
        P("dir", "box", None, None),
        P(),
        P(),
        P(),
        P(),
        P(("dir", "box")),
        P(None, ("dir", "box")),
        P(("dir", "box"), None),
    )
    out_specs = (P(("dir", "box"), None), P(("dir", "box")))
    return jax.shard_map(
        per_device, mesh=mesh, in_specs=in_specs, out_specs=out_specs, check_vma=False
    )
```

```python
import functools
import math

import jax
import jax.numpy as jnp
import numpy as np
from jax import lax
from jax.experimental import pallas as pl
from jax.experimental.pallas import tpu as pltpu
from jax.sharding import PartitionSpec as P

NT = 64
NP = 128
NT_F = 32
NP_F = 64
C = 128
HALF = 64
N_DIR = 8
N_BOX = 32
N_XY = 16
ROW_DEV = 2048
SLOT = 64
HOT = 256
SLOTS = N_BOX * SLOT + HOT
P_DEV = NP // N_BOX
T_DEV = NT // N_DIR
LAST = P_DEV - 1
FAR_FIRST = (2, 3, 1, 0)
SMALL = 11

box_phase = 50.265482

MESH = pl.DeviceIdType.MESH
BF = jnp.bfloat16
F32 = jnp.float32


def polynomials():
    z2 = 0.5 + 0.5 * np.cos(np.pi * (np.arange(400) + 0.5) / 400)
    z = np.sqrt(z2)
    s = np.polynomial.chebyshev.Chebyshev.fit(z2, np.sin(np.pi * z) / z, 7, domain=[0, 1])
    k = np.polynomial.chebyshev.Chebyshev.fit(z2, np.cos(np.pi * z), 8, domain=[0, 1])
    to = np.polynomial.polynomial.Polynomial
    return tuple(
        [float(v) for v in f.convert(kind=to, domain=[-1, 1], window=[-1, 1]).coef] for f in (s, k)
    )


SIN_POLY, COS_POLY = polynomials()


def turns(u):
    z = (u - jnp.round(u)) * 2.0
    w = z * z
    s = jnp.full_like(w, SIN_POLY[-1])
    for v in SIN_POLY[-2::-1]:
        s = s * w + v
    k = jnp.full_like(w, COS_POLY[-1])
    for v in COS_POLY[-2::-1]:
        k = k * w + v
    return k, s * z


def theta_signs():
    h = np.zeros((NT_F, NT_F), np.float32)
    for t in range(16):
        for c in range(2):
            h[c * 16 + t, t] = 1.0
            h[c * 16 + t, 31 - t] = (-1.0) ** c
    return h


def phi_signs():
    h = np.zeros((NP_F, NP_F), np.float32)
    for q in range(1, 16):
        for a in range(2):
            for b in range(2):
                r = q * 4 + a * 2 + b
                h[r, q] = 1.0
                h[r, 32 - q] = (-1.0) ** a
                h[r, 64 - q] = (-1.0) ** b
                h[r, 32 + q] = (-1.0) ** (a + b)
    for a in range(2):
        h[a * 2, 0] = 1.0
        h[a * 2, 32] = (-1.0) ** a
    h[1, 16], h[1, 48] = 1.0, -1.0
    h[3, 16], h[3, 48] = 1.0, 1.0
    return h


def one_hot(p, lane):
    parts = []
    for h in range(2):
        column = jnp.broadcast_to(p[:, h * 128 : (h + 1) * 128], (128, 128)).T
        parts.append(
            jnp.concatenate(
                [
                    jnp.where(column == lane + float(j * 128), 1.0, 0.0).astype(BF)
                    for j in range(SLOTS // 128)
                ],
                axis=1,
            )
        )
    return jnp.concatenate(parts, axis=0)


def spread(taps, weights, count):
    sample = lax.broadcasted_iota(jnp.int32, (count, taps.shape[1]), 0)
    total = jnp.zeros(sample.shape, F32)
    for j in range(taps.shape[0]):
        total = total + jnp.where(
            sample == taps[j : j + 1, :], weights[j : j + 1, :].astype(F32), 0.0
        )
    return total.astype(BF)


def step_kernel(pat, *refs):
    small, refs = refs[:SMALL], refs[SMALL:]
    (
        field, recv, ybuf, hbuf, twin, hsum, ry, rh, go, hotg, rg, mt, mp, geo, gacc, oh, gs, ex, ey, w,
        acc_own, acc_hot, gt, f, r, total, field_v,
        z_send, z_recv, g_send, g_recv, y_send, y_recv, t_send, t_recv, h_send, h_recv,
        r_send, r_recv, field_sem, small_sem,
    ) = refs[: len(refs) - SMALL]
    held = refs[len(refs) - SMALL :]
    tap_t, tap_p, wt_t, wt_p, sign_t, sign_p, box_of_row, off, sines, cosines, quad = held
    d = lax.axis_index("dir")
    b = lax.axis_index("box")
    zh = b // N_XY
    xy = b % N_XY
    e = zh * N_DIR + d

    barrier = pltpu.get_barrier_semaphore()

    def greet_z(k, carry):
        e2 = (e + k) % 16
        pl.semaphore_signal(
            barrier, inc=1, device_id=(e2 % N_DIR, e2 // N_DIR * N_XY + xy), device_id_type=MESH
        )
        return carry

    def greet_box(k, carry):
        pl.semaphore_signal(barrier, inc=1, device_id=(d, (b + k) % N_BOX), device_id_type=MESH)
        return carry

    lax.fori_loop(1, 16, greet_z, 0)
    lax.fori_loop(1, N_BOX, greet_box, 0)


    def z_copy(pi, k):
        e2 = (e + k) % 16
        d2, zh2 = e2 % N_DIR, e2 // N_DIR
        first = pl.multiple_of(d2 * N_BOX + zh2 * N_XY, N_XY)
        return pltpu.make_async_remote_copy(
            src_ref=pat.at[:, pi, pl.ds(first, N_XY), :],
            dst_ref=recv.at[pi, zh, d],
            send_sem=z_send.at[pi],
            recv_sem=z_recv.at[pi],
            device_id=(d2, zh2 * N_XY + xy),
            device_id_type=MESH,
        )

    def z_own(pi, half=0):
        first = pl.multiple_of(d * N_BOX + zh * N_XY, N_XY)
        return pltpu.make_async_copy(
            pat.at[:, pi, pl.ds(first, N_XY), :], recv.at[pi, zh, d], z_recv.at[pi + half]
        )

    def g_copy(k):
        b2 = (b + k) % N_BOX
        return pltpu.make_async_remote_copy(
            src_ref=go.at[b2 // 2],
            dst_ref=rg.at[b],
            send_sem=g_send,
            recv_sem=g_recv,
            device_id=(d, b2),
            device_id_type=MESH,
        )

    def y_copy(pi, k):
        xy2 = (xy + k) % N_XY
        return pltpu.make_async_remote_copy(
            src_ref=ybuf.at[pi, xy2],
            dst_ref=ry.at[pi, xy],
            send_sem=y_send.at[pi],
            recv_sem=y_recv.at[pi],
            device_id=(d, zh * N_XY + xy2),
            device_id_type=MESH,
        )

    def h_copy(pi, k):
        xy2 = (xy + k) % N_XY
        return pltpu.make_async_remote_copy(
            src_ref=hsum.at[pi],
            dst_ref=rh.at[pi, xy],
            send_sem=h_send.at[pi],
            recv_sem=h_recv.at[pi],
            device_id=(d, zh * N_XY + xy2),
            device_id_type=MESH,
        )

    def t_copy(pi):
        return pltpu.make_async_remote_copy(
            src_ref=hbuf.at[pi],
            dst_ref=twin.at[pi],
            send_sem=t_send.at[pi],
            recv_sem=t_recv.at[pi],
            device_id=(d, (b + N_XY) % N_BOX),
            device_id_type=MESH,
        )

    def y_own(pi):
        return pltpu.make_async_copy(ybuf.at[pi, xy], ry.at[pi, xy], y_recv.at[pi])

    def h_own(pi):
        return pltpu.make_async_copy(hsum.at[pi], rh.at[pi, xy], h_recv.at[pi])

    def g_own():
        return pltpu.make_async_copy(go.at[b // 2], rg.at[b], g_recv)

    def r_copy(b2):
        return pltpu.make_async_remote_copy(
            src_ref=f.at[pl.ds(pl.multiple_of(b2 * SLOT, SLOT), SLOT), :],
            dst_ref=r.at[pl.ds(pl.multiple_of(b * SLOT, SLOT), SLOT), :],
            send_sem=r_send,
            recv_sem=r_recv.at[(zh + b2 // N_XY) % 2 * (2 - (b2 // 4 + 8 - b // 4) % 4 // 2)],
            device_id=(d, b2),
            device_id_type=MESH,
        )

    def r_own():
        at = pl.ds(pl.multiple_of(b * SLOT, SLOT), SLOT)
        return pltpu.make_async_copy(f.at[at, :], r.at[at, :], r_recv.at[0])

    def each(n, copy):
        def one(k, carry):
            copy(k).start()
            return carry

        lax.fori_loop(1, n, one, 0)

    def wait_for(ref, sem):
        pltpu.make_async_copy(ref, ref, sem).wait()

    def z_half_copy(zh2, j):
        d2 = (d + j) % N_DIR
        first = pl.multiple_of(d2 * N_BOX + zh2 * N_XY, N_XY)
        return pltpu.make_async_remote_copy(
            src_ref=pat.at[:, LAST, pl.ds(first, N_XY), :],
            dst_ref=recv.at[LAST, zh, d],
            send_sem=z_send.at[LAST],
            recv_sem=z_recv.at[LAST + (zh + zh2 + 1) % 2],
            device_id=(d2, zh2 * N_XY + xy),
            device_id_type=MESH,
        )

    def z_start_last():
        def other(j, carry):
            z_half_copy(1 - zh, j).start()
            return carry

        lax.fori_loop(0, N_DIR, other, 0)
        each(N_DIR, functools.partial(z_half_copy, zh))
        z_own(LAST, 1).start()

    def far_first(n):
        u = 3 - n
        return u // 2 * 2 + (u // 2 + u % 2) % 2

    def y_half_copy(half, sem, k):
        x2 = (xy // 4 + far_first((k - 1) // 4)) % 4
        xy2 = x2 * 4 + (xy + far_first((k - 1) % 4)) % 4
        return pltpu.make_async_remote_copy(
            src_ref=ybuf.at[LAST, xy2, half],
            dst_ref=ry.at[LAST, xy, half],
            send_sem=y_send.at[LAST],
            recv_sem=y_recv.at[sem],
            device_id=(d, zh * N_XY + xy2),
            device_id_type=MESH,
        )

    def theta_half(half, sem):
        wait_for(recv.at[LAST, half], z_recv.at[sem])
        x = recv[LAST, half].reshape(NT * N_XY, C)
        y = jnp.dot(mt[...], x, preferred_element_type=F32).astype(BF)
        ybuf[LAST, :, half] = y[: N_XY * NT_F].reshape(N_XY, NT_F, C)
        hbuf[LAST, half] = y[N_XY * NT_F :]
        each(N_XY, functools.partial(y_half_copy, half, sem))
        pltpu.make_async_copy(
            ybuf.at[LAST, xy, half], ry.at[LAST, xy, half], y_recv.at[sem]
        ).start()

    def z_start(pi):
        each(16, functools.partial(z_copy, pi))
        z_own(pi).start()

    for i in range(SMALL):
        pltpu.make_async_copy(small[i], held[i], small_sem.at[i]).start()
    pl.semaphore_wait(barrier, 15 + N_BOX - 1)
    z_start(0)
    for i in range(SMALL):
        pltpu.make_async_copy(small[i], held[i], small_sem.at[i]).wait()


    box = box_of_row[...]
    parent = box // 8
    octant = box - parent * 8
    dest = parent % N_BOX
    owner = lax.broadcasted_iota(jnp.int32, (N_BOX, ROW_DEV), 0)
    onehot = jnp.where(owner == dest, 1.0, 0.0).astype(F32)
    width = 256
    before = jnp.where(
        lax.broadcasted_iota(jnp.int32, (width, width), 0)
        < lax.broadcasted_iota(jnp.int32, (width, width), 1),
        1.0,
        0.0,
    ).astype(BF)
    carry = jnp.zeros((N_BOX, 1), F32)
    ranks = []
    for i in range(ROW_DEV // width):
        one = onehot[:, i * width : (i + 1) * width]
        pre = jnp.dot(one.astype(BF), before, preferred_element_type=F32) + carry
        ranks.append(jnp.sum(one * pre, axis=0, keepdims=True))
        carry = carry + jnp.sum(one, axis=1, keepdims=True)
    rank = jnp.concatenate(ranks, axis=1)
    is_hot = jnp.where(carry > float(SLOT), 1.0, 0.0)
    hot_row = jnp.sum(onehot * is_hot, axis=0, keepdims=True)
    number = lax.broadcasted_iota(jnp.int32, (N_BOX, 1), 0).astype(F32)
    hot = jnp.sum(number * is_hot, axis=0, keepdims=True)

    pos = jnp.where(
        hot_row > 0.5, float(N_BOX * SLOT) + rank, dest.astype(F32) * float(SLOT) + rank
    )
    sub = lax.broadcasted_iota(jnp.int32, (16, ROW_DEV), 0)
    o = off[...].astype(F32)
    g = jnp.where(sub == 3, octant.astype(F32), 0.0)
    for i in range(3):
        g = jnp.where(sub == i, o[i : i + 1, :], g)
    g = g.astype(BF)
    for i in range(ROW_DEV // width):
        geo[i, :16] = g[:, i * width : (i + 1) * width].astype(F32)
        geo[i, 16:] = jnp.broadcast_to(pos[:, i * width : (i + 1) * width], (8, width))
    gacc[...] = jnp.zeros_like(gacc)
    lane128 = lax.broadcasted_iota(jnp.int32, (128, 128), 1).astype(F32)

    def sort_block(i, carry):
        hits = one_hot(geo[i, 16:17], lane128)
        oh[pl.ds(pl.multiple_of(i * width, width), width), :] = hits
        gacc[...] += jnp.dot(geo[i, :16].astype(BF), hits, preferred_element_type=F32)
        return carry

    lax.fori_loop(0, ROW_DEV // width, sort_block, 0)
    for m in range(N_BOX // 2):
        go[m] = gacc[:4, m * 128 : (m + 1) * 128].astype(BF)
    for m in range(2):
        hotg[m] = gacc[:8, N_BOX * SLOT + m * 128 : N_BOX * SLOT + (m + 1) * 128]
    each(N_BOX, g_copy)
    g_own().start()
    z_start(1)


    a_theta = spread(tap_t[...], wt_t[...], NT_F)
    ah = jnp.dot(sign_t[...], a_theta, preferred_element_type=F32).astype(BF)
    col = lax.broadcasted_iota(jnp.int32, (NT, NT * N_XY), 1)
    row = lax.broadcasted_iota(jnp.int32, (NT, NT * N_XY), 0)
    wide = jnp.where(col // N_XY == row, 1.0, 0.0).astype(BF)
    v = jnp.dot(ah, wide, preferred_element_type=F32)
    lane_g = lax.broadcasted_iota(jnp.int32, v.shape, 1) % N_XY
    for i in range(N_XY):
        mt[i * NT_F : (i + 1) * NT_F, :] = jnp.where(lane_g == i, v, 0.0).astype(BF)
    local = hot - (zh * N_XY).astype(F32)
    mt[N_XY * NT_F :, :] = jnp.where(lane_g.astype(F32) == local, v, 0.0).astype(BF)

    a_phi = spread(tap_p[...], wt_p[...], NP_F)
    bh = jnp.dot(sign_p[...], a_phi, preferred_element_type=F32).astype(BF)
    col = lax.broadcasted_iota(jnp.int32, (NP, NP * 16), 1) // 16
    row = lax.broadcasted_iota(jnp.int32, (NP, NP * 16), 0)
    sample = col % 2 * (NP // 2) + col // 2 % N_XY * P_DEV + col // N_BOX
    wide = jnp.where(sample == row, 1.0, 0.0).astype(BF)
    v = jnp.dot(bh, wide, preferred_element_type=F32)
    same = (
        lax.broadcasted_iota(jnp.int32, (16, NP * 16), 1) % 16
        == lax.broadcasted_iota(jnp.int32, (16, NP * 16), 0)
    )
    for i in range(NP_F):
        mp[i * 16 : (i + 1) * 16, :] = jnp.where(same, v[i : i + 1, :], 0.0).astype(BF)


    lane = lax.broadcasted_iota(jnp.int32, (16, C), 1)
    low = lane < HALF

    def gather_geometry():
        wait_for(rg, g_recv)
        odd = b % 2 == 1

        def side(m):
            t = rg[m].astype(F32)
            return jnp.where(odd, pltpu.roll(t, HALF, 1), t)

        for m in range(N_BOX // 2):
            second = pltpu.roll(side(2 * m + 1), HALF, 1)
            gs[m // 2, :4, m % 2 * 128 : (m % 2 + 1) * 128] = jnp.where(low[:4], side(2 * m), second)
        for m in range(2):
            gs[N_BOX // 4, :, m * 128 : (m + 1) * 128] = hotg[m]

    def phases(i, carry):
        g = gs[i]
        octant = g[3:4]
        bz = jnp.where(octant >= 4.0, 1.0, 0.0)
        rest = octant - 4.0 * bz
        by = jnp.where(rest >= 2.0, 1.0, 0.0)
        bx = rest - 2.0 * by

        def turned(axis, bit):
            place = box_phase * ((2.0 * bit - 1.0) * 0.25 + g[axis : axis + 1] * 0.5)
            return place * (0.5 / math.pi)

        for table, u, factor in (
            (ex, turned(0, bx) * 0.5, sines),
            (ey, turned(1, by) * 0.5, cosines),
        ):
            k, s = turns(u * factor[...])
            table[0, 16:, :] = k
            table[1, 16:, :] = s
            table[0, :16, :] = k[16:]
            table[1, :16, :] = -s[16:]
        cc, sc = turns(turned(2, bz) * cosines[:16, :])
        for q in range(16):
            lo, hi = 16 - q, 16 + q
            c1, s1 = ex[0, hi : hi + 16, :], ex[1, hi : hi + 16, :]
            c2, s2 = ex[0, lo : lo + 16, :], ex[1, lo : lo + 16, :]
            ca, sa = c1 * c2 - s1 * s2, s1 * c2 + c1 * s2
            if q == 0:
                lo, hi = 0, 32
            c1, s1 = ey[0, hi : hi + 16, :], ey[1, hi : hi + 16, :]
            c2, s2 = ey[0, lo : lo + 16, :], ey[1, lo : lo + 16, :]
            cb, sb = c1 * c2 + s1 * s2, s2 * c1 - c2 * s1
            if q == 0:
                four = (ca, sb, sa, cb)
            else:
                four = (ca * cb, ca * sb, sa * cb, sa * sb)
            for j, v in enumerate(four):
                at = q * 128 + j * 32
                w[i, at : at + 16, :] = (v * cc).astype(BF)
                w[i, at + 16 : at + 32, :] = (v * sc).astype(BF)
        return carry


    def theta_step(pi):
        wait_for(recv.at[pi], z_recv.at[pi])
        x = jnp.concatenate(
            [recv[pi, 0].reshape(NT * N_XY, C), recv[pi, 1].reshape(NT * N_XY, C)], axis=1
        )
        y = jnp.dot(mt[...], x, preferred_element_type=F32).astype(BF)
        for z in range(2):
            part = y[:, z * C : (z + 1) * C]
            ybuf[pi, :, z] = part[: N_XY * NT_F].reshape(N_XY, NT_F, C)
            hbuf[pi, z] = part[N_XY * NT_F :]
        each(N_XY, functools.partial(y_copy, pi))
        y_own(pi).start()
        if pi < 2:
            t_copy(pi).start()

    def hot_step(pi):
        t_copy(pi).wait_recv()
        hsum[pi] = hbuf[pi] + twin[pi]
        each(N_XY, functools.partial(h_copy, pi))
        h_own(pi).start()

    def phi_step(pi, part, sem, acc):
        bytes_of = part.at[pi, : N_XY // 2] if part is ry and pi == LAST else part.at[pi]
        wait_for(bytes_of, sem.at[pi])
        x = jnp.concatenate(
            [part[pi, :, :, c * 16 : (c + 1) * 16, :].reshape(512, C) for c in range(2)], axis=1
        )
        y = jnp.dot(mp[:, pi * 512 : (pi + 1) * 512], x, preferred_element_type=F32)
        if pi:
            acc[...] += y
        else:
            acc[...] = y

    def directions(acc):
        scale = quad[...]
        for q in range(16):
            parts = []
            for ab in range(4):
                for c in range(2):
                    at = q * 64 + ab * 16
                    v = acc[at : at + 16, c * C : (c + 1) * C] * scale
                    turn = (ab // 2 + ab % 2 + c) if (q or ab < 3) else c
                    if turn % 2:
                        v = pltpu.roll(v, HALF, 1)
                        v = jnp.where(low, -v, v) if turn == 1 else jnp.where(low, v, -v)
                    elif turn == 2:
                        v = -v
                    parts.append(v)
            gt[:, q * 128 : (q + 1) * 128] = jnp.concatenate(parts, axis=0).T.astype(BF)

    def field_block(i):
        return jnp.dot(gt[...], w[i], preferred_element_type=F32).T.astype(BF)

    def send_block(i, carry):
        u = 3 - i % 4
        at = (1 - zh + i // 4) % 2 * 4 + (b // 4 + u // 2 * 2 + (u // 2 + u % 2) % 2) % 4
        f[pl.ds(pl.multiple_of(at * 256, 256), 256), :] = field_block(at)
        for j in FAR_FIRST:
            b2 = at * 4 + (b + j) % 4

            @pl.when(b2 != b)
            def _():
                r_copy(b2).start()

            @pl.when(b2 == b)
            def _():
                r_own().start()

        return carry

    own_args = (ry, y_recv, acc_own)
    hot_args = (rh, h_recv, acc_hot)
    theta_step(0)
    z_start(2)
    gather_geometry()
    lax.fori_loop(0, 4, phases, 0)
    theta_step(1)
    z_start_last()
    hot_step(0)
    phi_step(0, *own_args)
    lax.fori_loop(4, 9, phases, 0)
    theta_step(2)
    hot_step(1)
    phi_step(1, *own_args)
    phi_step(0, *hot_args)
    theta_half(1 - zh, LAST)
    phi_step(2, *own_args)
    theta_half(zh, LAST + 1)
    t_copy(2).start()
    t_copy(3).start()
    phi_step(1, *hot_args)
    hot_step(2)
    wait_for(ry.at[LAST, : N_XY // 2], y_recv.at[LAST + 1])
    phi_step(3, *own_args)
    hot_step(3)
    directions(acc_own)
    lax.fori_loop(0, N_BOX // 4, send_block, 0)
    phi_step(2, *hot_args)
    for pi in range(P_DEV):
        wait_for(f.at[: 15 * 128], z_send.at[pi])
        wait_for(f.at[: 15 * SLOT], y_send.at[pi])
    wait_for(rg.at[: N_BOX - 1], g_send)
    phi_step(3, *hot_args)
    directions(acc_hot)
    f[N_BOX * SLOT :, :] = field_block(N_BOX // 4)

    half = N_BOX * SLOT // 2
    here = pl.multiple_of(zh * half, half)
    there = pl.multiple_of(half - zh * half, half)
    wait_for(r.at[pl.ds(here, half), :], r_recv.at[0])

    def place_here(i, carry):
        at = pl.multiple_of(i * 1024, 1024)
        v = jnp.dot(
            oh[pl.ds(at, 1024), pl.ds(here, half)],
            r[pl.ds(here, half), :],
            preferred_element_type=F32,
        )
        total[pl.ds(at, 1024), :] = v + jnp.dot(
            oh[pl.ds(at, 1024), N_BOX * SLOT :],
            f[N_BOX * SLOT :, :],
            preferred_element_type=F32,
        )
        return carry

    lax.fori_loop(0, ROW_DEV // 1024, place_here, 0)
    for pi in range(P_DEV):
        t_copy(pi).wait_send()
        wait_for(f.at[: 15 * SLOT], h_send.at[pi])
    wait_for(f.at[: 31 * SLOT], r_send)
    for piece in range(2):
        lanes = []
        for k in range(2):
            source = (b // 4 + 4 - FAR_FIRST[2 * piece + k]) % 4
            lanes.append(pl.ds(pl.multiple_of(there + source * 256, 256), 256))
        wait_for(f.at[:512, :], r_recv.at[1 + piece])
        part = jnp.concatenate([r[k, :] for k in lanes], axis=0)
        for i in range(4):
            at = pl.ds(i * 512, 512)
            hits = jnp.concatenate([oh[at, k] for k in lanes], axis=1)
            v = total[at, :] + jnp.dot(hits, part, preferred_element_type=F32)
            if piece == 0:
                total[at, :] = v
            else:
                field_v[at, :] = v.astype(BF)
                pltpu.make_async_copy(field_v.at[at, :], field.at[at, :], field_sem.at[i]).start()
    for i in range(4):
        at = pl.ds(i * 512, 512)
        pltpu.make_async_copy(field_v.at[at, :], field.at[at, :], field_sem.at[i]).wait()


def step(pattern, tap_theta, tap_phi, weight_theta, weight_phi, row_box, row_offset):
    n = np.arange(NT_F) + 0.5
    wide = lambda v: jnp.asarray(np.repeat(v[:, None], 256, axis=1), F32)
    sines = wide(np.sin(np.pi * n / NT_F))
    cosines = wide(np.cos(np.pi * n / NT_F))
    quad = wide(np.sin(np.pi * n[:16] / NT_F) * math.sqrt(2.0 / (NT_F * NP_F)))[:, :C]
    small = (
        tap_theta.T, tap_phi.T, weight_theta.T, weight_phi.T,
        jnp.asarray(theta_signs(), BF), jnp.asarray(phi_signs(), BF),
        row_box.reshape(1, ROW_DEV), row_offset, sines, cosines, quad,
    )
    anywhere = pl.BlockSpec(memory_space=pl.ANY)
    dma = pltpu.SemaphoreType.DMA
    theta = (P_DEV, N_XY, 2, NT_F, C)
    hot = (P_DEV, 2, NT_F, C)
    blocks = SLOTS // 256
    return pl.pallas_call(
        step_kernel,
        out_shape=jax.ShapeDtypeStruct((ROW_DEV, C), BF),
        in_specs=[anywhere] * (1 + SMALL),
        out_specs=anywhere,
        scratch_shapes=[
            pltpu.VMEM((P_DEV, 2, N_DIR, T_DEV, N_XY, C), BF),
            pltpu.VMEM(theta, BF),
            pltpu.VMEM(hot, BF),
            pltpu.VMEM(hot, BF),
            pltpu.VMEM(hot, BF),
            pltpu.VMEM(theta, BF),
            pltpu.VMEM(theta, BF),
            pltpu.VMEM((N_BOX // 2, 4, 128), BF),
            pltpu.VMEM((2, 8, 128), F32),
            pltpu.VMEM((N_BOX, 4, 128), BF),
            pltpu.VMEM((N_XY * NT_F + NT_F, NT * N_XY), BF),
            pltpu.VMEM((NP_F * 16, NP * 16), BF),
            pltpu.VMEM((ROW_DEV // 256, 24, 256), F32),
            pltpu.VMEM((16, SLOTS), F32),
            pltpu.VMEM((ROW_DEV, SLOTS), BF),
            pltpu.VMEM((blocks, 8, 256), F32),
            pltpu.VMEM((2, 48, 256), F32),
            pltpu.VMEM((2, 48, 256), F32),
            pltpu.VMEM((blocks, NT_F * NP_F, 256), BF),
            pltpu.VMEM((NP_F * 16, 2 * C), F32),
            pltpu.VMEM((NP_F * 16, 2 * C), F32),
            pltpu.VMEM((C, NT_F * NP_F), BF),
            pltpu.VMEM((SLOTS, C), BF),
            pltpu.VMEM((N_BOX * SLOT, C), BF),
            pltpu.VMEM((ROW_DEV, C), F32),
            pltpu.VMEM((ROW_DEV, C), BF),
            dma((P_DEV,)),
            dma((P_DEV + 1,)),
            dma,
            dma,
            dma((P_DEV,)),
            dma((P_DEV + 1,)),
            dma((P_DEV,)),
            dma((P_DEV,)),
            dma((P_DEV,)),
            dma((P_DEV,)),
            dma,
            dma((3,)),
            dma((4,)),
            dma((SMALL,)),
        ]
        + [pltpu.VMEM(v.shape, v.dtype) for v in small],
        compiler_params=pltpu.CompilerParams(
            collective_id=0, has_side_effects=True, vmem_limit_bytes=60 << 20
        ),
        name="step",
    )(pattern, *small)


def finish_kernel(field, fwd, out, grad):
    v = field[...]
    out[...] = v
    product = fwd[...].astype(F32) * v.astype(F32)
    grad[...] = (jnp.sum(product.T, axis=0, keepdims=True) * (0.5 / math.sqrt(C))).reshape(grad.shape)


def finish(field, fwd):
    rows = 1024
    block = pl.BlockSpec((rows, C), lambda i: (i, 0))
    return pl.pallas_call(
        finish_kernel,
        out_shape=(
            jax.ShapeDtypeStruct((ROW_DEV, C), BF),
            jax.ShapeDtypeStruct((ROW_DEV,), F32),
        ),
        grid=(ROW_DEV // rows,),
        in_specs=[block, block],
        out_specs=(block, pl.BlockSpec((rows,), lambda i: (i,))),
        name="finish",
    )(field, fwd)


def per_device(*arrays):
    field = step(*arrays[:-1])
    return finish(field, arrays[-1])


def solution(mesh):
    in_specs = (
        P("dir", "box", None, None),
        P(),
        P(),
        P(),
        P(),
        P(("dir", "box")),
        P(None, ("dir", "box")),
        P(("dir", "box"), None),
    )
    out_specs = (P(("dir", "box"), None), P(("dir", "box")))
    return jax.shard_map(
        per_device, mesh=mesh, in_specs=in_specs, out_specs=out_specs, check_vma=False
    )
```
